32 devices in a mesh: dp: 16 (over z, y, core), seq: 2 (over x).
Axes of the slice: x: 2, y: 2, z: 4, core: 2. Of those that a mesh axis runs over, the one named last changes fastest.
Arguments:
- tokens: bfloat16 [16384, 768], P(('dp', 'seq')), may hold values from -6 to 6
- lengths: int32 [16, 6], P('dp'), may hold values from 1 to 768, 1024 in all within a row
- w_qkv: bfloat16 [768, 2304], P('dp'), may hold values from -0.21875 to 0.21875
- w_out: bfloat16 [768, 768], P('dp'), may hold values from -2.5 to 2.5
- w_up: bfloat16 [768, 3072], P('dp'), may hold values from -0.21875 to 0.21875
- w_down: bfloat16 [3072, 768], P('dp'), may hold values from -0.109375 to 0.109375
- bias_q: bfloat16 [768], P('dp'), may hold values from -4 to 4
- bias_v: bfloat16 [768], P('dp'), may hold values from -4 to 4
- bias_out: bfloat16 [768], P('dp'), may hold values from -4 to 4
- bias_up: bfloat16 [3072], P('dp'), may hold values from -4 to 4
- bias_down: bfloat16 [768], P('dp'), may hold values from -4 to 4
- gain_one: bfloat16 [768], P('dp'), may hold values from 0.5 to 1.5
- shift_one: bfloat16 [768], P('dp'), may hold values from -4 to 4
- gain_two: bfloat16 [768], P('dp'), may hold values from 0.5 to 1.5
- shift_two: bfloat16 [768], P('dp'), may hold values from -4 to 4
- cotangent: bfloat16 [16384, 768], P(('dp', 'seq')), may hold values from -6 to 6
Outputs:
- block_out: bfloat16 [16384, 768], P(('dp', 'seq'))
- grad_tokens: float32 [16384, 768], P(('dp', 'seq'))
- grad_w_qkv: float32 [768, 2304], P('dp')
- grad_w_out: float32 [768, 768], P('dp')
- grad_w_up: float32 [768, 3072], P('dp')
- grad_w_down: float32 [3072, 768], P('dp')
- grad_bias_q: float32 [768], P('dp')
- grad_bias_v: float32 [768], P('dp')
- grad_bias_out: float32 [768], P('dp')
- grad_bias_up: float32 [3072], P('dp')
- grad_bias_down: float32 [768], P('dp')
- grad_gain_one: float32 [768], P('dp')
- grad_shift_one: float32 [768], P('dp')
- grad_gain_two: float32 [768], P('dp')
- grad_shift_two: float32 [768], P('dp')
The draws below stay inside these ranges and needn't reach their ends.
Inputs may be any that keep to these rules, and one draw needn't show every extreme that they name: Row g holds the lengths of the 6 slots that fill the 1024 positions of group g in order; the last slot is padding; the longest slot of each row has exactly 768 positions.
All inputs are finite; a program needn't handle non-finite values.
Results may differ from the reference program's by a relative error of at most 0.011.
Values may be sent and summed in bfloat16 or wider, within the bound.
A program may use at most 192 MiB of HBM per device.

```python
import math
import jax
import jax.numpy as jnp
import numpy as np
from jax import lax

D = 768
HEADS = 12
HEAD_DIM = 64
FF = 3072
NSEG = 6
GROUP = 1024
GROUPS = 16
TOKENS = 16384
MOST = 768


def strengthened(values, own_key, source, target, shards_of, factor):
    def block_of(axis_at):
        return (jnp.arange(values.shape[axis_at]) // (values.shape[axis_at] // shards_of)).reshape((-1,) + (1,) * (values.ndim - 1 - axis_at))

    near = jax.random.permutation(own_key, shards_of)[block_of(target)]
    second = (block_of(target) + shards_of // 2) % shards_of
    return jnp.where((block_of(source) == near) | (block_of(source) == second), factor * values, values)


def level_of(key, extent, cuts, least, high):
    factor_of, own = 1.0, jax.random.fold_in(key, 6)
    for dim, parts in cuts:
        heights = jnp.exp(jax.random.uniform(jax.random.fold_in(own, dim), (parts,), jnp.float32, least / len(cuts), high / len(cuts)))
        factor_of = factor_of * jnp.repeat(heights, extent[dim] // parts).reshape([-1 if axis == dim else 1 for axis in range(len(extent))])
    return factor_of


def split_up(amount, total, limit, lean):
    weights = [(1 << 20) // math.isqrt(grade ** lean) + 1 for grade in range(2, amount + 1)]
    surplus, holding = total - limit - (amount - 1), [1] * (amount - 1)
    while surplus > 0:
        free = [i for i in range(amount - 1) if holding[i] < limit]
        mass, remaining = sum([weights[i] for i in free]), surplus
        for i in free:
            addition = min(limit - holding[i], max(1, remaining * weights[i] // mass), surplus)
            holding[i] = holding[i] + addition
            surplus = surplus - addition
    return np.array([limit] + holding)


def ragged_sizes(rng, count, total, bound, lean):
    if count == 2:
        one = jax.random.randint(rng, (), max(1, total - bound), min(bound, total - 1) + 1)
        return jnp.stack([one, total - one])
    sizes = jnp.asarray(split_up(count, total, bound, lean), jnp.int32)
    couples = (count - 1) // 2
    donor, receiver = sizes[1:1 + 2 * couples:2], sizes[2:2 + 2 * couples:2]
    margin = jnp.minimum(donor - 1, bound - receiver)
    shifted = jax.random.randint(jax.random.fold_in(rng, 1), (couples,), 0, 1 << 20) % (margin + 1)
    sizes = sizes.at[1:1 + 2 * couples:2].set(donor - shifted).at[2:2 + 2 * couples:2].set(receiver + shifted)
    return sizes[jax.random.permutation(jax.random.fold_in(rng, 2), count)]


def noise(rng, shape, deviation, reach, split=(), held_as=jnp.bfloat16):
    array = deviation * jax.random.normal(rng, shape, jnp.float32)
    if split:
        array = array * level_of(rng, shape, split, -0.22, 0.18)
    return jnp.clip(array, -reach, reach).astype(held_as)


def heavy_noise(own_key, dims, deviation, bound, shards, heavy, kind=jnp.bfloat16):
    array = deviation * jax.random.normal(own_key, dims, jnp.float32)
    if shards:
        array = array * level_of(own_key, dims, shards, -0.22, 0.18)
    return jnp.clip(strengthened(array, jax.random.fold_in(own_key, 3), *heavy), -bound, bound).astype(kind)


def setup_inputs(seed: int = 0) -> dict:
    splits = jax.random.split(jax.random.key(seed), 17)
    tokens = noise(splits[0], (TOKENS, D), 1.0, 6.0, ((0, 32),))
    lengths = jax.vmap(lambda own: ragged_sizes(own, NSEG, GROUP, MOST, 2))(jax.random.split(splits[1], GROUPS)).reshape((GROUPS, NSEG)).astype(jnp.int32)
    w_qkv = noise(splits[2], (D, 3 * D), D ** -0.5, 0.21875, ((0, 16),))
    w_out = noise(splits[3], (D, D), (D // 128) ** -0.5, 2.5, ((0, 16),))
    w_up = noise(splits[4], (D, FF), D ** -0.5, 0.21875, ((0, 16),))
    w_down = noise(splits[5], (FF, D), FF ** -0.5, 0.109375, ((0, 16),))
    bias_q = noise(splits[6], (D,), 0.3, 4.0, ((0, 16),))
    bias_v = noise(splits[7], (D,), 0.3, 4.0, ((0, 16),))
    bias_out = noise(splits[8], (D,), 0.3, 4.0, ((0, 16),))
    bias_up = noise(splits[9], (FF,), 0.3, 4.0, ((0, 16),))
    bias_down = noise(splits[10], (D,), 0.3, 4.0, ((0, 16),))
    gain_one = jnp.clip(1.0 + 0.1 * jax.random.normal(splits[11], (D,), jnp.float32), 0.5, 1.5).astype(jnp.bfloat16)
    shift_one = noise(splits[12], (D,), 0.3, 4.0, ((0, 16),))
    gain_two = jnp.clip(1.0 + 0.1 * jax.random.normal(splits[13], (D,), jnp.float32), 0.5, 1.5).astype(jnp.bfloat16)
    shift_two = noise(splits[14], (D,), 0.3, 4.0, ((0, 16),))
    cotangent = heavy_noise(splits[15], (TOKENS, D), 1.0, 6.0, ((0, 32),), (0, 1, 32, 2.75))
    return {"tokens": tokens, "lengths": lengths, "w_qkv": w_qkv, "w_out": w_out, "w_up": w_up, "w_down": w_down, "bias_q": bias_q, "bias_v": bias_v, "bias_out": bias_out, "bias_up": bias_up, "bias_down": bias_down, "gain_one": gain_one, "shift_one": shift_one, "gain_two": gain_two, "shift_two": shift_two, "cotangent": cotangent}


EPSILON = 1e-05
MASKED = -1e+30
SLOPE = 0.7978845608028654
CUBIC = 0.044715

@jax.custom_vjp
def low(v):
    return lax.optimization_barrier(v.astype(jnp.bfloat16)).astype(jnp.float32)

@jax.custom_vjp
def low_back(v):
    return v

def low_keep(v):
    return (low(v), None)

def low_pass(kept, grad):
    return (grad,)

def back_keep(v):
    return (v, None)

def back_low(kept, grad):
    return (low(grad),)
low.defvjp(low_keep, low_pass)
low_back.defvjp(back_keep, back_low)

def product(left, right):
    return jnp.dot(left, right, precision=lax.Precision.HIGHEST)

def normed(value, gain, shift):
    mean = lax.optimization_barrier(jnp.mean(value, axis=-1, keepdims=True))
    centred = value - mean
    spread = lax.optimization_barrier(jnp.mean(centred * centred, axis=-1, keepdims=True))
    return centred * lax.rsqrt(spread + EPSILON) * gain + shift

def gelu_tanh(value):
    return 0.5 * value * (1.0 + jnp.tanh(SLOPE * (value + CUBIC * value * value * value)))

def group_block(x, segment, params):
    w_qkv, w_out, w_up, w_down, bias_q, bias_v, bias_out, bias_up, bias_down, gain_one, shift_one, gain_two, shift_two = params
    position = jnp.arange(GROUP, dtype=jnp.int32)
    allowed = (segment[:, None] == segment[None, :]) & (position[None, :] <= position[:, None])
    valid = segment < NSEG - 1
    first = low(normed(x, gain_one, shift_one))
    bias_qkv = jnp.concatenate([bias_q, jnp.zeros_like(bias_q), bias_v])
    qkv = low(low_back(product(first, w_qkv) + bias_qkv))
    query = qkv[:, :D].reshape(GROUP, HEADS, HEAD_DIM)
    keys = qkv[:, D:2 * D].reshape(GROUP, HEADS, HEAD_DIM)
    values = qkv[:, 2 * D:].reshape(GROUP, HEADS, HEAD_DIM)
    scores = jnp.einsum('qhd,khd->hqk', query, keys, precision=lax.Precision.HIGHEST) * HEAD_DIM ** (-0.5)
    scores = jnp.where(allowed[None], low_back(scores), MASKED)
    top = lax.optimization_barrier(jnp.max(scores, axis=-1, keepdims=True))
    weights = jnp.exp(scores - top)
    probs = low(weights / lax.optimization_barrier(jnp.sum(weights, axis=-1, keepdims=True)))
    mixed = jnp.einsum('hqk,khd->qhd', probs, values, precision=lax.Precision.HIGHEST).reshape(GROUP, D)
    mixed = low(low_back(mixed))
    attended = low_back(product(mixed, w_out) + bias_out)
    middle = x + attended
    second = low(normed(middle, gain_two, shift_two))
    pre = low_back(product(second, w_up) + bias_up)
    hidden = low(gelu_tanh(pre))
    result = middle + product(hidden, w_down) + bias_down
    return jnp.where(valid[:, None], result, 0.0)

def reference(tokens, lengths, w_qkv, w_out, w_up, w_down, bias_q, bias_v, bias_out, bias_up, bias_down, gain_one, shift_one, gain_two, shift_two, cotangent):
    position = jnp.arange(GROUP, dtype=jnp.int32)
    ends = jnp.cumsum(lengths, axis=1).astype(jnp.int32)
    segments = lax.optimization_barrier(jnp.sum((position[None, :, None] >= ends[:, None, :]).astype(jnp.int32), axis=2))
    params = tuple((p.astype(jnp.float32) for p in (w_qkv, w_out, w_up, w_down, bias_q, bias_v, bias_out, bias_up, bias_down, gain_one, shift_one, gain_two, shift_two)))
    inputs = tokens.astype(jnp.float32).reshape(GROUPS, GROUP, D)

    def forward(inputs, params):
        step = jax.checkpoint(lambda x, segment: group_block(x, segment, params))
        return lax.map(lambda item: step(item[0], item[1]), (inputs, segments))
    outputs, pull = jax.vjp(forward, inputs, params)
    grad_inputs, grads = pull(cotangent.astype(jnp.float32).reshape(GROUPS, GROUP, D))
    return (outputs.reshape(TOKENS, D).astype(jnp.bfloat16), grad_inputs.reshape(TOKENS, D), grads[0], grads[1], grads[2], grads[3], grads[4], grads[5], grads[6], grads[7], grads[8], grads[9], grads[10], grads[11], grads[12])
```

```python
import jax
import jax.numpy as jnp
from jax import lax
from jax.experimental import pallas as pl
from jax.experimental.pallas import tpu as pltpu
from jax.sharding import PartitionSpec as P

HEAD_DIM = 64


EPSILON = 1e-05
MASKED = -1e30
SLOPE = 0.7978845608028654
CUBIC = 0.044715


def as_sent(array):
    return jax.tree.map(lambda a: a.astype(jnp.bfloat16) if a.dtype == jnp.float32 else a, array)


def dense(left, right):
    return jnp.dot(left, right, preferred_element_type=jnp.float32)


def dense_left(left, right):
    return lax.dot_general(
        left, right, (((0,), (0,)), ((), ())), preferred_element_type=jnp.float32
    )


def dense_right(left, right):
    return lax.dot_general(
        left, right, (((1,), (1,)), ((), ())), preferred_element_type=jnp.float32
    )


def norm_parts(value):
    mean = jnp.mean(value, axis=-1, keepdims=True)
    centred = value - mean
    inverse = lax.rsqrt(jnp.mean(centred * centred, axis=-1, keepdims=True) + EPSILON)
    return (centred * inverse, inverse)


def norm_back(grad, scaled, inverse, gain):
    shaped = grad * gain
    inner = jnp.mean(shaped * scaled, axis=-1, keepdims=True)
    return inverse * (shaped - jnp.mean(shaped, axis=-1, keepdims=True) - scaled * inner)


def gelu_value(value):
    return 0.5 * value * (1.0 + jnp.tanh(SLOPE * (value + CUBIC * value * value * value)))


def gelu_slope(value):
    bent = jnp.tanh(SLOPE * (value + CUBIC * value * value * value))
    return 0.5 * (1.0 + bent) + 0.5 * value * (1.0 - bent * bent) * SLOPE * (
        1.0 + 3.0 * CUBIC * value * value
    )


def per_device_plain(
    tokens,
    lengths,
    w_qkv,
    w_out,
    w_up,
    w_down,
    bias_q,
    bias_v,
    bias_out,
    bias_up,
    bias_down,
    gain_one,
    shift_one,
    gain_two,
    shift_two,
    cotangent,
):
    width = tokens.shape[1]
    rows = tokens.shape[0]
    pair = lax.axis_size("seq")
    rank = lax.axis_index("seq")
    group = rows * pair
    local = width // pair
    heads = local // HEAD_DIM
    scale = HEAD_DIM ** (-0.5)
    block = 512
    blocks = group // block
    whole = (
        lax.all_gather(w_qkv, "dp", axis=0, tiled=True),
        lax.all_gather(w_out, "dp", axis=0, tiled=True),
        lax.all_gather(w_up, "dp", axis=0, tiled=True),
        lax.all_gather(w_down, "dp", axis=0, tiled=True),
        lax.all_gather(bias_q, "dp", axis=0, tiled=True),
        lax.all_gather(bias_v, "dp", axis=0, tiled=True),
        lax.all_gather(bias_out, "dp", axis=0, tiled=True),
        lax.all_gather(bias_up, "dp", axis=0, tiled=True),
        lax.all_gather(bias_down, "dp", axis=0, tiled=True),
        lax.all_gather(gain_one, "dp", axis=0, tiled=True),
        lax.all_gather(shift_one, "dp", axis=0, tiled=True),
        lax.all_gather(gain_two, "dp", axis=0, tiled=True),
        lax.all_gather(shift_two, "dp", axis=0, tiled=True),
    )
    weight_qkv, weight_out, weight_up, weight_down = whole[0:4]
    add_q, add_v, add_out, add_up, add_down, scale_one, move_one, scale_two, move_two = [
        piece.astype(jnp.float32) for piece in whole[4:]
    ]
    slots = lengths.shape[1]
    position = jnp.arange(group, dtype=jnp.int32)
    ends = jnp.cumsum(lengths[0])
    segment = jnp.sum((position[:, None] >= ends[None, :]).astype(jnp.int32), axis=1)
    own_segment = lax.dynamic_slice_in_dim(segment, rank * rows, rows)
    valid = (own_segment < slots - 1)[:, None]
    inputs = tokens.astype(jnp.float32)
    scaled_one, inverse_one = norm_parts(inputs)
    first = (scaled_one * scale_one + move_one).astype(jnp.bfloat16)
    bias_qkv = jnp.concatenate([add_q, jnp.zeros_like(add_q), add_v])
    qkv = (dense(first, weight_qkv) + bias_qkv).astype(jnp.bfloat16)
    head_side = lax.all_to_all(
        qkv.reshape(rows, 3, pair, local), "seq", split_axis=2, concat_axis=0, tiled=True
    )
    query = head_side[:, 0, 0].reshape(group, heads, HEAD_DIM)
    keys = head_side[:, 1, 0].reshape(group, heads, HEAD_DIM)
    values = head_side[:, 2, 0].reshape(group, heads, HEAD_DIM)

    def block_scores(index):
        start = index * block
        query_rows = lax.dynamic_slice_in_dim(query, start, block)
        raw = (
            jnp.einsum("qhd,khd->hqk", query_rows, keys, preferred_element_type=jnp.float32) * scale
        )
        row_segment = lax.dynamic_slice_in_dim(segment, start, block)
        row_position = lax.dynamic_slice_in_dim(position, start, block)
        allowed = (row_segment[:, None] == segment[None, :]) & (
            position[None, :] <= row_position[:, None]
        )
        return (jnp.where(allowed[None], raw, MASKED), query_rows)

    def attend(index):
        scores, unused = block_scores(index)
        top = jnp.max(scores, axis=-1, keepdims=True)
        weights = jnp.exp(scores - top)
        total = jnp.sum(weights, axis=-1, keepdims=True)
        probs = (weights / total).astype(jnp.bfloat16)
        mixed_rows = jnp.einsum("hqk,khd->qhd", probs, values, preferred_element_type=jnp.float32)
        return (
            mixed_rows.reshape(block, local).astype(jnp.bfloat16),
            (top + jnp.log(total))[:, :, 0],
        )

    mixed_blocks, log_totals = lax.map(attend, jnp.arange(blocks))
    mixed_head = mixed_blocks.reshape(group, 1, local)
    mixed = lax.all_to_all(mixed_head, "seq", split_axis=0, concat_axis=1, tiled=True).reshape(
        rows, width
    )
    middle = inputs + dense(mixed, weight_out) + add_out
    scaled_two, inverse_two = norm_parts(middle)
    second = (scaled_two * scale_two + move_two).astype(jnp.bfloat16)
    pre = dense(second, weight_up) + add_up
    hidden = gelu_value(pre).astype(jnp.bfloat16)
    result = middle + dense(hidden, weight_down) + add_down
    block_out = jnp.where(valid, result, 0.0).astype(jnp.bfloat16)
    grad_out = jnp.where(valid, cotangent, jnp.zeros_like(cotangent))
    grad_weight_down = dense_left(hidden, grad_out)
    grad_add_down = jnp.sum(grad_out.astype(jnp.float32), axis=0)
    grad_pre = (dense_right(grad_out, weight_down) * gelu_slope(pre)).astype(jnp.bfloat16)
    grad_weight_up = dense_left(second, grad_pre)
    grad_add_up = jnp.sum(grad_pre.astype(jnp.float32), axis=0)
    grad_second = dense_right(grad_pre, weight_up)
    grad_scale_two = jnp.sum(grad_second * scaled_two, axis=0)
    grad_move_two = jnp.sum(grad_second, axis=0)
    grad_middle = grad_out.astype(jnp.float32) + norm_back(
        grad_second, scaled_two, inverse_two, scale_two
    )
    grad_attn = grad_middle.astype(jnp.bfloat16)
    grad_weight_out = dense_left(mixed, grad_attn)
    grad_add_out = jnp.sum(grad_attn.astype(jnp.float32), axis=0)
    grad_mixed = dense_right(grad_attn, weight_out).astype(jnp.bfloat16)
    branch_grads = (
        grad_weight_out,
        grad_weight_up,
        grad_weight_down,
        grad_add_out,
        grad_add_up,
        grad_add_down,
        grad_scale_two,
        grad_move_two,
    )
    grad_head = lax.all_to_all(
        grad_mixed.reshape(rows, pair, local), "seq", split_axis=1, concat_axis=0, tiled=True
    )
    grad_head = grad_head.reshape(group, heads, HEAD_DIM)

    def attend_back(carry, index):
        grad_keys, grad_values = carry
        scores, query_rows = block_scores(index)
        probs = jnp.exp(scores - log_totals[index][:, :, None])
        grad_rows = lax.dynamic_slice_in_dim(grad_head, index * block, block)
        grad_probs = jnp.einsum(
            "qhd,khd->hqk", grad_rows, values, preferred_element_type=jnp.float32
        )
        centre = jnp.sum(probs * grad_probs, axis=-1, keepdims=True)
        grad_scores = (probs * (grad_probs - centre)).astype(jnp.bfloat16)
        grad_values = grad_values + jnp.einsum(
            "hqk,qhd->khd",
            probs.astype(jnp.bfloat16),
            grad_rows,
            preferred_element_type=jnp.float32,
        )
        grad_keys = (
            grad_keys
            + jnp.einsum(
                "hqk,qhd->khd", grad_scores, query_rows, preferred_element_type=jnp.float32
            )
            * scale
        )
        grad_query = (
            jnp.einsum("hqk,khd->qhd", grad_scores, keys, preferred_element_type=jnp.float32)
            * scale
        )
        return ((grad_keys, grad_values), grad_query)

    empty = jnp.zeros((group, heads, HEAD_DIM), jnp.float32)
    (grad_keys, grad_values), grad_queries = lax.scan(
        attend_back, (empty, empty), jnp.arange(blocks)
    )
    grad_side = jnp.stack(
        [
            grad_queries.reshape(group, local),
            grad_keys.reshape(group, local),
            grad_values.reshape(group, local),
        ],
        axis=1,
    ).astype(jnp.bfloat16)
    grad_qkv = lax.all_to_all(
        grad_side.reshape(group, 3, 1, local), "seq", split_axis=0, concat_axis=2, tiled=True
    )
    grad_qkv = grad_qkv.reshape(rows, 3 * width)
    grad_weight_qkv = dense_left(first, grad_qkv)
    column_sums = jnp.sum(grad_qkv.astype(jnp.float32), axis=0)
    grad_add_q = column_sums[:width]
    grad_add_v = column_sums[2 * width :]
    grad_first = dense_right(grad_qkv, weight_qkv)
    grad_scale_one = jnp.sum(grad_first * scaled_one, axis=0)
    grad_move_one = jnp.sum(grad_first, axis=0)
    grad_tokens = grad_middle + norm_back(grad_first, scaled_one, inverse_one, scale_one)
    stem_grads = (grad_weight_qkv, grad_add_q, grad_add_v, grad_scale_one, grad_move_one)
    halves = lax.psum_scatter(
        stem_grads + branch_grads, ("dp", "seq"), scatter_dimension=0, tiled=True
    )
    shares = jax.tree.map(
        lambda part, own: part.astype(own.dtype),
        lax.all_gather(as_sent(halves), "seq", axis=0, tiled=True),
        halves,
    )
    stem_shares = shares[0:5]
    branch_shares = shares[5:13]
    return (
        block_out,
        grad_tokens,
        stem_shares[0],
        branch_shares[0],
        branch_shares[1],
        branch_shares[2],
        stem_shares[1],
        stem_shares[2],
        branch_shares[3],
        branch_shares[4],
        branch_shares[5],
        stem_shares[3],
        stem_shares[4],
        branch_shares[6],
        branch_shares[7],
    )


FAR = pl.DeviceIdType.MESH
NT = (((1,), (1,)), ((), ()))
BF = jnp.bfloat16
F32 = jnp.float32


def mul(left, right):
    return jnp.dot(left, right, preferred_element_type=F32)


def mul_nt(left, right):
    return lax.dot_general(left, right, NT, preferred_element_type=F32)


def flat(blocks):
    return blocks.reshape(blocks.shape[0] * blocks.shape[1], blocks.shape[2])


def normed(value):
    width = value.shape[1]
    mean = jnp.sum(value, axis=1, keepdims=True) * (1.0 / width)
    centred = value - mean
    spread = jnp.sum(centred * centred, axis=1, keepdims=True) * (1.0 / width)
    inverse = lax.rsqrt(spread + EPSILON)
    return (centred * inverse, inverse)


def normed_back(grad, scaled, inverse, gain):
    width = grad.shape[1]
    shaped = grad * gain
    inner = jnp.sum(shaped * scaled, axis=1, keepdims=True) * (1.0 / width)
    outer = jnp.sum(shaped, axis=1, keepdims=True) * (1.0 / width)
    return inverse * (shaped - outer - scaled * inner)


def column_sum(value):
    return jnp.sum(value, axis=0, keepdims=True)


class Numbers:
    def __init__(self):
        self.used = 0

    def take(self, count):
        start = self.used
        self.used = start + count
        return start


BIAS_Q, BIAS_V, BIAS_OUT, BIAS_DOWN, GAIN_1, SHIFT_1, GAIN_2, SHIFT_2, BIAS_UP = range(9)
TABLE = 16
FAR_COUNT = 160
NEAR_COUNT = 32


def fused_kernel(
    lengths, table, tok, cot, own_q, own_o, own_u, own_d,
    out, gtok, out_q, out_o, out_u, out_d, out_v,
    wq, wo, wu, wd, gwq,
    tok_far, first, first_t, qkv, k_t, v_t, lower, lse, o_t,
    mixed_near, mixed, mixed_t, middle, second, second_t, gout, result,
    hidden, hidden_t, gpre, gmix, gmix_head, gattn, dk, dv, dq_t, gqkv,
    e_own, e_z, e_y, e_c, vec, gvec, v_z, v_y, v_c, v_x, v_sum,
    r1_d, r2_d, r3_d, r5_d, r1_u, r2_u, r3_u, r5_u,
    r1_o, r2_o, r3_o, r5_o, r1_q, r2_q, r3_q, r5_q,
    gf_send, gf_recv,
    near_sem, send_sem, recv_sem,
):
    d = lax.axis_index("dp")
    s = lax.axis_index("seq")
    z = lax.div(d, 4)
    y = lax.rem(lax.div(d, 2), 2)
    c = lax.rem(d, 2)
    zs = wq.shape[0]
    rows, width = tok.shape
    group = 2 * rows
    local = width // 2
    pairs = local // 128
    rq = width // (4 * zs)
    rd = own_d.shape[0]
    tile = 4 * rd
    tiles = zs
    z_peers = [(lax.rem(z + dz, zs) * 4 + y * 2 + c, s) for dz in range(1, zs)]
    y_peer = (z * 4 + (1 - y) * 2 + c, s)
    c_peer = (z * 4 + y * 2 + (1 - c), s)
    x_peer = (d, 1 - s)
    number = Numbers()
    local_number = Numbers()

    def far(src, dst, slot, device):
        return pltpu.make_async_remote_copy(
            src_ref=src, dst_ref=dst, send_sem=send_sem.at[slot], recv_sem=recv_sem.at[slot],
            device_id=device, device_id_type=FAR,
        )

    def z_at(dz):
        return lax.rem(z + zs - dz, zs)

    def loop(count, body):
        lax.fori_loop(0, count, lambda i, carry: (body(i), carry)[1], 0)

    def block_rows(r, yy, cc):
        return pl.ds(pl.multiple_of((yy * 2 + cc) * r, r), r)

    barrier = pltpu.get_barrier_semaphore()
    everyone = z_peers + [y_peer, c_peer, x_peer]
    for peer in everyone:
        pl.semaphore_signal(barrier, inc=1, device_id=peer, device_id_type=FAR)
    pl.semaphore_wait(barrier, len(everyone))

    class Gather:
        def __init__(self, ref, r, columns, base):
            self.ref, self.r, self.columns, self.base = ref, r, columns, base

        def part(self, zz, yy, cc):
            return self.ref.at[zz, block_rows(self.r, yy, cc), self.columns]

        def layer(self, yy, cc):
            return self.ref.at[:, block_rows(self.r, yy, cc), self.columns]

        def z_copy(self, dz):
            return far(self.part(z, y, c), self.part(z, y, c), self.base + dz - 1, z_peers[dz - 1])

        def z_start(self):
            for dz in range(1, zs):
                self.z_copy(dz).start()

        def z_wait(self):
            for dz in range(1, zs):
                block = self.part(z_at(dz), y, c)
                far(block, block, self.base + dz - 1, z_peers[dz - 1]).wait_recv()

        def y_copy(self, yy):
            return far(self.layer(yy, c), self.layer(yy, c), self.base + zs - 1, y_peer)

        def c_copy(self, yy, cc, other):
            return far(self.layer(yy, cc), self.layer(yy, cc), self.base + zs + other, c_peer)

        def relay(self):
            self.z_wait()
            self.y_copy(y).start()
            self.c_copy(y, c, 0).start()

        def relay_y(self):
            self.y_copy(1 - y).wait_recv()
            self.c_copy(1 - y, c, 1).start()

        def finish(self):
            self.c_copy(y, 1 - c, 0).wait_recv()
            self.c_copy(1 - y, 1 - c, 1).wait_recv()

        def sent(self):
            for dz in range(1, zs):
                self.z_copy(dz).wait_send()
            self.y_copy(y).wait_send()
            self.c_copy(y, c, 0).wait_send()
            self.c_copy(1 - y, c, 1).wait_send()

    steps = zs + 2
    base_q = number.take(pairs * steps)

    def gather_q(p):
        return Gather(wq, rq, pl.ds(pl.multiple_of(p * local, 128), local), base_q + p * steps)

    gather_o = Gather(wo, rq, pl.ds(0, width), number.take(steps))
    halves_u = 2
    span_u = wu.shape[2] // halves_u
    gather_u = [Gather(wu, rq, pl.ds(i * span_u, span_u), number.take(steps)) for i in range(halves_u)]
    gather_d = Gather(wd, rd, pl.ds(0, width), number.take(steps))

    near_q = []
    for p in range(pairs):
        for part in range(3):
            start = pl.multiple_of(part * width + s * local + p * 128, 128)
            near_q.append(
                pltpu.make_async_copy(
                    own_q.at[:, pl.ds(start, 128)],
                    wq.at[z, block_rows(rq, y, c), pl.ds(p * local + part * 128, 128)],
                    near_sem.at[local_number.take(1)],
                )
            )
    near_rest = []
    for own, whole, r in ((own_o, wo, rq), (own_u, wu, rq), (own_d, wd, rd)):
        near_rest.append(
            pltpu.make_async_copy(
                own, whole.at[z, block_rows(r, y, c), :], near_sem.at[local_number.take(1)]
            )
        )
    for copy in near_q + near_rest:
        copy.start()

    base_e = number.take(zs + 1)
    for dz in range(1, zs):
        far(table, e_z.at[dz - 1], base_e + dz - 1, z_peers[dz - 1]).start()
    send_tok = far(tok, tok_far, number.take(1), x_peer)
    send_tok.start()
    for copy in near_q:
        copy.wait()
    for p in range(pairs):
        gather_q(p).z_start()

    for dz in range(1, zs):
        far(table, e_z.at[dz - 1], base_e + dz - 1, z_peers[dz - 1]).wait_recv()
    total = table[...].astype(F32)
    for dz in range(1, zs):
        total = total + e_z[dz - 1].astype(F32)
    e_own[0] = total.astype(BF)
    y_table = far(e_own.at[0], e_y, base_e + zs - 1, y_peer)
    y_table.start()

    ends = []
    end = jnp.int32(0)
    for j in range(lengths.shape[1]):
        end = end + lengths[0, j]
        ends.append(end)
    position = lax.broadcasted_iota(jnp.int32, (1, group), 1)
    start = jnp.zeros((1, group), jnp.int32)
    for end in ends[:-1]:
        start = jnp.where(position >= end, end, start)
    lower[...] = start
    last_valid = ends[-2]

    y_table.wait_recv()
    total = total + e_y[...].astype(F32)
    e_own[1] = total.astype(BF)
    c_table = far(e_own.at[1], e_c, base_e + zs, c_peer)
    c_table.start()
    c_table.wait_recv()
    total = total + e_c[...].astype(F32)
    for i in range(TABLE):
        vec[i] = total[i : i + 1, :]

    def first_norm(source, at):
        def body(i):
            x = source[pl.ds(pl.multiple_of(i * 128, 128), 128), :].astype(F32)
            scaled, unused = normed(x)
            value = (scaled * vec[GAIN_1] + vec[SHIFT_1]).astype(BF)
            there = pl.ds(pl.multiple_of(at + i * 128, 128), 128)
            first[there, :] = value
            first_t[:, there] = value.T

        loop(rows // 128, body)

    first_norm(tok, s * rows)

    for p in range(pairs):
        gather_q(p).relay()
    for copy in near_rest:
        copy.wait()
    gather_o.z_start()
    for part in gather_u:
        part.z_start()

    send_tok.wait_recv()
    first_norm(tok_far, (1 - s) * rows)

    base_mixed = number.take(pairs)
    near_mixed = local_number.take(pairs)

    def lanes(p, part):
        return pl.ds(pl.multiple_of(p * local + part * 128, 128), 128)

    def send_mixed(p):
        there = pl.ds(pl.multiple_of(s * local + p * 128, 128), 128)
        here = pl.ds(pl.multiple_of(p * 128, 128), 128)
        away = pl.ds(pl.multiple_of((1 - s) * rows, 128), rows)
        return far(mixed_near.at[away, here], mixed.at[:, there], base_mixed + p, x_peer)

    def keep_mixed(p):
        there = pl.ds(pl.multiple_of(s * local + p * 128, 128), 128)
        here = pl.ds(pl.multiple_of(p * 128, 128), 128)
        stay = pl.ds(pl.multiple_of(s * rows, 128), rows)
        return pltpu.make_async_copy(
            mixed_near.at[stay, here], mixed.at[:, there], near_sem.at[near_mixed + p]
        )

    side = 256
    blocks = group // side
    key_at = lax.broadcasted_iota(jnp.int32, (side, side), 0)
    query_at = lax.broadcasted_iota(jnp.int32, (side, side), 1)
    lane = lax.broadcasted_iota(jnp.int32, (side, 128), 1)

    def head_lanes(value, h):
        inside = (lane >= h * HEAD_DIM) & (lane < h * HEAD_DIM + HEAD_DIM)
        return jnp.where(inside, value, 0.0).astype(BF)

    def scores(p, keys_block, query, qi, j):
        raw = mul_nt(keys_block, query)
        ok = key_at + j * side >= lower[:, qi * side : (qi + 1) * side]
        if j == qi:
            ok = ok & (key_at <= query_at)
        return jnp.where(ok, raw, MASKED)

    scale = HEAD_DIM ** (-0.5)

    def attend(p):
        def head(h):
            half = pl.ds(pl.multiple_of(h * HEAD_DIM, HEAD_DIM), HEAD_DIM)
            for qi in range(blocks):
                query = head_lanes(
                    qkv[qi * side : (qi + 1) * side, lanes(p, 0)].astype(F32) * scale, h
                )
                raw = []
                top = None
                for j in range(qi + 1):
                    block = scores(p, qkv[j * side : (j + 1) * side, lanes(p, 1)], query, qi, j)
                    raw.append(block)
                    high = jnp.max(block, axis=0, keepdims=True)
                    top = high if top is None else jnp.maximum(top, high)
                amount = jnp.zeros((1, side), F32)
                gathered = jnp.zeros((HEAD_DIM, side), F32)
                for j in range(qi + 1):
                    weight = jnp.exp(raw[j] - top)
                    amount = amount + column_sum(weight)
                    gathered = gathered + mul(
                        v_t[p, half, j * side : (j + 1) * side], weight.astype(BF)
                    )
                o_t[half, qi * side : (qi + 1) * side] = gathered / amount
                lse[p, h, :, qi * side : (qi + 1) * side] = top + jnp.log(amount)

        loop(2, head)
        here = pl.ds(pl.multiple_of(p * 128, 128), 128)
        for qi in range(blocks):
            at = slice(qi * side, (qi + 1) * side)
            mixed_near[at, here] = o_t[:, at].T.astype(BF)

    def project(p):
        zero = jnp.zeros((1, 128), F32)
        there = pl.ds(pl.multiple_of(s * local + p * 128, 128), 128)
        bias = jnp.concatenate([vec[BIAS_Q, :, there], zero, vec[BIAS_V, :, there]], axis=1)
        weight = flat(wq[:, :, pl.ds(pl.multiple_of(p * local, 128), local)])

        def body(i):
            at = pl.ds(pl.multiple_of(i * side, side), side)
            value = (mul(first[at, :], weight) + bias).astype(BF)
            qkv[at, pl.ds(pl.multiple_of(p * local, 128), local)] = value
            k_t[p, :, at] = value[:, 128:256].T
            v_t[p, :, at] = value[:, 256:384].T

        loop(blocks, body)

    def pair_forward(p):
        gather_q(p).relay_y()
        gather_q(p).finish()
        project(p)
        attend(p)
        send_mixed(p).start()
        keep_mixed(p).start()

        @pl.when(p == 0)
        def _():
            gather_o.relay()
            gather_u[0].relay()

        @pl.when(p == 1)
        def _():
            gather_u[1].relay()
            gather_d.z_start()

    loop(pairs, pair_forward)

    gather_o.relay_y()
    gather_u[0].relay_y()
    gather_o.finish()
    for p in range(pairs):
        keep_mixed(p).wait()
    for p in range(pairs):
        far(
            mixed_near.at[pl.ds(0, rows), pl.ds(0, 128)],
            mixed.at[:, pl.ds(pl.multiple_of((1 - s) * local + p * 128, 128), 128)],
            base_mixed + p, x_peer,
        ).wait_recv()

    def project_out(i):
        at = pl.ds(pl.multiple_of(i * 128, 128), 128)
        near = mixed[at, :]
        mixed_t[:, at] = near.T
        value = tok[at, :].astype(F32) + mul(near, flat(wo[...])) + vec[BIAS_OUT]
        middle[at, :] = value
        result[at, :] = value + vec[BIAS_DOWN]
        scaled, unused = normed(value)
        rounded = (scaled * vec[GAIN_2] + vec[SHIFT_2]).astype(BF)
        second[at, :] = rounded
        second_t[:, at] = rounded.T
        spot = s * rows + i * 128 + lax.broadcasted_iota(jnp.int32, (128, width), 0)
        gout[at, :] = jnp.where(spot < last_valid, cot[at, :].astype(F32), 0.0).astype(BF)
        gtok[at, :] = jnp.zeros((128, width), F32)

    loop(rows // 128, project_out)

    gather_u[1].relay_y()
    gather_d.relay()
    gather_u[0].finish()
    gather_u[1].finish()
    gather_d.relay_y()
    gather_d.finish()
    for part in gather_u + [gather_d]:
        part.sent()

    base_sib = number.take(tiles * 4)
    base_ys = number.take(tiles * 2)
    base_zd = number.take(zs - 1)
    base_zu = number.take(tiles * (zs - 1))
    base_xs = number.take(2)

    def tile_lanes(t):
        return pl.ds(pl.multiple_of(t * tile, 128), tile)

    def sib_d(t, yy):
        return far(
            wd.at[t, block_rows(rd, yy, 1 - c), :],
            r1_d.at[t, pl.ds(pl.multiple_of(yy * rd, rd), rd), :],
            base_sib + t * 4 + yy, c_peer,
        )

    def sib_u(t, yy):
        return far(
            wu.at[:, block_rows(rq, yy, 1 - c), tile_lanes(t)],
            r1_u.at[:, pl.ds(pl.multiple_of(yy * rq, rq), rq), tile_lanes(t)],
            base_sib + t * 4 + 2 + yy, c_peer,
        )

    def sib_start(t):
        for yy in (1 - y, y):
            sib_d(t, yy).start()
            sib_u(t, yy).start()

    def y_d(t):
        return far(
            r1_d.at[t, pl.ds(pl.multiple_of((1 - y) * rd, rd), rd), :], r2_d.at[t],
            base_ys + t * 2, y_peer,
        )

    def y_u(t):
        return far(
            r1_u.at[:, pl.ds(pl.multiple_of((1 - y) * rq, rq), rq), tile_lanes(t)],
            r2_u.at[:, :, tile_lanes(t)], base_ys + t * 2 + 1, y_peer,
        )

    def y_start(t):
        yy = 1 - y
        sib_d(t, yy).wait_recv()
        at = pl.ds(pl.multiple_of(yy * rd, rd), rd)
        r1_d[t, at, :] = (
            r1_d[t, at, :].astype(F32) + wd[t, block_rows(rd, yy, c), :].astype(F32)
        ).astype(BF)
        sib_u(t, yy).wait_recv()
        at = pl.ds(pl.multiple_of(yy * rq, rq), rq)
        for zz in range(zs):
            r1_u[zz, at, tile_lanes(t)] = (
                r1_u[zz, at, tile_lanes(t)].astype(F32)
                + wu[zz, block_rows(rq, yy, c), tile_lanes(t)].astype(F32)
            ).astype(BF)
        y_d(t).start()
        y_u(t).start()

    def z_d(t, dz):
        return far(r2_d.at[t], r3_d.at[dz - 1], base_zd + dz - 1, (t * 4 + y * 2 + c, s))

    def z_u(t, dz):
        return far(
            r2_u.at[lax.rem(z + dz, zs), :, tile_lanes(t)], r3_u.at[dz - 1, :, tile_lanes(t)],
            base_zu + t * (zs - 1) + dz - 1, z_peers[dz - 1],
        )

    def z_start(t):
        sib_d(t, y).wait_recv()
        y_d(t).wait_recv()
        at = pl.ds(pl.multiple_of(y * rd, rd), rd)
        r2_d[t] = (
            r2_d[t].astype(F32)
            + r1_d[t, at, :].astype(F32)
            + wd[t, block_rows(rd, y, c), :].astype(F32)
        ).astype(BF)
        sib_u(t, y).wait_recv()
        y_u(t).wait_recv()
        at = pl.ds(pl.multiple_of(y * rq, rq), rq)
        for zz in range(zs):
            r2_u[zz, :, tile_lanes(t)] = (
                r2_u[zz, :, tile_lanes(t)].astype(F32)
                + r1_u[zz, at, tile_lanes(t)].astype(F32)
                + wu[zz, block_rows(rq, y, c), tile_lanes(t)].astype(F32)
            ).astype(BF)
        dz = lax.rem(t + zs - z, zs)

        @pl.when(dz > 0)
        def _():
            z_d(t, dz).start()

        for step in range(1, zs):
            z_u(t, step).start()

    sub = 256

    def feed(t):
        def part(u):
            at = pl.ds(pl.multiple_of(t * tile + u * sub, 128), sub)
            near = pl.ds(pl.multiple_of(u * sub, sub), sub)
            pre = mul(second[...], flat(wu[:, :, at])) + vec[BIAS_UP + t, :, near]
            bent = jnp.tanh(SLOPE * (pre + CUBIC * pre * pre * pre))
            value = (0.5 * pre * (1.0 + bent)).astype(BF)
            slope = 0.5 * (1.0 + bent) + 0.5 * pre * (1.0 - bent * bent) * SLOPE * (
                1.0 + 3.0 * CUBIC * pre * pre
            )
            hidden[:, near] = value
            hidden_t[near, :] = value.T
            grad = (mul_nt(gout[...], wd[t, near, :]) * slope).astype(BF)
            gpre[:, near] = grad
            gvec[BIAS_UP + t, :, near] = column_sum(grad.astype(F32))

        loop(tile // sub, part)

        def add(i):
            at = pl.ds(pl.multiple_of(i * side, side), side)
            result[at, :] += mul(hidden[at, :], wd[t])
            gtok[at, :] += mul_nt(gpre[at, :], flat(wu[:, :, tile_lanes(t)]))

        loop(rows // side, add)

        def weigh(m):
            at = pl.ds(pl.multiple_of(m * rd, rd), rd)
            wd[t, at, :] = mul(hidden_t[at, :], gout[...]).astype(BF)

        loop(4, weigh)

        def weigh_up(m):
            at = pl.ds(pl.multiple_of(m * 4 * rq, 4 * rq), 4 * rq)
            wu[m, :, tile_lanes(t)] = mul(second_t[at, :], gpre[...]).astype(BF)

        loop(zs, weigh_up)
        sib_start(t)

        @pl.when(t > 0)
        def _():
            y_start(t - 1)

    loop(tiles, feed)

    for row in (BIAS_Q, BIAS_V, BIAS_OUT, BIAS_DOWN, GAIN_1, SHIFT_1, GAIN_2, SHIFT_2):
        gvec[row] = jnp.zeros((1, width), F32)
    for row in range(BIAS_UP + tiles, TABLE):
        gvec[row] = jnp.zeros((1, width), F32)

    def middle_back(i):
        at = pl.ds(pl.multiple_of(i * 128, 128), 128)
        scaled, inverse = normed(middle[at, :])
        grad = gtok[at, :]
        ahead = gout[at, :].astype(F32)
        gvec[GAIN_2] += column_sum(grad * scaled)
        gvec[SHIFT_2] += column_sum(grad)
        gvec[BIAS_DOWN] += column_sum(ahead)
        total = ahead + normed_back(grad, scaled, inverse, vec[GAIN_2])
        middle[at, :] = total
        rounded = total.astype(BF)
        gattn[at, :] = rounded
        gvec[BIAS_OUT] += column_sum(rounded.astype(F32))
        gmix[at, :] = mul_nt(rounded, flat(wo[...])).astype(BF)
        spot = s * rows + i * 128 + lax.broadcasted_iota(jnp.int32, (128, width), 0)
        out[at, :] = jnp.where(spot < last_valid, result[at, :], 0.0).astype(BF)

    loop(rows // 128, middle_back)

    slot_gmix = number.take(1)
    send_gmix = far(
        gmix.at[:, pl.ds(pl.multiple_of((1 - s) * local, 128), local)],
        gmix_head.at[pl.ds(pl.multiple_of(s * rows, 128), rows), :],
        slot_gmix, x_peer,
    )
    keep_gmix = pltpu.make_async_copy(
        gmix.at[:, pl.ds(pl.multiple_of(s * local, 128), local)],
        gmix_head.at[pl.ds(pl.multiple_of(s * rows, 128), rows), :],
        near_sem.at[local_number.take(1)],
    )
    send_gmix.start()
    keep_gmix.start()
    y_start(tiles - 1)

    gather_o.sent()

    def weigh_out(m):
        at = pl.ds(pl.multiple_of(m * 4 * rq, 4 * rq), 4 * rq)
        wo[m] = mul(mixed_t[at, :], gattn[...]).astype(BF)

    loop(zs, weigh_out)

    class Spread:
        def __init__(self, ref, columns, r1, r2, r3, base):
            self.ref, self.columns, self.r1, self.r2, self.r3 = ref, columns, r1, r2, r3
            self.base = base

        def sib(self, yy):
            return far(
                self.ref.at[:, block_rows(rq, yy, 1 - c), self.columns],
                self.r1.at[:, pl.ds(pl.multiple_of(yy * rq, rq), rq), self.columns],
                self.base + yy, c_peer,
            )

        def sib_start(self):
            self.sib(1 - y).start()
            self.sib(y).start()

        def along_y(self):
            return far(
                self.r1.at[:, pl.ds(pl.multiple_of((1 - y) * rq, rq), rq), self.columns],
                self.r2.at[:, :, self.columns], self.base + 2, y_peer,
            )

        def y_start(self):
            self.sib(1 - y).wait_recv()
            at = pl.ds(pl.multiple_of((1 - y) * rq, rq), rq)
            for zz in range(zs):
                self.r1[zz, at, self.columns] = (
                    self.r1[zz, at, self.columns].astype(F32)
                    + self.ref[zz, block_rows(rq, 1 - y, c), self.columns].astype(F32)
                ).astype(BF)
            self.along_y().start()

        def along_z(self, dz):
            return far(
                self.r2.at[lax.rem(z + dz, zs), :, self.columns],
                self.r3.at[dz - 1, :, self.columns], self.base + 2 + dz, z_peers[dz - 1],
            )

        def z_start(self):
            self.sib(y).wait_recv()
            self.along_y().wait_recv()
            at = pl.ds(pl.multiple_of(y * rq, rq), rq)
            for zz in range(zs):
                self.r2[zz, :, self.columns] = (
                    self.r2[zz, :, self.columns].astype(F32)
                    + self.r1[zz, at, self.columns].astype(F32)
                    + self.ref[zz, block_rows(rq, y, c), self.columns].astype(F32)
                ).astype(BF)
            for dz in range(1, zs):
                self.along_z(dz).start()

        def z_finish(self):
            total = self.r2[z, :, self.columns].astype(F32)
            for dz in range(1, zs):
                self.along_z(dz).wait_recv()
                total = total + self.r3[dz - 1, :, self.columns].astype(F32)
            return total

        def sent(self):
            self.sib(0).wait_send()
            self.sib(1).wait_send()
            self.along_y().wait_send()
            for dz in range(1, zs):
                self.along_z(dz).wait_send()

    spread_steps = zs + 2
    sum_o = Spread(wo, pl.ds(0, width), r1_o, r2_o, r3_o, number.take(spread_steps))
    base_sq = number.take(pairs * spread_steps)

    def sum_q(p):
        return Spread(
            gwq, pl.ds(pl.multiple_of(p * local, 128), local), r1_q, r2_q, r3_q,
            base_sq + p * spread_steps,
        )

    sum_o.sib_start()
    send_gmix.wait_send()
    keep_gmix.wait()
    far(
        gmix.at[:, pl.ds(0, local)],
        gmix_head.at[pl.ds(pl.multiple_of((1 - s) * rows, 128), rows), :],
        slot_gmix, x_peer,
    ).wait_recv()
    sum_o.y_start()

    def attend_back(p):
        dk[...] = jnp.zeros_like(dk)
        dv[...] = jnp.zeros_like(dv)

        def head(h):
            half = pl.ds(pl.multiple_of(h * HEAD_DIM, HEAD_DIM), HEAD_DIM)
            here = pl.ds(pl.multiple_of(p * 128, 128), 128)
            for qi in range(blocks):
                at = slice(qi * side, (qi + 1) * side)
                query = head_lanes(qkv[at, lanes(p, 0)].astype(F32) * scale, h)
                grad = head_lanes(gmix_head[at, here].astype(F32), h)
                level = lse[p, h, :, at]
                weights, slopes = [], []
                centre = jnp.zeros((1, side), F32)
                for j in range(qi + 1):
                    there = slice(j * side, (j + 1) * side)
                    raw = scores(p, qkv[there, lanes(p, 1)], query, qi, j)
                    weight = jnp.exp(raw - level)
                    slope = mul_nt(qkv[there, lanes(p, 2)], grad)
                    centre = centre + column_sum(weight * slope)
                    weights.append(weight)
                    slopes.append(slope)
                total = jnp.zeros((HEAD_DIM, side), F32)
                for j in range(qi + 1):
                    there = slice(j * side, (j + 1) * side)
                    bend = (weights[j] * (slopes[j] - centre)).astype(BF)
                    dk[there, :] += mul(bend, query)
                    dv[there, :] += mul(weights[j].astype(BF), grad)
                    total = total + mul(k_t[p, half, there], bend)
                dq_t[half, at] = total * scale

        loop(2, head)
        for qi in range(blocks):
            at = slice(qi * side, (qi + 1) * side)
            gqkv[at, lanes(p, 0)] = dq_t[:, at].T.astype(BF)
            gqkv[at, lanes(p, 1)] = dk[at, :].astype(BF)
            gqkv[at, lanes(p, 2)] = dv[at, :].astype(BF)
        own = pl.ds(pl.multiple_of(s * local + p * 128, 128), 128)
        gvec[BIAS_Q, :, own] = column_sum(gqkv[:, lanes(p, 0)].astype(F32))
        gvec[BIAS_V, :, own] = column_sum(gqkv[:, lanes(p, 2)].astype(F32))
        both = pl.ds(pl.multiple_of(p * local, 128), local)

        def weigh(m):
            at = pl.ds(pl.multiple_of(m * 4 * rq, 4 * rq), 4 * rq)
            gwq[m, :, both] = mul(first_t[at, :], gqkv[:, both]).astype(BF)

        loop(zs, weigh)

    def pair_back(p):
        z_start(p)
        attend_back(p)
        sum_q(p).sib_start()

        @pl.when(p > 0)
        def _():
            sum_q(p - 1).y_start()

    loop(pairs, pair_back)

    base_gf = number.take(rows // side)

    def send_gf(i):
        at = pl.ds(pl.multiple_of(i * side, side), side)
        return far(gf_send.at[at, :], gf_recv.at[at, :], base_gf + i, x_peer)

    def first_back(i, source, at):
        there = pl.ds(pl.multiple_of(at + i * side, side), side)
        grad = mul_nt(gqkv[there, :], flat(wq[...]))
        scaled, unused = normed(source[pl.ds(pl.multiple_of(i * side, side), side), :].astype(F32))
        gvec[GAIN_1] += column_sum(grad * scaled)
        gvec[SHIFT_1] += column_sum(grad)
        return grad

    def away(i):
        grad = first_back(i, tok_far, (1 - s) * rows)
        gf_send[pl.ds(pl.multiple_of(i * side, side), side), :] = grad.astype(BF)
        send_gf(i).start()

    loop(rows // side, away)
    sum_q(pairs - 1).y_start()

    def stay(i):
        gtok[pl.ds(pl.multiple_of(i * side, side), side), :] = first_back(i, tok, s * rows)

    loop(rows // side, stay)

    base_v = number.take(zs + 2)
    for dz in range(1, zs):
        far(gvec, v_z.at[dz - 1], base_v + dz - 1, z_peers[dz - 1]).start()
    z_start(tiles - 1)
    sum_o.z_start()
    for dz in range(1, zs):
        far(gvec, v_z.at[dz - 1], base_v + dz - 1, z_peers[dz - 1]).wait_recv()
    for i in range(TABLE):
        total = gvec[i]
        for dz in range(1, zs):
            total = total + v_z[dz - 1, i]
        v_sum[0, i] = total
    vy = far(v_sum.at[0], v_y, base_v + zs - 1, y_peer)
    vy.start()
    for p in range(pairs):
        sum_q(p).z_start()
    vy.wait_recv()
    v_sum[1] = v_sum[0] + v_y[...]
    vc = far(v_sum.at[1], v_c, base_v + zs, c_peer)
    vc.start()
    vc.wait_recv()
    v_sum[2] = v_sum[1] + v_c[...]
    vx = far(v_sum.at[2], v_x, base_v + zs + 1, x_peer)
    vx.start()

    total = r2_d[z].astype(F32)
    for dz in range(1, zs):
        far(r2_d.at[0], r3_d.at[dz - 1], base_zd + dz - 1, z_peers[dz - 1]).wait_recv()
        total = total + r3_d[dz - 1].astype(F32)
    r5_d[0] = total.astype(BF)
    xd = far(r5_d.at[0], r5_d.at[1], base_xs, x_peer)
    xd.start()
    for t in range(tiles):
        for dz in range(1, zs):
            z_u(t, dz).wait_recv()

    def finish_u(t):
        total = r2_u[z, :, tile_lanes(t)].astype(F32)
        for dz in range(1, zs):
            total = total + r3_u[dz - 1, :, tile_lanes(t)].astype(F32)
        r5_u[0, :, tile_lanes(t)] = total.astype(BF)

    loop(tiles, finish_u)
    xu = far(r5_u.at[0], r5_u.at[1], base_xs + 1, x_peer)
    xu.start()
    r5_o[0] = sum_o.z_finish().astype(BF)
    xo = far(r5_o.at[0], r5_o.at[1], number.take(1), x_peer)
    xo.start()
    for p in range(pairs):
        r5_q[s, :, p * local : (p + 1) * local] = sum_q(p).z_finish().astype(BF)
    slot_q = number.take(1)
    xq = far(r5_q.at[s], r5_q.at[s], slot_q, x_peer)
    xq.start()

    for i in range(rows // side):
        send_gf(i).wait_recv()

    def last(i):
        at = pl.ds(pl.multiple_of(i * 128, 128), 128)
        scaled, inverse = normed(tok[at, :].astype(F32))
        grad = gtok[at, :] + gf_recv[at, :].astype(F32)
        gtok[at, :] = middle[at, :] + normed_back(grad, scaled, inverse, vec[GAIN_1])

    loop(rows // 128, last)

    vx.wait_recv()
    out_v[...] = v_sum[2] + v_x[...]
    xd.wait_recv()
    out_d[...] = r5_d[0].astype(F32) + r5_d[1].astype(F32)
    xu.wait_recv()

    def store_u(t):
        out_u[:, tile_lanes(t)] = r5_u[0, :, tile_lanes(t)].astype(F32) + r5_u[1, :, tile_lanes(t)].astype(F32)

    loop(tiles, store_u)
    xo.wait_recv()
    out_o[...] = r5_o[0].astype(F32) + r5_o[1].astype(F32)
    far(r5_q.at[1 - s], r5_q.at[1 - s], slot_q, x_peer).wait_recv()
    for half in range(2):
        for p in range(pairs):
            for part in range(3):
                at = part * width + half * local + p * 128
                out_q[:, at : at + 128] = r5_q[
                    half, :, p * local + part * 128 : p * local + part * 128 + 128
                ].astype(F32)

    for dz in range(1, zs):
        far(table, e_z.at[dz - 1], base_e + dz - 1, z_peers[dz - 1]).wait_send()
        far(gvec, v_z.at[dz - 1], base_v + dz - 1, z_peers[dz - 1]).wait_send()
        far(r2_d.at[0], r3_d.at[dz - 1], base_zd + dz - 1, z_peers[dz - 1]).wait_send()
    for copy in (y_table, c_table, send_tok, vy, vc, vx, xd, xu, xo, xq):
        copy.wait_send()
    for p in range(pairs):
        gather_q(p).sent()
        send_mixed(p).wait_send()
        sum_q(p).sent()
    sum_o.sent()
    for t in range(tiles):
        for yy in range(2):
            sib_d(t, yy).wait_send()
            sib_u(t, yy).wait_send()
        y_d(t).wait_send()
        y_u(t).wait_send()
        for dz in range(1, zs):
            z_u(t, dz).wait_send()
    for i in range(rows // side):
        send_gf(i).wait_send()


def fused_fits(tokens, lengths, own_q, own_d, shards, pair):
    rows, width = tokens.shape
    return (
        shards == 16
        and pair == 2
        and rows % 256 == 0
        and (width // pair) % 128 == 0
        and own_q.shape[0] % 16 == 0
        and own_d.shape[0] % 64 == 0
        and own_d.shape[0] * shards == 4 * width
    )


def fused(tokens, lengths, w_qkv, w_out, w_up, w_down, small, bias_up, cotangent):
    rows, width = tokens.shape
    shards = lax.axis_size("dp")
    zs = shards // 4
    d = lax.axis_index("dp")
    rq, rd = w_qkv.shape[0], w_down.shape[0]
    deep = 4 * rd * zs
    group = 2 * rows
    local = width // 2
    pairs = local // 128
    lane = jnp.arange(width)
    own = jnp.where(lane // rq == d, jnp.tile(jnp.stack(small), (1, shards)), 0)
    at = jnp.arange(zs)[:, None] * width + lane[None, :]
    up = jnp.where(at // rd == d, jnp.tile(bias_up, (width // rd,))[None, :], 0)
    table = jnp.concatenate([own, up, jnp.zeros((TABLE - 8 - zs, width), own.dtype)], axis=0)

    def vm(shape, kind=BF):
        return pltpu.VMEM(shape, kind)

    scratch = [
        vm((zs, 4 * rq, 3 * local)), vm((zs, 4 * rq, width)), vm((zs, 4 * rq, deep)),
        vm((zs, 4 * rd, width)), vm((zs, 4 * rq, 3 * local)),
        vm((rows, width)), vm((group, width)), vm((width, group)), vm((group, 3 * local)),
        vm((pairs, 128, group)), vm((pairs, 128, group)), vm((1, group), jnp.int32),
        vm((pairs, 2, 1, group), F32), vm((128, group), F32),
        vm((group, local)), vm((rows, width)), vm((width, rows)), vm((rows, width), F32),
        vm((rows, width)), vm((width, rows)), vm((rows, width)), vm((rows, width), F32),
        vm((rows, 4 * rd)), vm((4 * rd, rows)), vm((rows, 4 * rd)), vm((rows, width)),
        vm((group, local)), vm((rows, width)), vm((group, 128), F32), vm((group, 128), F32),
        vm((128, group), F32), vm((group, 3 * local)),
        vm((2, TABLE, width)), vm((zs - 1, TABLE, width)), vm((TABLE, width)), vm((TABLE, width)),
        vm((TABLE, 1, width), F32), vm((TABLE, 1, width), F32), vm((zs - 1, TABLE, 1, width), F32),
        vm((TABLE, 1, width), F32), vm((TABLE, 1, width), F32), vm((TABLE, 1, width), F32),
        vm((3, TABLE, 1, width), F32),
        vm((zs, 2 * rd, width)), vm((zs, rd, width)), vm((zs - 1, rd, width)), vm((2, rd, width)),
        vm((zs, 2 * rq, deep)), vm((zs, rq, deep)), vm((zs - 1, rq, deep)), vm((2, rq, deep)),
        vm((zs, 2 * rq, width)), vm((zs, rq, width)), vm((zs - 1, rq, width)), vm((2, rq, width)),
        vm((zs, 2 * rq, 3 * local)), vm((zs, rq, 3 * local)), vm((zs - 1, rq, 3 * local)),
        vm((2, rq, 3 * local)),
        vm((rows, width)), vm((rows, width)),
        pltpu.SemaphoreType.DMA((NEAR_COUNT,)),
        pltpu.SemaphoreType.DMA((FAR_COUNT,)),
        pltpu.SemaphoreType.DMA((FAR_COUNT,)),
    ]
    here = pl.BlockSpec(memory_space=pltpu.VMEM)
    away = pl.BlockSpec(memory_space=pl.ANY)
    return pl.pallas_call(
        fused_kernel,
        out_shape=(
            jax.ShapeDtypeStruct((rows, width), BF),
            jax.ShapeDtypeStruct((rows, width), F32),
            jax.ShapeDtypeStruct((rq, 3 * width), F32),
            jax.ShapeDtypeStruct((rq, width), F32),
            jax.ShapeDtypeStruct((rq, deep), F32),
            jax.ShapeDtypeStruct((rd, width), F32),
            jax.ShapeDtypeStruct((TABLE, 1, width), F32),
        ),
        in_specs=[pl.BlockSpec(memory_space=pltpu.SMEM), here, here, here, away, away, away, away],
        out_specs=[here] * 7,
        scratch_shapes=scratch,
        compiler_params=pltpu.CompilerParams(
            collective_id=0, has_side_effects=True, vmem_limit_bytes=67_043_328
        ),
        name="block",
    )(lengths, table, tokens, cotangent, w_qkv, w_out, w_up, w_down)


def per_device(
    tokens, lengths, w_qkv, w_out, w_up, w_down, bias_q, bias_v, bias_out, bias_up, bias_down,
    gain_one, shift_one, gain_two, shift_two, cotangent,
):
    if not fused_fits(
        tokens, lengths, w_qkv, w_down, lax.axis_size("dp"), lax.axis_size("seq")
    ):
        return per_device_plain(
            tokens, lengths, w_qkv, w_out, w_up, w_down, bias_q, bias_v, bias_out, bias_up,
            bias_down, gain_one, shift_one, gain_two, shift_two, cotangent,
        )
    small = [bias_q, bias_v, bias_out, bias_down, gain_one, shift_one, gain_two, shift_two]
    out, gtok, gq, go, gu, gd, table = fused(
        tokens, lengths, w_qkv, w_out, w_up, w_down, small, bias_up, cotangent
    )
    d = lax.axis_index("dp")
    width = tokens.shape[1]
    rq, rd = w_qkv.shape[0], w_down.shape[0]
    own = lax.dynamic_slice_in_dim(table[:8, 0], d * rq, rq, axis=1)
    up = lax.dynamic_slice_in_dim(
        table[8:].reshape((TABLE - 8) * width), d * rd, rd, axis=0
    )
    return (
        out, gtok, gq, go, gu, gd,
        own[0], own[1], own[2], up, own[3], own[4], own[5], own[6], own[7],
    )


def solution(mesh):
    return jax.shard_map(
        per_device,
        mesh=mesh,
        in_specs=(
            P(("dp", "seq"), None),
            P("dp", None),
            P("dp", None),
            P("dp", None),
            P("dp", None),
            P("dp", None),
            P("dp"),
            P("dp"),
            P("dp"),
            P("dp"),
            P("dp"),
            P("dp"),
            P("dp"),
            P("dp"),
            P("dp"),
            P(("dp", "seq"), None),
        ),
        out_specs=(
            P(("dp", "seq"), None),
            P(("dp", "seq"), None),
            P("dp", None),
            P("dp", None),
            P("dp", None),
            P("dp", None),
            P("dp"),
            P("dp"),
            P("dp"),
            P("dp"),
            P("dp"),
            P("dp"),
            P("dp"),
            P("dp"),
            P("dp"),
        ),
        check_vma=False,
    )
```

```python
import jax
import jax.numpy as jnp
from jax import lax
from jax.experimental import pallas as pl
from jax.experimental.pallas import tpu as pltpu
from jax.sharding import PartitionSpec as P

HEAD_DIM = 64


EPSILON = 1e-05
MASKED = -1e30
SLOPE = 0.7978845608028654
CUBIC = 0.044715


def as_sent(array):
    return jax.tree.map(lambda a: a.astype(jnp.bfloat16) if a.dtype == jnp.float32 else a, array)


def dense(left, right):
    return jnp.dot(left, right, preferred_element_type=jnp.float32)


def dense_left(left, right):
    return lax.dot_general(
        left, right, (((0,), (0,)), ((), ())), preferred_element_type=jnp.float32
    )


def dense_right(left, right):
    return lax.dot_general(
        left, right, (((1,), (1,)), ((), ())), preferred_element_type=jnp.float32
    )


def norm_parts(value):
    mean = jnp.mean(value, axis=-1, keepdims=True)
    centred = value - mean
    inverse = lax.rsqrt(jnp.mean(centred * centred, axis=-1, keepdims=True) + EPSILON)
    return (centred * inverse, inverse)


def norm_back(grad, scaled, inverse, gain):
    shaped = grad * gain
    inner = jnp.mean(shaped * scaled, axis=-1, keepdims=True)
    return inverse * (shaped - jnp.mean(shaped, axis=-1, keepdims=True) - scaled * inner)


def gelu_value(value):
    return 0.5 * value * (1.0 + jnp.tanh(SLOPE * (value + CUBIC * value * value * value)))


def gelu_slope(value):
    bent = jnp.tanh(SLOPE * (value + CUBIC * value * value * value))
    return 0.5 * (1.0 + bent) + 0.5 * value * (1.0 - bent * bent) * SLOPE * (
        1.0 + 3.0 * CUBIC * value * value
    )


def per_device_plain(
    tokens,
    lengths,
    w_qkv,
    w_out,
    w_up,
    w_down,
    bias_q,
    bias_v,
    bias_out,
    bias_up,
    bias_down,
    gain_one,
    shift_one,
    gain_two,
    shift_two,
    cotangent,
):
    width = tokens.shape[1]
    rows = tokens.shape[0]
    pair = lax.axis_size("seq")
    rank = lax.axis_index("seq")
    group = rows * pair
    local = width // pair
    heads = local // HEAD_DIM
    scale = HEAD_DIM ** (-0.5)
    block = 512
    blocks = group // block
    whole = (
        lax.all_gather(w_qkv, "dp", axis=0, tiled=True),
        lax.all_gather(w_out, "dp", axis=0, tiled=True),
        lax.all_gather(w_up, "dp", axis=0, tiled=True),
        lax.all_gather(w_down, "dp", axis=0, tiled=True),
        lax.all_gather(bias_q, "dp", axis=0, tiled=True),
        lax.all_gather(bias_v, "dp", axis=0, tiled=True),
        lax.all_gather(bias_out, "dp", axis=0, tiled=True),
        lax.all_gather(bias_up, "dp", axis=0, tiled=True),
        lax.all_gather(bias_down, "dp", axis=0, tiled=True),
        lax.all_gather(gain_one, "dp", axis=0, tiled=True),
        lax.all_gather(shift_one, "dp", axis=0, tiled=True),
        lax.all_gather(gain_two, "dp", axis=0, tiled=True),
        lax.all_gather(shift_two, "dp", axis=0, tiled=True),
    )
    weight_qkv, weight_out, weight_up, weight_down = whole[0:4]
    add_q, add_v, add_out, add_up, add_down, scale_one, move_one, scale_two, move_two = [
        piece.astype(jnp.float32) for piece in whole[4:]
    ]
    slots = lengths.shape[1]
    position = jnp.arange(group, dtype=jnp.int32)
    ends = jnp.cumsum(lengths[0])
    segment = jnp.sum((position[:, None] >= ends[None, :]).astype(jnp.int32), axis=1)
    own_segment = lax.dynamic_slice_in_dim(segment, rank * rows, rows)
    valid = (own_segment < slots - 1)[:, None]
    inputs = tokens.astype(jnp.float32)
    scaled_one, inverse_one = norm_parts(inputs)
    first = (scaled_one * scale_one + move_one).astype(jnp.bfloat16)
    bias_qkv = jnp.concatenate([add_q, jnp.zeros_like(add_q), add_v])
    qkv = (dense(first, weight_qkv) + bias_qkv).astype(jnp.bfloat16)
    head_side = lax.all_to_all(
        qkv.reshape(rows, 3, pair, local), "seq", split_axis=2, concat_axis=0, tiled=True
    )
    query = head_side[:, 0, 0].reshape(group, heads, HEAD_DIM)
    keys = head_side[:, 1, 0].reshape(group, heads, HEAD_DIM)
    values = head_side[:, 2, 0].reshape(group, heads, HEAD_DIM)

    def block_scores(index):
        start = index * block
        query_rows = lax.dynamic_slice_in_dim(query, start, block)
        raw = (
            jnp.einsum("qhd,khd->hqk", query_rows, keys, preferred_element_type=jnp.float32) * scale
        )
        row_segment = lax.dynamic_slice_in_dim(segment, start, block)
        row_position = lax.dynamic_slice_in_dim(position, start, block)
        allowed = (row_segment[:, None] == segment[None, :]) & (
            position[None, :] <= row_position[:, None]
        )
        return (jnp.where(allowed[None], raw, MASKED), query_rows)

    def attend(index):
        scores, unused = block_scores(index)
        top = jnp.max(scores, axis=-1, keepdims=True)
        weights = jnp.exp(scores - top)
        total = jnp.sum(weights, axis=-1, keepdims=True)
        probs = (weights / total).astype(jnp.bfloat16)
        mixed_rows = jnp.einsum("hqk,khd->qhd", probs, values, preferred_element_type=jnp.float32)
        return (
            mixed_rows.reshape(block, local).astype(jnp.bfloat16),
            (top + jnp.log(total))[:, :, 0],
        )

    mixed_blocks, log_totals = lax.map(attend, jnp.arange(blocks))
    mixed_head = mixed_blocks.reshape(group, 1, local)
    mixed = lax.all_to_all(mixed_head, "seq", split_axis=0, concat_axis=1, tiled=True).reshape(
        rows, width
    )
    middle = inputs + dense(mixed, weight_out) + add_out
    scaled_two, inverse_two = norm_parts(middle)
    second = (scaled_two * scale_two + move_two).astype(jnp.bfloat16)
    pre = dense(second, weight_up) + add_up
    hidden = gelu_value(pre).astype(jnp.bfloat16)
    result = middle + dense(hidden, weight_down) + add_down
    block_out = jnp.where(valid, result, 0.0).astype(jnp.bfloat16)
    grad_out = jnp.where(valid, cotangent, jnp.zeros_like(cotangent))
    grad_weight_down = dense_left(hidden, grad_out)
    grad_add_down = jnp.sum(grad_out.astype(jnp.float32), axis=0)
    grad_pre = (dense_right(grad_out, weight_down) * gelu_slope(pre)).astype(jnp.bfloat16)
    grad_weight_up = dense_left(second, grad_pre)
    grad_add_up = jnp.sum(grad_pre.astype(jnp.float32), axis=0)
    grad_second = dense_right(grad_pre, weight_up)
    grad_scale_two = jnp.sum(grad_second * scaled_two, axis=0)
    grad_move_two = jnp.sum(grad_second, axis=0)
    grad_middle = grad_out.astype(jnp.float32) + norm_back(
        grad_second, scaled_two, inverse_two, scale_two
    )
    grad_attn = grad_middle.astype(jnp.bfloat16)
    grad_weight_out = dense_left(mixed, grad_attn)
    grad_add_out = jnp.sum(grad_attn.astype(jnp.float32), axis=0)
    grad_mixed = dense_right(grad_attn, weight_out).astype(jnp.bfloat16)
    branch_grads = (
        grad_weight_out,
        grad_weight_up,
        grad_weight_down,
        grad_add_out,
        grad_add_up,
        grad_add_down,
        grad_scale_two,
        grad_move_two,
    )
    grad_head = lax.all_to_all(
        grad_mixed.reshape(rows, pair, local), "seq", split_axis=1, concat_axis=0, tiled=True
    )
    grad_head = grad_head.reshape(group, heads, HEAD_DIM)

    def attend_back(carry, index):
        grad_keys, grad_values = carry
        scores, query_rows = block_scores(index)
        probs = jnp.exp(scores - log_totals[index][:, :, None])
        grad_rows = lax.dynamic_slice_in_dim(grad_head, index * block, block)
        grad_probs = jnp.einsum(
            "qhd,khd->hqk", grad_rows, values, preferred_element_type=jnp.float32
        )
        centre = jnp.sum(probs * grad_probs, axis=-1, keepdims=True)
        grad_scores = (probs * (grad_probs - centre)).astype(jnp.bfloat16)
        grad_values = grad_values + jnp.einsum(
            "hqk,qhd->khd",
            probs.astype(jnp.bfloat16),
            grad_rows,
            preferred_element_type=jnp.float32,
        )
        grad_keys = (
            grad_keys
            + jnp.einsum(
                "hqk,qhd->khd", grad_scores, query_rows, preferred_element_type=jnp.float32
            )
            * scale
        )
        grad_query = (
            jnp.einsum("hqk,khd->qhd", grad_scores, keys, preferred_element_type=jnp.float32)
            * scale
        )
        return ((grad_keys, grad_values), grad_query)

    empty = jnp.zeros((group, heads, HEAD_DIM), jnp.float32)
    (grad_keys, grad_values), grad_queries = lax.scan(
        attend_back, (empty, empty), jnp.arange(blocks)
    )
    grad_side = jnp.stack(
        [
            grad_queries.reshape(group, local),
            grad_keys.reshape(group, local),
            grad_values.reshape(group, local),
        ],
        axis=1,
    ).astype(jnp.bfloat16)
    grad_qkv = lax.all_to_all(
        grad_side.reshape(group, 3, 1, local), "seq", split_axis=0, concat_axis=2, tiled=True
    )
    grad_qkv = grad_qkv.reshape(rows, 3 * width)
    grad_weight_qkv = dense_left(first, grad_qkv)
    column_sums = jnp.sum(grad_qkv.astype(jnp.float32), axis=0)
    grad_add_q = column_sums[:width]
    grad_add_v = column_sums[2 * width :]
    grad_first = dense_right(grad_qkv, weight_qkv)
    grad_scale_one = jnp.sum(grad_first * scaled_one, axis=0)
    grad_move_one = jnp.sum(grad_first, axis=0)
    grad_tokens = grad_middle + norm_back(grad_first, scaled_one, inverse_one, scale_one)
    stem_grads = (grad_weight_qkv, grad_add_q, grad_add_v, grad_scale_one, grad_move_one)
    halves = lax.psum_scatter(
        stem_grads + branch_grads, ("dp", "seq"), scatter_dimension=0, tiled=True
    )
    shares = jax.tree.map(
        lambda part, own: part.astype(own.dtype),
        lax.all_gather(as_sent(halves), "seq", axis=0, tiled=True),
        halves,
    )
    stem_shares = shares[0:5]
    branch_shares = shares[5:13]
    return (
        block_out,
        grad_tokens,
        stem_shares[0],
        branch_shares[0],
        branch_shares[1],
        branch_shares[2],
        stem_shares[1],
        stem_shares[2],
        branch_shares[3],
        branch_shares[4],
        branch_shares[5],
        stem_shares[3],
        stem_shares[4],
        branch_shares[6],
        branch_shares[7],
    )


FAR = pl.DeviceIdType.MESH
NT = (((1,), (1,)), ((), ()))
BF = jnp.bfloat16
F32 = jnp.float32


def mul(left, right):
    return jnp.dot(left, right, preferred_element_type=F32)


def mul_nt(left, right):
    return lax.dot_general(left, right, NT, preferred_element_type=F32)


def flat(blocks):
    return blocks.reshape(blocks.shape[0] * blocks.shape[1], blocks.shape[2])


def normed(value):
    width = value.shape[1]
    mean = jnp.sum(value, axis=1, keepdims=True) * (1.0 / width)
    centred = value - mean
    spread = jnp.sum(centred * centred, axis=1, keepdims=True) * (1.0 / width)
    inverse = lax.rsqrt(spread + EPSILON)
    return (centred * inverse, inverse)


def normed_back(grad, scaled, inverse, gain):
    width = grad.shape[1]
    shaped = grad * gain
    inner = jnp.sum(shaped * scaled, axis=1, keepdims=True) * (1.0 / width)
    outer = jnp.sum(shaped, axis=1, keepdims=True) * (1.0 / width)
    return inverse * (shaped - outer - scaled * inner)


def column_sum(value):
    return jnp.sum(value, axis=0, keepdims=True)


class Numbers:
    def __init__(self):
        self.used = 0

    def take(self, count):
        start = self.used
        self.used = start + count
        return start


BIAS_Q, BIAS_V, BIAS_OUT, BIAS_DOWN, GAIN_1, SHIFT_1, GAIN_2, SHIFT_2, BIAS_UP = range(9)
TABLE = 16
FAR_COUNT = 240
NEAR_COUNT = 32


def fused_kernel(
    lengths, table, tok_own, cot, own_q, own_o, own_u, own_d,
    out, gtok, out_q, out_o, out_u, out_d, out_v,
    wq, wo, wu, wd, gwq, gwd,
    tok, tok_far, first, first_t, qkv, k_t, v_t, lower, lse, o_t,
    mixed_near, mixed, mixed_t, middle, second, second_t, gout,
    hidden, hidden_t, slope, gmix_head, dk, dv,
    e_own, e_z, e_y, e_c, vec, gvec, v_z, v_y, v_c, v_x, v_sum,
    r1_d, rx_d, ry_d, rz_d, r5_d, r1_u, r2_u, r3_u, r5_u,
    r1_o, r2_o, r3_o, r5_o, r1_q, r2_q, r3_q, r5_q,
    near_sem, send_sem, recv_sem,
):
    d = lax.axis_index("dp")
    s = lax.axis_index("seq")
    z = lax.div(d, 4)
    y = lax.rem(lax.div(d, 2), 2)
    c = lax.rem(d, 2)
    zs = wq.shape[0]
    rows, width = tok_own.shape
    group = 2 * rows
    local = width // 2
    pairs = local // 128
    rq = width // (4 * zs)
    rd = own_d.shape[0]
    tile = 4 * rd
    tiles = zs
    z_peers = [(lax.rem(z + dz, zs) * 4 + y * 2 + c, s) for dz in range(1, zs)]
    y_peer = (z * 4 + (1 - y) * 2 + c, s)
    c_peer = (z * 4 + y * 2 + (1 - c), s)
    x_peer = (d, 1 - s)
    number = Numbers()
    local_number = Numbers()

    def far(src, dst, slot, device):
        return pltpu.make_async_remote_copy(
            src_ref=src, dst_ref=dst, send_sem=send_sem.at[slot], recv_sem=recv_sem.at[slot],
            device_id=device, device_id_type=FAR,
        )

    far_w, far_g = far, far

    def z_at(dz):
        return lax.rem(z + zs - dz, zs)

    def loop(count, body):
        lax.fori_loop(0, count, lambda i, carry: (body(i), carry)[1], 0)

    def block_rows(r, yy, cc):
        return pl.ds(pl.multiple_of((yy * 2 + cc) * r, r), r)

    barrier = pltpu.get_barrier_semaphore()
    everyone = z_peers + [y_peer, c_peer, x_peer]
    for peer in everyone:
        pl.semaphore_signal(barrier, inc=1, device_id=peer, device_id_type=FAR)
    pl.semaphore_wait(barrier, len(everyone))

    class Gather:
        def __init__(self, ref, r, columns, base, own=None, columns_at=None):
            self.ref, self.r, self.columns, self.base, self.own = ref, r, columns, base, own
            self.columns_at = columns_at

        def part(self, zz, yy, cc):
            return self.ref.at[zz, block_rows(self.r, yy, cc), self.columns]

        def layer(self, yy, cc, columns=None):
            columns = self.columns if columns is None else columns
            return self.ref.at[:, block_rows(self.r, yy, cc), columns]

        def z_copy(self, dz):
            columns = self.columns if self.columns_at is None else self.columns_at(dz)
            there = self.ref.at[z, block_rows(self.r, y, c), columns]
            here = there if self.own is None else self.own.at[:, columns]
            return far_w(here, there, self.base + dz - 1, z_peers[dz - 1])

        def z_start(self):
            for dz in range(1, zs):
                self.z_copy(dz).start()

        def z_wait(self):
            for dz in range(1, zs):
                block = self.part(z_at(dz), y, c)
                far_w(block, block, self.base + dz - 1, z_peers[dz - 1]).wait_recv()

        def y_copy(self, yy):
            return far_w(self.layer(yy, c), self.layer(yy, c), self.base + zs - 1, y_peer)

        def c_copy(self, yy, cc, other):
            return far_w(self.layer(yy, cc), self.layer(yy, cc), self.base + zs + other, c_peer)

        def relay(self, *following):
            self.z_wait()
            for other in following:
                other.z_start()
            self.y_copy(y).start()
            self.c_copy(y, c, 0).start()

        def relay_y(self):
            self.y_copy(1 - y).wait_recv()
            self.c_copy(1 - y, c, 1).start()

        def finish(self):
            self.c_copy(y, 1 - c, 0).wait_recv()
            self.c_copy(1 - y, 1 - c, 1).wait_recv()

        def sent(self):
            for dz in range(1, zs):
                self.z_copy(dz).wait_send()
            self.y_copy(y).wait_send()
            self.c_copy(y, c, 0).wait_send()
            self.c_copy(1 - y, c, 1).wait_send()

    class GatherHalf(Gather):
        def __init__(self, ref, r, columns, others, base, own):
            super().__init__(ref, r, columns, base, own)
            self.others = others

        def x_copy(self, yy, columns, other):
            block = self.layer(yy, c, columns)
            return far_w(block, block, self.base + zs + 2 + other, x_peer)

        def c_other(self, yy, cc, other):
            block = self.layer(yy, cc, self.others)
            return far_w(block, block, self.base + zs + 4 + other, c_peer)

        def push_x(self):
            self.x_copy(y, self.columns, 0).start()

        def relay_y(self):
            super().relay_y()
            self.x_copy(1 - y, self.columns, 1).start()

        def relay_x(self):
            self.x_copy(y, self.others, 0).wait_recv()
            self.c_other(y, c, 0).start()
            self.x_copy(1 - y, self.others, 1).wait_recv()
            self.c_other(1 - y, c, 1).start()

        def finish(self):
            super().finish()
            self.c_other(y, 1 - c, 0).wait_recv()
            self.c_other(1 - y, 1 - c, 1).wait_recv()

        def sent(self):
            super().sent()
            self.x_copy(y, self.columns, 0).wait_send()
            self.x_copy(1 - y, self.columns, 1).wait_send()
            self.c_other(y, c, 0).wait_send()
            self.c_other(1 - y, c, 1).wait_send()

    steps = zs + 2
    base_q = number.take(pairs * steps)

    def gather_q(p):
        return Gather(wq, rq, pl.ds(pl.multiple_of(p * local, 128), local), base_q + p * steps)

    gather_o = Gather(wo, rq, pl.ds(0, width), number.take(steps), own_o)
    base_gu = number.take(tiles * steps)

    def tile_lanes(t):
        return pl.ds(pl.multiple_of(t * tile, 128), tile)

    def turn(i, zz):
        return lax.rem(zz + i + 1, zs)

    def gather_u(i):
        return Gather(
            wu, rq, tile_lanes(turn(i, z)), base_gu + i * steps, own_u,
            lambda dz: tile_lanes(turn(i, lax.rem(z + dz, zs))),
        )

    cuts = local // 128 - 1
    base_gd = number.take(cuts * (zs + 6))
    base_gw = number.take(2 * steps)

    def gather_d(i):
        mine = pl.ds(pl.multiple_of(s * local + i * 128, 128), 128)
        others = pl.ds(pl.multiple_of((1 - s) * local + i * 128, 128), 128)
        return GatherHalf(wd, rd, mine, others, base_gd + i * (zs + 6), own_d)

    def gather_w(i):
        return Gather(wd, rd, pl.ds(i * local + cuts * 128, 128), base_gw + i * steps, own_d)

    near_q = []
    for p in range(pairs):
        for part in range(3):
            start = pl.multiple_of(part * width + s * local + p * 128, 128)
            near_q.append(
                pltpu.make_async_copy(
                    own_q.at[:, pl.ds(start, 128)],
                    wq.at[z, block_rows(rq, y, c), pl.ds(p * local + part * 128, 128)],
                    near_sem.at[local_number.take(1)],
                )
            )
    near_rest = []
    for own, whole, r in ((own_o, wo, rq), (own_u, wu, rq), (own_d, wd, rd)):
        near_rest.append(
            pltpu.make_async_copy(
                own, whole.at[z, block_rows(r, y, c), :], near_sem.at[local_number.take(1)]
            )
        )
    near_cot = pltpu.make_async_copy(cot, gout, near_sem.at[local_number.take(1)])
    near_tok = pltpu.make_async_copy(tok_own, tok, near_sem.at[local_number.take(1)])
    for copy in near_q + [near_tok] + near_rest + [near_cot]:
        copy.start()

    base_e = number.take(zs + 1)
    for dz in range(1, zs):
        far(table, e_z.at[dz - 1], base_e + dz - 1, z_peers[dz - 1]).start()
    send_tok = far(tok_own, tok_far, number.take(1), x_peer)
    send_tok.start()
    for copy in near_q:
        copy.wait()
    for p in range(pairs):
        gather_q(p).z_start()

    for dz in range(1, zs):
        far(table, e_z.at[dz - 1], base_e + dz - 1, z_peers[dz - 1]).wait_recv()
    total = table[...].astype(F32)
    for dz in range(1, zs):
        total = total + e_z[dz - 1].astype(F32)
    e_own[0] = total.astype(BF)
    y_table = far(e_own.at[0], e_y, base_e + zs - 1, y_peer)
    y_table.start()
    gather_q(0).relay(gather_o)

    ends = []
    end = jnp.int32(0)
    for j in range(lengths.shape[1]):
        end = end + lengths[0, j]
        ends.append(end)
    position = lax.broadcasted_iota(jnp.int32, (1, group), 1)
    start = jnp.zeros((1, group), jnp.int32)
    for end in ends[:-1]:
        start = jnp.where(position >= end, end, start)
    lower[...] = start
    last_valid = ends[-2]

    y_table.wait_recv()
    total = total + e_y[...].astype(F32)
    e_own[1] = total.astype(BF)
    c_table = far(e_own.at[1], e_c, base_e + zs, c_peer)
    c_table.start()
    gather_q(1).relay(gather_u(0))
    c_table.wait_recv()
    total = total + e_c[...].astype(F32)
    for i in range(TABLE):
        vec[i] = total[i : i + 1, :]

    def first_norm(source, at):
        def body(i):
            x = source[pl.ds(pl.multiple_of(i * 128, 128), 128), :].astype(F32)
            scaled, unused = normed(x)
            value = (scaled * vec[GAIN_1] + vec[SHIFT_1]).astype(BF)
            there = pl.ds(pl.multiple_of(at + i * 128, 128), 128)
            first[there, :] = value
            first_t[:, there] = value.T

        loop(rows // 128, body)

    near_tok.wait()
    first_norm(tok, s * rows)

    base_mixed = number.take(pairs)
    near_mixed = local_number.take(pairs)

    def lanes(p, part):
        return pl.ds(pl.multiple_of(p * local + part * 128, 128), 128)

    def send_mixed(p):
        there = pl.ds(pl.multiple_of(s * local + p * 128, 128), 128)
        here = pl.ds(pl.multiple_of(p * 128, 128), 128)
        away = pl.ds(pl.multiple_of((1 - s) * rows, 128), rows)
        return far(mixed_near.at[away, here], mixed.at[:, there], base_mixed + p, x_peer)

    def keep_mixed(p):
        there = pl.ds(pl.multiple_of(s * local + p * 128, 128), 128)
        here = pl.ds(pl.multiple_of(p * 128, 128), 128)
        stay = pl.ds(pl.multiple_of(s * rows, 128), rows)
        return pltpu.make_async_copy(
            mixed_near.at[stay, here], mixed.at[:, there], near_sem.at[near_mixed + p]
        )

    side = 256
    blocks = group // side
    key_at = lax.broadcasted_iota(jnp.int32, (side, side), 0)
    query_at = lax.broadcasted_iota(jnp.int32, (side, side), 1)
    lane = lax.broadcasted_iota(jnp.int32, (side, 128), 1)

    def head_lanes(value, h):
        inside = (lane >= h * HEAD_DIM) & (lane < h * HEAD_DIM + HEAD_DIM)
        return jnp.where(inside, value, 0.0).astype(BF)

    def scores(p, keys_block, query, qi, j):
        raw = mul_nt(keys_block, query)
        ok = key_at + j * side >= lower[:, qi * side : (qi + 1) * side]
        if j == qi:
            ok = ok & (key_at <= query_at)
        return jnp.where(ok, raw, MASKED)

    scale = HEAD_DIM ** (-0.5)

    def pass_on(k):
        @pl.when(k == 0)
        def _():
            gather_u(0).relay(gather_d(0))
            gather_o.relay_y()

        @pl.when(k == 3)
        def _():
            gather_u(1).relay(gather_d(1))
            gather_u(0).relay_y()

    def attend(p):
        def head(h):
            half = pl.ds(pl.multiple_of(h * HEAD_DIM, HEAD_DIM), HEAD_DIM)
            for qi in range(blocks):
                query = head_lanes(
                    qkv[qi * side : (qi + 1) * side, lanes(p, 0)].astype(F32) * scale, h
                )
                raw = []
                top = None
                for j in range(qi + 1):
                    block = scores(p, qkv[j * side : (j + 1) * side, lanes(p, 1)], query, qi, j)
                    raw.append(block)
                    high = jnp.max(block, axis=0, keepdims=True)
                    top = high if top is None else jnp.maximum(top, high)
                amount = jnp.zeros((1, side), F32)
                gathered = jnp.zeros((HEAD_DIM, side), F32)
                for j in range(qi + 1):
                    weight = jnp.exp(raw[j] - top)
                    amount = amount + column_sum(weight)
                    gathered = gathered + mul(
                        v_t[p, half, j * side : (j + 1) * side], weight.astype(BF)
                    )
                o_t[half, qi * side : (qi + 1) * side] = gathered / amount
                lse[p, h, :, qi * side : (qi + 1) * side] = top + jnp.log(amount)
            pass_on(p * 2 + h)

        loop(2, head)
        here = pl.ds(pl.multiple_of(p * 128, 128), 128)
        for qi in range(blocks):
            at = slice(qi * side, (qi + 1) * side)
            mixed_near[at, here] = o_t[:, at].T.astype(BF)

    def project(p, at_row):
        zero = jnp.zeros((1, 128), F32)
        there = pl.ds(pl.multiple_of(s * local + p * 128, 128), 128)
        bias = jnp.concatenate([vec[BIAS_Q, :, there], zero, vec[BIAS_V, :, there]], axis=1)
        weight = flat(wq[:, :, pl.ds(pl.multiple_of(p * local, 128), local)])

        def body(i):
            at = pl.ds(pl.multiple_of(at_row + i * side, side), side)
            value = (mul(first[at, :], weight) + bias).astype(BF)
            qkv[at, pl.ds(pl.multiple_of(p * local, 128), local)] = value
            k_t[p, :, at] = value[:, 128:256].T
            v_t[p, :, at] = value[:, 256:384].T

        loop(rows // side, body)

    gather_q(0).relay_y()
    gather_q(2).relay(gather_u(1))
    gather_q(0).finish()
    project(0, s * rows)
    gather_q(1).relay_y()
    for copy in near_rest:
        copy.wait()
    gather_o.relay(gather_u(2))
    gather_q(2).relay_y()
    send_tok.wait_recv()
    first_norm(tok_far, (1 - s) * rows)

    def pair_forward(p):
        @pl.when(p > 0)
        def _():
            gather_q(p).finish()
            project(p, s * rows)

        project(p, (1 - s) * rows)
        attend(p)
        send_mixed(p).start()
        keep_mixed(p).start()

    loop(pairs, pair_forward)
    gather_u(2).relay(gather_u(3))
    gather_u(1).relay_y()

    gather_o.finish()
    near_cot.wait()
    for p in range(pairs):
        keep_mixed(p).wait()
    for p in range(pairs):
        far(
            mixed_near.at[pl.ds(0, rows), pl.ds(0, 128)],
            mixed.at[:, pl.ds(pl.multiple_of((1 - s) * local + p * 128, 128), 128)],
            base_mixed + p, x_peer,
        ).wait_recv()

    def project_out(i):
        at = pl.ds(pl.multiple_of(i * 128, 128), 128)
        near = mixed[at, :]
        mixed_t[:, at] = near.T
        value = tok[at, :].astype(F32) + mul(near, flat(wo[...])) + vec[BIAS_OUT]
        middle[at, :] = value
        scaled, unused = normed(value)
        rounded = (scaled * vec[GAIN_2] + vec[SHIFT_2]).astype(BF)
        second[at, :] = rounded
        second_t[:, at] = rounded.T
        gtok[at, :] = jnp.zeros((128, width), F32)
        spot = s * rows + i * 128 + lax.broadcasted_iota(jnp.int32, (128, width), 0)
        gout[at, :] = jnp.where(spot < last_valid, gout[at, :].astype(F32), 0.0).astype(BF)

    loop(rows // 128, project_out)
    gather_d(0).relay(gather_w(0))
    gather_d(0).push_x()


    base_sib = number.take(tiles * 4)
    base_dx = number.take(tiles * 2)
    base_uy = number.take(tiles)
    base_zd = number.take(zs - 1)
    base_zu = number.take(tiles * (zs - 1))
    base_xs = number.take(2)
    mine = pl.ds(pl.multiple_of(s * local, 128), local)
    others = pl.ds(pl.multiple_of((1 - s) * local, 128), local)

    def rows_y(r, yy):
        return pl.ds(pl.multiple_of(yy * r, r), r)

    def sib_d(t, yy):
        return far_g(
            gwd.at[t, block_rows(rd, yy, 1 - c), :], r1_d.at[t, rows_y(rd, yy), :],
            base_sib + t * 4 + yy, c_peer,
        )

    def sib_start_d(t):
        for yy in range(2):
            sib_d(t, yy).start()

    def x_d(t):
        return far_g(r1_d.at[t, :, others], rx_d.at[t], base_dx + t * 2, x_peer)

    def x_start_d(t):
        for yy in range(2):
            sib_d(t, yy).wait_recv()
            at = rows_y(rd, yy)
            r1_d[t, at, :] = (
                r1_d[t, at, :].astype(F32) + gwd[t, block_rows(rd, yy, c), :].astype(F32)
            ).astype(BF)
        x_d(t).start()

    def y_d(t):
        return far_g(rx_d.at[t, rows_y(rd, 1 - y), :], ry_d.at[t], base_dx + t * 2 + 1, y_peer)

    def y_start_d(t):
        x_d(t).wait_recv()
        rx_d[t] = (rx_d[t].astype(F32) + r1_d[t, :, mine].astype(F32)).astype(BF)
        y_d(t).start()

    def z_d(t, dz):
        return far_g(ry_d.at[t], rz_d.at[dz - 1], base_zd + dz - 1, (t * 4 + y * 2 + c, s))

    def z_start_d(t):
        y_d(t).wait_recv()
        ry_d[t] = (ry_d[t].astype(F32) + rx_d[t, rows_y(rd, y), :].astype(F32)).astype(BF)
        dz = lax.rem(t + zs - z, zs)

        @pl.when(dz > 0)
        def _():
            z_d(t, dz).start()

    def sib_u(t, yy):
        return far_g(
            wu.at[:, block_rows(rq, yy, 1 - c), tile_lanes(t)],
            r1_u.at[:, rows_y(rq, yy), tile_lanes(t)],
            base_sib + t * 4 + 2 + yy, c_peer,
        )

    def sib_start_u(t):
        for yy in (1 - y, y):
            sib_u(t, yy).start()

    def y_u(t):
        return far_g(
            r1_u.at[:, rows_y(rq, 1 - y), tile_lanes(t)], r2_u.at[:, :, tile_lanes(t)],
            base_uy + t, y_peer,
        )

    def y_start_u(t):
        yy = 1 - y
        sib_u(t, yy).wait_recv()
        at = rows_y(rq, yy)
        for zz in range(zs):
            r1_u[zz, at, tile_lanes(t)] = (
                r1_u[zz, at, tile_lanes(t)].astype(F32)
                + wu[zz, block_rows(rq, yy, c), tile_lanes(t)].astype(F32)
            ).astype(BF)
        y_u(t).start()

    def z_u(t, dz):
        return far_g(
            r2_u.at[lax.rem(z + dz, zs), :, tile_lanes(t)], r3_u.at[dz - 1, :, tile_lanes(t)],
            base_zu + t * (zs - 1) + dz - 1, z_peers[dz - 1],
        )

    def z_start_u(t):
        sib_u(t, y).wait_recv()
        y_u(t).wait_recv()
        at = rows_y(rq, y)
        for zz in range(zs):
            r2_u[zz, :, tile_lanes(t)] = (
                r2_u[zz, :, tile_lanes(t)].astype(F32)
                + r1_u[zz, at, tile_lanes(t)].astype(F32)
                + wu[zz, block_rows(rq, y, c), tile_lanes(t)].astype(F32)
            ).astype(BF)
        for step in range(1, zs):
            z_u(t, step).start()

    sub = 256

    def pass_up(k):
        @pl.when(k == 1)
        def _():
            gather_u(2).relay_y()

        @pl.when(k == 2)
        def _():
            gather_d(1).relay(gather_w(1))
            gather_d(1).push_x()

        @pl.when(k == 3)
        def _():
            gather_d(0).relay_y()

        @pl.when(k == 4)
        def _():
            x_start_d(turn(0, z))

        @pl.when(k == 5)
        def _():
            gather_u(3).relay()

        @pl.when(k == 6)
        def _():
            gather_d(1).relay_y()
            gather_d(0).relay_x()

        @pl.when(k == 7)
        def _():
            gather_w(0).relay()

        @pl.when(k == 8)
        def _():
            gather_u(3).relay_y()

        @pl.when(k == 9)
        def _():
            gather_w(1).relay()
            gather_d(1).relay_x()

        @pl.when(k == 10)
        def _():
            gather_w(0).relay_y()
            x_start_d(turn(1, z))

    def feed(i):
        t = turn(i, z)
        gather_u(i).finish()

        def part(u):
            at = pl.ds(pl.multiple_of(t * tile + u * sub, 128), sub)
            near = pl.ds(pl.multiple_of(u * sub, sub), sub)
            pre = mul(second[...], flat(wu[:, :, at])) + vec[BIAS_UP + t, :, near]
            bent = jnp.tanh(SLOPE * (pre + CUBIC * pre * pre * pre))
            value = (0.5 * pre * (1.0 + bent)).astype(BF)
            bend = 0.5 * (1.0 + bent) + 0.5 * pre * (1.0 - bent * bent) * SLOPE * (
                1.0 + 3.0 * CUBIC * pre * pre
            )
            hidden[:, at] = value
            hidden_t[near, :] = value.T
            slope[:, at] = bend.astype(BF)
            pass_up(i * (tile // sub) + u)

        loop(tile // sub, part)

        def weigh(m):
            at = pl.ds(pl.multiple_of(m * rd, rd), rd)
            gwd[t, at, :] = mul(hidden_t[at, :], gout[...]).astype(BF)

        loop(4, weigh)
        sib_start_d(t)

    loop(tiles, feed)
    y_start_d(turn(0, z))
    x_start_d(turn(2, z))
    gather_w(1).relay_y()
    for i in range(cuts):
        gather_d(i).finish()
    for i in range(2):
        gather_w(i).finish()

    def slopes_back(i):
        at = pl.ds(pl.multiple_of(i * sub, sub), sub)
        t = lax.div(i, tile // sub)
        near = pl.ds(pl.multiple_of((i - t * (tile // sub)) * sub, sub), sub)
        grad = (mul_nt(gout[...], wd[t, near, :]) * slope[:, at].astype(F32)).astype(BF)
        slope[:, at] = grad
        gvec[BIAS_UP + t, :, near] = column_sum(grad.astype(F32))

    loop(tiles * (tile // sub), slopes_back)
    y_start_d(turn(1, z))
    x_start_d(z)
    z_start_d(turn(0, z))

    def grow(t):
        def add(i):
            at = pl.ds(pl.multiple_of(i * side, side), side)
            gtok[at, :] += mul_nt(slope[at, tile_lanes(t)], flat(wu[:, :, tile_lanes(t)]))

        loop(rows // side, add)

    loop(tiles, grow)

    for row in (BIAS_Q, BIAS_V, BIAS_OUT, BIAS_DOWN, GAIN_1, SHIFT_1, GAIN_2, SHIFT_2):
        gvec[row] = jnp.zeros((1, width), F32)
    for row in range(BIAS_UP + tiles, TABLE):
        gvec[row] = jnp.zeros((1, width), F32)
    gattn = mixed
    gmix = second

    def middle_back(i):
        at = pl.ds(pl.multiple_of(i * 128, 128), 128)
        grad = gtok[at, :]
        scaled, inverse = normed(middle[at, :])
        ahead = gout[at, :].astype(F32)
        gvec[GAIN_2] += column_sum(grad * scaled)
        gvec[SHIFT_2] += column_sum(grad)
        gvec[BIAS_DOWN] += column_sum(ahead)
        total = ahead + normed_back(grad, scaled, inverse, vec[GAIN_2])
        gtok[at, :] = total
        rounded = total.astype(BF)
        gattn[at, :] = rounded
        gvec[BIAS_OUT] += column_sum(rounded.astype(F32))
        gmix[at, :] = mul_nt(rounded, flat(wo[...])).astype(BF)

    loop(rows // 128, middle_back)

    base_gmix = number.take(pairs)
    near_gmix = local_number.take(1)
    here_rows = pl.ds(pl.multiple_of(s * rows, 128), rows)
    there_rows = pl.ds(pl.multiple_of((1 - s) * rows, 128), rows)

    def send_gmix(p):
        lanes_p = pl.ds(pl.multiple_of((1 - s) * local + p * 128, 128), 128)
        at = pl.ds(pl.multiple_of(p * 128, 128), 128)
        return far(gmix.at[:, lanes_p], gmix_head.at[here_rows, at], base_gmix + p, x_peer)

    def take_gmix(p):
        at = pl.ds(pl.multiple_of(p * 128, 128), 128)
        return far(gmix.at[:, pl.ds(0, 128)], gmix_head.at[there_rows, at], base_gmix + p, x_peer)

    keep_gmix = pltpu.make_async_copy(
        gmix.at[:, mine], gmix_head.at[here_rows, :], near_sem.at[near_gmix]
    )
    for p in range(pairs):
        send_gmix(p).start()
    keep_gmix.start()

    gather_o.sent()

    def weigh_out(m):
        at = pl.ds(pl.multiple_of(m * 4 * rq, 4 * rq), 4 * rq)
        wo[m] = mul(mixed_t[at, :], gattn[...]).astype(BF)

    loop(zs, weigh_out)
    y_start_d(turn(2, z))
    z_start_d(turn(1, z))
    for t in range(tiles):
        gather_u(t).sent()

    class Spread:
        def __init__(self, ref, columns, r1, r2, r3, base):
            self.ref, self.columns, self.r1, self.r2, self.r3 = ref, columns, r1, r2, r3
            self.base = base

        def sib(self, yy):
            return far_g(
                self.ref.at[:, block_rows(rq, yy, 1 - c), self.columns],
                self.r1.at[:, pl.ds(pl.multiple_of(yy * rq, rq), rq), self.columns],
                self.base + yy, c_peer,
            )

        def sib_start(self):
            self.sib(1 - y).start()
            self.sib(y).start()

        def along_y(self):
            return far_g(
                self.r1.at[:, pl.ds(pl.multiple_of((1 - y) * rq, rq), rq), self.columns],
                self.r2.at[:, :, self.columns], self.base + 2, y_peer,
            )

        def y_start(self):
            self.sib(1 - y).wait_recv()
            at = pl.ds(pl.multiple_of((1 - y) * rq, rq), rq)
            for zz in range(zs):
                self.r1[zz, at, self.columns] = (
                    self.r1[zz, at, self.columns].astype(F32)
                    + self.ref[zz, block_rows(rq, 1 - y, c), self.columns].astype(F32)
                ).astype(BF)
            self.along_y().start()

        def along_z(self, dz):
            return far_g(
                self.r2.at[lax.rem(z + dz, zs), :, self.columns],
                self.r3.at[dz - 1, :, self.columns], self.base + 2 + dz, z_peers[dz - 1],
            )

        def z_start(self):
            self.sib(y).wait_recv()
            self.along_y().wait_recv()
            at = pl.ds(pl.multiple_of(y * rq, rq), rq)
            for zz in range(zs):
                self.r2[zz, :, self.columns] = (
                    self.r2[zz, :, self.columns].astype(F32)
                    + self.r1[zz, at, self.columns].astype(F32)
                    + self.ref[zz, block_rows(rq, y, c), self.columns].astype(F32)
                ).astype(BF)
            for dz in range(1, zs):
                self.along_z(dz).start()

        def z_finish(self):
            total = self.r2[z, :, self.columns].astype(F32)
            for dz in range(1, zs):
                self.along_z(dz).wait_recv()
                total = total + self.r3[dz - 1, :, self.columns].astype(F32)
            return total

        def sent(self):
            self.sib(0).wait_send()
            self.sib(1).wait_send()
            self.along_y().wait_send()
            for dz in range(1, zs):
                self.along_z(dz).wait_send()

    spread_steps = zs + 2
    sum_o = Spread(wo, pl.ds(0, width), r1_o, r2_o, r3_o, number.take(spread_steps))
    base_sq = number.take(pairs * spread_steps)

    def sum_q(p):
        return Spread(
            gwq, pl.ds(pl.multiple_of(p * local, 128), local), r1_q, r2_q, r3_q,
            base_sq + p * spread_steps,
        )

    sum_o.sib_start()

    def weigh_up_tile(t):
        def weigh_up(m):
            at = pl.ds(pl.multiple_of(m * 4 * rq, 4 * rq), 4 * rq)
            wu[m, :, tile_lanes(t)] = mul(second_t[at, :], slope[:, tile_lanes(t)]).astype(BF)

        loop(zs, weigh_up)
        sib_start_u(t)

        @pl.when(t == 0)
        def _():
            sum_o.y_start()

        @pl.when(t > 0)
        def _():
            y_start_u(t - 1)

        @pl.when(t == 2)
        def _():
            y_start_d(z)
            z_start_d(turn(2, z))

    loop(tiles, weigh_up_tile)
    y_start_u(tiles - 1)

    def fall(t):
        def add(i):
            at = pl.ds(pl.multiple_of(i * side, side), side)
            middle[at, :] += mul(hidden[at, tile_lanes(t)], wd[t])

        loop(rows // side, add)

    loop(tiles, fall)

    def finish_out(i):
        at = pl.ds(pl.multiple_of(i * 128, 128), 128)
        value = middle[at, :] + vec[BIAS_DOWN]
        spot = s * rows + i * 128 + lax.broadcasted_iota(jnp.int32, (128, width), 0)
        out[at, :] = jnp.where(spot < last_valid, value, 0.0).astype(BF)

    loop(rows // 128, finish_out)
    keep_gmix.wait()

    xd = far_g(r5_d.at[s], r5_d.at[s], base_xs, x_peer)
    xo = far_g(r5_o.at[0], r5_o.at[1], number.take(1), x_peer)

    def finish_d():
        total = ry_d[z].astype(F32)
        for dz in range(1, zs):
            far_g(ry_d.at[0], rz_d.at[dz - 1], base_zd + dz - 1, z_peers[dz - 1]).wait_recv()
            total = total + rz_d[dz - 1].astype(F32)
        r5_d[s] = total.astype(BF)
        xd.start()

    def finish_o():
        r5_o[0] = sum_o.z_finish().astype(BF)
        xo.start()

    def serve(k):
        @pl.when(k == 0)
        def _():
            sum_o.z_start()

        @pl.when(k == 2)
        def _():
            z_start_u(0)

        @pl.when(k == 3)
        def _():
            z_start_u(1)
            finish_o()

        @pl.when(k == 4)
        def _():
            z_start_u(2)

        @pl.when(k == 5)
        def _():
            z_start_d(z)

    def attend_back(p):
        dk[...] = jnp.zeros_like(dk)
        dv[...] = jnp.zeros_like(dv)

        def head(h):
            half = pl.ds(pl.multiple_of(h * HEAD_DIM, HEAD_DIM), HEAD_DIM)
            here = pl.ds(pl.multiple_of(p * 128, 128), 128)
            for qi in range(blocks):
                at = slice(qi * side, (qi + 1) * side)
                query = head_lanes(qkv[at, lanes(p, 0)].astype(F32) * scale, h)
                grad = head_lanes(gmix_head[at, here].astype(F32), h)
                level = lse[p, h, :, at]
                weights, slopes = [], []
                centre = jnp.zeros((1, side), F32)
                for j in range(qi + 1):
                    there = slice(j * side, (j + 1) * side)
                    raw = scores(p, qkv[there, lanes(p, 1)], query, qi, j)
                    weight = jnp.exp(raw - level)
                    slope = mul_nt(qkv[there, lanes(p, 2)], grad)
                    centre = centre + column_sum(weight * slope)
                    weights.append(weight)
                    slopes.append(slope)
                total = jnp.zeros((HEAD_DIM, side), F32)
                for j in range(qi + 1):
                    there = slice(j * side, (j + 1) * side)
                    bend = (weights[j] * (slopes[j] - centre)).astype(BF)
                    dk[there, :] += mul(bend, query)
                    dv[there, :] += mul(weights[j].astype(BF), grad)
                    total = total + mul(k_t[p, half, there], bend)
                o_t[half, at] = total * scale
            serve(p * 2 + h)

        loop(2, head)
        for qi in range(blocks):
            at = slice(qi * side, (qi + 1) * side)
            qkv[at, lanes(p, 0)] = o_t[:, at].T.astype(BF)
            qkv[at, lanes(p, 1)] = dk[at, :].astype(BF)
            qkv[at, lanes(p, 2)] = dv[at, :].astype(BF)
        own = pl.ds(pl.multiple_of(s * local + p * 128, 128), 128)
        gvec[BIAS_Q, :, own] = column_sum(qkv[:, lanes(p, 0)].astype(F32))
        gvec[BIAS_V, :, own] = column_sum(qkv[:, lanes(p, 2)].astype(F32))
        both = pl.ds(pl.multiple_of(p * local, 128), local)

        def weigh(m):
            at = pl.ds(pl.multiple_of(m * 4 * rq, 4 * rq), 4 * rq)
            gwq[m, :, both] = mul(first_t[at, :], qkv[:, both]).astype(BF)

        loop(zs, weigh)

    def pair_back(p):
        take_gmix(p).wait_recv()
        attend_back(p)
        sum_q(p).sib_start()

        @pl.when(p > 0)
        def _():
            sum_q(p - 1).y_start()

    loop(pairs, pair_back)

    base_gf = number.take(rows // side)

    def send_gf(i):
        at = pl.ds(pl.multiple_of(i * side, side), side)
        there = pl.ds(pl.multiple_of(rows + i * side, side), side)
        return far(first.at[at, :], first.at[there, :], base_gf + i, x_peer)

    def first_back(i, source, at):
        there = pl.ds(pl.multiple_of(at + i * side, side), side)
        grad = mul_nt(qkv[there, :], flat(wq[...]))
        scaled, unused = normed(source[pl.ds(pl.multiple_of(i * side, side), side), :].astype(F32))
        gvec[GAIN_1] += column_sum(grad * scaled)
        gvec[SHIFT_1] += column_sum(grad)
        return grad

    def away(i):
        grad = first_back(i, tok_far, (1 - s) * rows)
        first[pl.ds(pl.multiple_of(i * side, side), side), :] = grad.astype(BF)
        send_gf(i).start()

    loop(rows // side, away)
    sum_q(pairs - 1).y_start()
    z_start_u(3)

    def stay(i):
        middle[pl.ds(pl.multiple_of(i * side, side), side), :] = first_back(i, tok, s * rows)

    loop(rows // side, stay)

    base_v = number.take(zs + 2)
    for dz in range(1, zs):
        far(gvec, v_z.at[dz - 1], base_v + dz - 1, z_peers[dz - 1]).start()
    for dz in range(1, zs):
        far(gvec, v_z.at[dz - 1], base_v + dz - 1, z_peers[dz - 1]).wait_recv()
    for i in range(TABLE):
        total = gvec[i]
        for dz in range(1, zs):
            total = total + v_z[dz - 1, i]
        v_sum[0, i] = total
    vy = far(v_sum.at[0], v_y, base_v + zs - 1, y_peer)
    vy.start()
    for p in range(pairs):
        sum_q(p).z_start()
    vy.wait_recv()
    v_sum[1] = v_sum[0] + v_y[...]
    vc = far(v_sum.at[1], v_c, base_v + zs, c_peer)
    vc.start()
    vc.wait_recv()
    v_sum[2] = v_sum[1] + v_c[...]
    vx = far(v_sum.at[2], v_x, base_v + zs + 1, x_peer)
    vx.start()

    finish_d()
    for t in range(tiles):
        for dz in range(1, zs):
            z_u(t, dz).wait_recv()

    def finish_u(t):
        total = r2_u[z, :, tile_lanes(t)].astype(F32)
        for dz in range(1, zs):
            total = total + r3_u[dz - 1, :, tile_lanes(t)].astype(F32)
        r5_u[0, :, tile_lanes(t)] = total.astype(BF)

    loop(tiles, finish_u)
    xu = far_g(r5_u.at[0], r5_u.at[1], base_xs + 1, x_peer)
    xu.start()
    for p in range(pairs):
        r5_q[s, :, p * local : (p + 1) * local] = sum_q(p).z_finish().astype(BF)
    slot_q = number.take(1)
    xq = far_g(r5_q.at[s], r5_q.at[s], slot_q, x_peer)
    xq.start()

    for i in range(rows // side):
        send_gf(i).wait_recv()

    def last(i):
        at = pl.ds(pl.multiple_of(i * 128, 128), 128)
        scaled, inverse = normed(tok[at, :].astype(F32))
        there = pl.ds(pl.multiple_of(rows + i * 128, 128), 128)
        grad = middle[at, :] + first[there, :].astype(F32)
        gtok[at, :] = gtok[at, :] + normed_back(grad, scaled, inverse, vec[GAIN_1])

    loop(rows // 128, last)

    vx.wait_recv()
    out_v[...] = v_sum[2] + v_x[...]
    far_g(r5_d.at[1 - s], r5_d.at[1 - s], base_xs, x_peer).wait_recv()
    for half in range(2):
        out_d[:, half * local : (half + 1) * local] = r5_d[half].astype(F32)
    xu.wait_recv()

    def store_u(t):
        out_u[:, tile_lanes(t)] = r5_u[0, :, tile_lanes(t)].astype(F32) + r5_u[1, :, tile_lanes(t)].astype(F32)

    loop(tiles, store_u)
    xo.wait_recv()
    out_o[...] = r5_o[0].astype(F32) + r5_o[1].astype(F32)
    far_g(r5_q.at[1 - s], r5_q.at[1 - s], slot_q, x_peer).wait_recv()
    for half in range(2):
        for p in range(pairs):
            for part in range(3):
                at = part * width + half * local + p * 128
                out_q[:, at : at + 128] = r5_q[
                    half, :, p * local + part * 128 : p * local + part * 128 + 128
                ].astype(F32)

    for dz in range(1, zs):
        far(table, e_z.at[dz - 1], base_e + dz - 1, z_peers[dz - 1]).wait_send()
        far(gvec, v_z.at[dz - 1], base_v + dz - 1, z_peers[dz - 1]).wait_send()
        far_g(ry_d.at[0], rz_d.at[dz - 1], base_zd + dz - 1, z_peers[dz - 1]).wait_send()
    for copy in (y_table, c_table, send_tok, vy, vc, vx, xd, xu, xo, xq):
        copy.wait_send()
    for p in range(pairs):
        gather_q(p).sent()
        send_mixed(p).wait_send()
        sum_q(p).sent()
    sum_o.sent()
    for i in range(cuts):
        gather_d(i).sent()
    for i in range(2):
        gather_w(i).sent()
    for p in range(pairs):
        send_gmix(p).wait_send()
    for t in range(tiles):
        for yy in range(2):
            sib_d(t, yy).wait_send()
            sib_u(t, yy).wait_send()
        x_d(t).wait_send()
        y_d(t).wait_send()
        y_u(t).wait_send()
        for dz in range(1, zs):
            z_u(t, dz).wait_send()
    for i in range(rows // side):
        send_gf(i).wait_send()


def fused_fits(tokens, lengths, own_q, own_d, shards, pair):
    rows, width = tokens.shape
    return (
        shards == 16
        and pair == 2
        and rows % 256 == 0
        and (width // pair) % 128 == 0
        and own_q.shape[0] % 16 == 0
        and own_d.shape[0] % 64 == 0
        and own_d.shape[0] * shards == 4 * width
    )


def fused(tokens, lengths, w_qkv, w_out, w_up, w_down, small, bias_up, cotangent):
    rows, width = tokens.shape
    shards = lax.axis_size("dp")
    zs = shards // 4
    d = lax.axis_index("dp")
    rq, rd = w_qkv.shape[0], w_down.shape[0]
    deep = 4 * rd * zs
    group = 2 * rows
    local = width // 2
    pairs = local // 128
    lane = jnp.arange(width)
    own = jnp.where(lane // rq == d, jnp.tile(jnp.stack(small), (1, shards)), 0)
    at = jnp.arange(zs)[:, None] * width + lane[None, :]
    up = jnp.where(at // rd == d, jnp.tile(bias_up, (width // rd,))[None, :], 0)
    table = jnp.concatenate([own, up, jnp.zeros((TABLE - 8 - zs, width), own.dtype)], axis=0)

    def vm(shape, kind=BF):
        return pltpu.VMEM(shape, kind)

    scratch = [
        vm((zs, 4 * rq, 3 * local)), vm((zs, 4 * rq, width)), vm((zs, 4 * rq, deep)),
        vm((zs, 4 * rd, width)), vm((zs, 4 * rq, 3 * local)), vm((zs, 4 * rd, width)),
        vm((rows, width)), vm((rows, width)), vm((group, width)), vm((width, group)), vm((group, 3 * local)),
        vm((pairs, 128, group)), vm((pairs, 128, group)), vm((1, group), jnp.int32),
        vm((pairs, 2, 1, group), F32), vm((128, group), F32),
        vm((group, local)), vm((rows, width)), vm((width, rows)), vm((rows, width), F32),
        vm((rows, width)), vm((width, rows)), vm((rows, width)),
        vm((rows, deep)), vm((4 * rd, rows)), vm((rows, deep)),
        vm((group, local)), vm((group, 128), F32), vm((group, 128), F32),
        vm((2, TABLE, width)), vm((zs - 1, TABLE, width)), vm((TABLE, width)), vm((TABLE, width)),
        vm((TABLE, 1, width), F32), vm((TABLE, 1, width), F32), vm((zs - 1, TABLE, 1, width), F32),
        vm((TABLE, 1, width), F32), vm((TABLE, 1, width), F32), vm((TABLE, 1, width), F32),
        vm((3, TABLE, 1, width), F32),
        vm((zs, 2 * rd, width)), vm((zs, 2 * rd, local)), vm((zs, rd, local)),
        vm((zs - 1, rd, local)), vm((2, rd, local)),
        vm((zs, 2 * rq, deep)), vm((zs, rq, deep)), vm((zs - 1, rq, deep)), vm((2, rq, deep)),
        vm((zs, 2 * rq, width)), vm((zs, rq, width)), vm((zs - 1, rq, width)), vm((2, rq, width)),
        vm((zs, 2 * rq, 3 * local)), vm((zs, rq, 3 * local)), vm((zs - 1, rq, 3 * local)),
        vm((2, rq, 3 * local)),
        pltpu.SemaphoreType.DMA((NEAR_COUNT,)),
        pltpu.SemaphoreType.DMA((FAR_COUNT,)),
        pltpu.SemaphoreType.DMA((FAR_COUNT,)),
    ]
    here = pl.BlockSpec(memory_space=pltpu.VMEM)
    away = pl.BlockSpec(memory_space=pl.ANY)
    return pl.pallas_call(
        fused_kernel,
        out_shape=(
            jax.ShapeDtypeStruct((rows, width), BF),
            jax.ShapeDtypeStruct((rows, width), F32),
            jax.ShapeDtypeStruct((rq, 3 * width), F32),
            jax.ShapeDtypeStruct((rq, width), F32),
            jax.ShapeDtypeStruct((rq, deep), F32),
            jax.ShapeDtypeStruct((rd, width), F32),
            jax.ShapeDtypeStruct((TABLE, 1, width), F32),
        ),
        in_specs=[pl.BlockSpec(memory_space=pltpu.SMEM), here, away, away, away, away, away, away],
        out_specs=[here] * 7,
        scratch_shapes=scratch,
        compiler_params=pltpu.CompilerParams(
            collective_id=0, has_side_effects=True, vmem_limit_bytes=67_043_328
        ),
        name="block",
    )(lengths, table, tokens, cotangent, w_qkv, w_out, w_up, w_down)


def per_device(
    tokens, lengths, w_qkv, w_out, w_up, w_down, bias_q, bias_v, bias_out, bias_up, bias_down,
    gain_one, shift_one, gain_two, shift_two, cotangent,
):
    if not fused_fits(
        tokens, lengths, w_qkv, w_down, lax.axis_size("dp"), lax.axis_size("seq")
    ):
        return per_device_plain(
            tokens, lengths, w_qkv, w_out, w_up, w_down, bias_q, bias_v, bias_out, bias_up,
            bias_down, gain_one, shift_one, gain_two, shift_two, cotangent,
        )
    small = [bias_q, bias_v, bias_out, bias_down, gain_one, shift_one, gain_two, shift_two]
    out, gtok, gq, go, gu, gd, table = fused(
        tokens, lengths, w_qkv, w_out, w_up, w_down, small, bias_up, cotangent
    )
    d = lax.axis_index("dp")
    width = tokens.shape[1]
    rq, rd = w_qkv.shape[0], w_down.shape[0]
    own = lax.dynamic_slice_in_dim(table[:8, 0], d * rq, rq, axis=1)
    up = lax.dynamic_slice_in_dim(
        table[8:].reshape((TABLE - 8) * width), d * rd, rd, axis=0
    )
    return (
        out, gtok, gq, go, gu, gd,
        own[0], own[1], own[2], up, own[3], own[4], own[5], own[6], own[7],
    )


def solution(mesh):
    return jax.shard_map(
        per_device,
        mesh=mesh,
        in_specs=(
            P(("dp", "seq"), None),
            P("dp", None),
            P("dp", None),
            P("dp", None),
            P("dp", None),
            P("dp", None),
            P("dp"),
            P("dp"),
            P("dp"),
            P("dp"),
            P("dp"),
            P("dp"),
            P("dp"),
            P("dp"),
            P("dp"),
            P(("dp", "seq"), None),
        ),
        out_specs=(
            P(("dp", "seq"), None),
            P(("dp", "seq"), None),
            P("dp", None),
            P("dp", None),
            P("dp", None),
            P("dp", None),
            P("dp"),
            P("dp"),
            P("dp"),
            P("dp"),
            P("dp"),
            P("dp"),
            P("dp"),
            P("dp"),
            P("dp"),
        ),
        check_vma=False,
    )
```

```python
import jax
import jax.numpy as jnp
from jax import lax
from jax.experimental import pallas as pl
from jax.experimental.pallas import tpu as pltpu
from jax.sharding import PartitionSpec as P

HEAD_DIM = 64


EPSILON = 1e-05
MASKED = -1e30
SLOPE = 0.7978845608028654
CUBIC = 0.044715


def as_sent(array):
    return jax.tree.map(lambda a: a.astype(jnp.bfloat16) if a.dtype == jnp.float32 else a, array)


def dense(left, right):
    return jnp.dot(left, right, preferred_element_type=jnp.float32)


def dense_left(left, right):
    return lax.dot_general(
        left, right, (((0,), (0,)), ((), ())), preferred_element_type=jnp.float32
    )


def dense_right(left, right):
    return lax.dot_general(
        left, right, (((1,), (1,)), ((), ())), preferred_element_type=jnp.float32
    )


def norm_parts(value):
    mean = jnp.mean(value, axis=-1, keepdims=True)
    centred = value - mean
    inverse = lax.rsqrt(jnp.mean(centred * centred, axis=-1, keepdims=True) + EPSILON)
    return (centred * inverse, inverse)


def norm_back(grad, scaled, inverse, gain):
    shaped = grad * gain
    inner = jnp.mean(shaped * scaled, axis=-1, keepdims=True)
    return inverse * (shaped - jnp.mean(shaped, axis=-1, keepdims=True) - scaled * inner)


def gelu_value(value):
    return 0.5 * value * (1.0 + jnp.tanh(SLOPE * (value + CUBIC * value * value * value)))


def gelu_slope(value):
    bent = jnp.tanh(SLOPE * (value + CUBIC * value * value * value))
    return 0.5 * (1.0 + bent) + 0.5 * value * (1.0 - bent * bent) * SLOPE * (
        1.0 + 3.0 * CUBIC * value * value
    )


def per_device_plain(
    tokens,
    lengths,
    w_qkv,
    w_out,
    w_up,
    w_down,
    bias_q,
    bias_v,
    bias_out,
    bias_up,
    bias_down,
    gain_one,
    shift_one,
    gain_two,
    shift_two,
    cotangent,
):
    width = tokens.shape[1]
    rows = tokens.shape[0]
    pair = lax.axis_size("seq")
    rank = lax.axis_index("seq")
    group = rows * pair
    local = width // pair
    heads = local // HEAD_DIM
    scale = HEAD_DIM ** (-0.5)
    block = 512
    blocks = group // block
    whole = (
        lax.all_gather(w_qkv, "dp", axis=0, tiled=True),
        lax.all_gather(w_out, "dp", axis=0, tiled=True),
        lax.all_gather(w_up, "dp", axis=0, tiled=True),
        lax.all_gather(w_down, "dp", axis=0, tiled=True),
        lax.all_gather(bias_q, "dp", axis=0, tiled=True),
        lax.all_gather(bias_v, "dp", axis=0, tiled=True),
        lax.all_gather(bias_out, "dp", axis=0, tiled=True),
        lax.all_gather(bias_up, "dp", axis=0, tiled=True),
        lax.all_gather(bias_down, "dp", axis=0, tiled=True),
        lax.all_gather(gain_one, "dp", axis=0, tiled=True),
        lax.all_gather(shift_one, "dp", axis=0, tiled=True),
        lax.all_gather(gain_two, "dp", axis=0, tiled=True),
        lax.all_gather(shift_two, "dp", axis=0, tiled=True),
    )
    weight_qkv, weight_out, weight_up, weight_down = whole[0:4]
    add_q, add_v, add_out, add_up, add_down, scale_one, move_one, scale_two, move_two = [
        piece.astype(jnp.float32) for piece in whole[4:]
    ]
    slots = lengths.shape[1]
    position = jnp.arange(group, dtype=jnp.int32)
    ends = jnp.cumsum(lengths[0])
    segment = jnp.sum((position[:, None] >= ends[None, :]).astype(jnp.int32), axis=1)
    own_segment = lax.dynamic_slice_in_dim(segment, rank * rows, rows)
    valid = (own_segment < slots - 1)[:, None]
    inputs = tokens.astype(jnp.float32)
    scaled_one, inverse_one = norm_parts(inputs)
    first = (scaled_one * scale_one + move_one).astype(jnp.bfloat16)
    bias_qkv = jnp.concatenate([add_q, jnp.zeros_like(add_q), add_v])
    qkv = (dense(first, weight_qkv) + bias_qkv).astype(jnp.bfloat16)
    head_side = lax.all_to_all(
        qkv.reshape(rows, 3, pair, local), "seq", split_axis=2, concat_axis=0, tiled=True
    )
    query = head_side[:, 0, 0].reshape(group, heads, HEAD_DIM)
    keys = head_side[:, 1, 0].reshape(group, heads, HEAD_DIM)
    values = head_side[:, 2, 0].reshape(group, heads, HEAD_DIM)

    def block_scores(index):
        start = index * block
        query_rows = lax.dynamic_slice_in_dim(query, start, block)
        raw = (
            jnp.einsum("qhd,khd->hqk", query_rows, keys, preferred_element_type=jnp.float32) * scale
        )
        row_segment = lax.dynamic_slice_in_dim(segment, start, block)
        row_position = lax.dynamic_slice_in_dim(position, start, block)
        allowed = (row_segment[:, None] == segment[None, :]) & (
            position[None, :] <= row_position[:, None]
        )
        return (jnp.where(allowed[None], raw, MASKED), query_rows)

    def attend(index):
        scores, unused = block_scores(index)
        top = jnp.max(scores, axis=-1, keepdims=True)
        weights = jnp.exp(scores - top)
        total = jnp.sum(weights, axis=-1, keepdims=True)
        probs = (weights / total).astype(jnp.bfloat16)
        mixed_rows = jnp.einsum("hqk,khd->qhd", probs, values, preferred_element_type=jnp.float32)
        return (
            mixed_rows.reshape(block, local).astype(jnp.bfloat16),
            (top + jnp.log(total))[:, :, 0],
        )

    mixed_blocks, log_totals = lax.map(attend, jnp.arange(blocks))
    mixed_head = mixed_blocks.reshape(group, 1, local)
    mixed = lax.all_to_all(mixed_head, "seq", split_axis=0, concat_axis=1, tiled=True).reshape(
        rows, width
    )
    middle = inputs + dense(mixed, weight_out) + add_out
    scaled_two, inverse_two = norm_parts(middle)
    second = (scaled_two * scale_two + move_two).astype(jnp.bfloat16)
    pre = dense(second, weight_up) + add_up
    hidden = gelu_value(pre).astype(jnp.bfloat16)
    result = middle + dense(hidden, weight_down) + add_down
    block_out = jnp.where(valid, result, 0.0).astype(jnp.bfloat16)
    grad_out = jnp.where(valid, cotangent, jnp.zeros_like(cotangent))
    grad_weight_down = dense_left(hidden, grad_out)
    grad_add_down = jnp.sum(grad_out.astype(jnp.float32), axis=0)
    grad_pre = (dense_right(grad_out, weight_down) * gelu_slope(pre)).astype(jnp.bfloat16)
    grad_weight_up = dense_left(second, grad_pre)
    grad_add_up = jnp.sum(grad_pre.astype(jnp.float32), axis=0)
    grad_second = dense_right(grad_pre, weight_up)
    grad_scale_two = jnp.sum(grad_second * scaled_two, axis=0)
    grad_move_two = jnp.sum(grad_second, axis=0)
    grad_middle = grad_out.astype(jnp.float32) + norm_back(
        grad_second, scaled_two, inverse_two, scale_two
    )
    grad_attn = grad_middle.astype(jnp.bfloat16)
    grad_weight_out = dense_left(mixed, grad_attn)
    grad_add_out = jnp.sum(grad_attn.astype(jnp.float32), axis=0)
    grad_mixed = dense_right(grad_attn, weight_out).astype(jnp.bfloat16)
    branch_grads = (
        grad_weight_out,
        grad_weight_up,
        grad_weight_down,
        grad_add_out,
        grad_add_up,
        grad_add_down,
        grad_scale_two,
        grad_move_two,
    )
    grad_head = lax.all_to_all(
        grad_mixed.reshape(rows, pair, local), "seq", split_axis=1, concat_axis=0, tiled=True
    )
    grad_head = grad_head.reshape(group, heads, HEAD_DIM)

    def attend_back(carry, index):
        grad_keys, grad_values = carry
        scores, query_rows = block_scores(index)
        probs = jnp.exp(scores - log_totals[index][:, :, None])
        grad_rows = lax.dynamic_slice_in_dim(grad_head, index * block, block)
        grad_probs = jnp.einsum(
            "qhd,khd->hqk", grad_rows, values, preferred_element_type=jnp.float32
        )
        centre = jnp.sum(probs * grad_probs, axis=-1, keepdims=True)
        grad_scores = (probs * (grad_probs - centre)).astype(jnp.bfloat16)
        grad_values = grad_values + jnp.einsum(
            "hqk,qhd->khd",
            probs.astype(jnp.bfloat16),
            grad_rows,
            preferred_element_type=jnp.float32,
        )
        grad_keys = (
            grad_keys
            + jnp.einsum(
                "hqk,qhd->khd", grad_scores, query_rows, preferred_element_type=jnp.float32
            )
            * scale
        )
        grad_query = (
            jnp.einsum("hqk,khd->qhd", grad_scores, keys, preferred_element_type=jnp.float32)
            * scale
        )
        return ((grad_keys, grad_values), grad_query)

    empty = jnp.zeros((group, heads, HEAD_DIM), jnp.float32)
    (grad_keys, grad_values), grad_queries = lax.scan(
        attend_back, (empty, empty), jnp.arange(blocks)
    )
    grad_side = jnp.stack(
        [
            grad_queries.reshape(group, local),
            grad_keys.reshape(group, local),
            grad_values.reshape(group, local),
        ],
        axis=1,
    ).astype(jnp.bfloat16)
    grad_qkv = lax.all_to_all(
        grad_side.reshape(group, 3, 1, local), "seq", split_axis=0, concat_axis=2, tiled=True
    )
    grad_qkv = grad_qkv.reshape(rows, 3 * width)
    grad_weight_qkv = dense_left(first, grad_qkv)
    column_sums = jnp.sum(grad_qkv.astype(jnp.float32), axis=0)
    grad_add_q = column_sums[:width]
    grad_add_v = column_sums[2 * width :]
    grad_first = dense_right(grad_qkv, weight_qkv)
    grad_scale_one = jnp.sum(grad_first * scaled_one, axis=0)
    grad_move_one = jnp.sum(grad_first, axis=0)
    grad_tokens = grad_middle + norm_back(grad_first, scaled_one, inverse_one, scale_one)
    stem_grads = (grad_weight_qkv, grad_add_q, grad_add_v, grad_scale_one, grad_move_one)
    halves = lax.psum_scatter(
        stem_grads + branch_grads, ("dp", "seq"), scatter_dimension=0, tiled=True
    )
    shares = jax.tree.map(
        lambda part, own: part.astype(own.dtype),
        lax.all_gather(as_sent(halves), "seq", axis=0, tiled=True),
        halves,
    )
    stem_shares = shares[0:5]
    branch_shares = shares[5:13]
    return (
        block_out,
        grad_tokens,
        stem_shares[0],
        branch_shares[0],
        branch_shares[1],
        branch_shares[2],
        stem_shares[1],
        stem_shares[2],
        branch_shares[3],
        branch_shares[4],
        branch_shares[5],
        stem_shares[3],
        stem_shares[4],
        branch_shares[6],
        branch_shares[7],
    )


FAR = pl.DeviceIdType.MESH
NT = (((1,), (1,)), ((), ()))
BF = jnp.bfloat16
F32 = jnp.float32


def mul(left, right):
    return jnp.dot(left, right, preferred_element_type=F32)


def mul_nt(left, right):
    return lax.dot_general(left, right, NT, preferred_element_type=F32)


def flat(blocks):
    return blocks.reshape(blocks.shape[0] * blocks.shape[1], blocks.shape[2])


def normed(value):
    width = value.shape[1]
    mean = jnp.sum(value, axis=1, keepdims=True) * (1.0 / width)
    centred = value - mean
    spread = jnp.sum(centred * centred, axis=1, keepdims=True) * (1.0 / width)
    inverse = lax.rsqrt(spread + EPSILON)
    return (centred * inverse, inverse)


def normed_back(grad, scaled, inverse, gain):
    width = grad.shape[1]
    shaped = grad * gain
    inner = jnp.sum(shaped * scaled, axis=1, keepdims=True) * (1.0 / width)
    outer = jnp.sum(shaped, axis=1, keepdims=True) * (1.0 / width)
    return inverse * (shaped - outer - scaled * inner)


def column_sum(value):
    return jnp.sum(value, axis=0, keepdims=True)


class Numbers:
    def __init__(self):
        self.used = 0

    def take(self, count):
        start = self.used
        self.used = start + count
        return start


BIAS_Q, BIAS_V, GAIN_1, SHIFT_1, BIAS_OUT, BIAS_DOWN, GAIN_2, SHIFT_2, BIAS_UP = range(9)
TABLE = 16
FAR_COUNT = 240
NEAR_COUNT = 32


def fused_kernel(
    lengths, table, tok_own, cot, own_q, own_o, own_u, own_d,
    out, gtok, out_q, out_o, out_u, out_d, out_v,
    wq, wo, wu, wd, gwq, gwd,
    tok, tok_far, first, first_t, qkv, k_t, v_t, lower, lse, o_t,
    mixed_near, mixed, mixed_t, middle, second, second_t, gout,
    hidden, hidden_t, slope, pieces,
    e_own, e_z, e_y, e_c, vec, gvec, v_z, v_y, v_c, v_x, v_sum,
    r1_d, rx_d, ry_d, rz_d, r5_d, r1_u, rx_u, ry_u, rz_u, r5_u,
    r2_u, r3_u, r4_u, r1_o, r2_o, r3_o, r4_o, r1_q, r2_q, r3_q, r5_q,
    near_sem, send_sem, recv_sem,
):
    d = lax.axis_index("dp")
    s = lax.axis_index("seq")
    z = lax.div(d, 4)
    y = lax.rem(lax.div(d, 2), 2)
    c = lax.rem(d, 2)
    zs = wq.shape[0]
    rows, width = tok_own.shape
    group = 2 * rows
    local = width // 2
    pairs = local // 128
    rq = width // (4 * zs)
    rd = own_d.shape[0]
    tile = 4 * rd
    tiles = zs
    z_peers = [(lax.rem(z + dz, zs) * 4 + y * 2 + c, s) for dz in range(1, zs)]
    y_peer = (z * 4 + (1 - y) * 2 + c, s)
    c_peer = (z * 4 + y * 2 + (1 - c), s)
    x_peer = (d, 1 - s)
    number = Numbers()
    local_number = Numbers()

    def far(src, dst, slot, device):
        return pltpu.make_async_remote_copy(
            src_ref=src, dst_ref=dst, send_sem=send_sem.at[slot], recv_sem=recv_sem.at[slot],
            device_id=device, device_id_type=FAR,
        )

    far_w, far_g = far, far

    def z_at(dz):
        return lax.rem(z + zs - dz, zs)

    def loop(count, body):
        lax.fori_loop(0, count, lambda i, carry: (body(i), carry)[1], 0)

    def block_rows(r, yy, cc):
        return pl.ds(pl.multiple_of((yy * 2 + cc) * r, r), r)

    barrier = pltpu.get_barrier_semaphore()
    everyone = z_peers + [y_peer, c_peer, x_peer]
    for peer in everyone:
        pl.semaphore_signal(barrier, inc=1, device_id=peer, device_id_type=FAR)
    pl.semaphore_wait(barrier, len(everyone))

    class Gather:
        def __init__(self, ref, r, columns, base, own=None, columns_at=None):
            self.ref, self.r, self.columns, self.base, self.own = ref, r, columns, base, own
            self.columns_at = columns_at

        def part(self, zz, yy, cc):
            return self.ref.at[zz, block_rows(self.r, yy, cc), self.columns]

        def layer(self, yy, cc, columns=None):
            columns = self.columns if columns is None else columns
            return self.ref.at[:, block_rows(self.r, yy, cc), columns]

        def z_copy(self, dz):
            columns = self.columns if self.columns_at is None else self.columns_at(dz)
            there = self.ref.at[z, block_rows(self.r, y, c), columns]
            here = there if self.own is None else self.own.at[:, columns]
            return far_w(here, there, self.base + dz - 1, z_peers[dz - 1])

        def z_start(self):
            for dz in range(1, zs):
                self.z_copy(dz).start()

        def z_wait(self):
            for dz in range(1, zs):
                block = self.part(z_at(dz), y, c)
                far_w(block, block, self.base + dz - 1, z_peers[dz - 1]).wait_recv()

        def y_copy(self, yy):
            return far_w(self.layer(yy, c), self.layer(yy, c), self.base + zs - 1, y_peer)

        def c_copy(self, yy, cc, other):
            return far_w(self.layer(yy, cc), self.layer(yy, cc), self.base + zs + other, c_peer)

        def relay(self, *following):
            self.z_wait()
            for other in following:
                other.z_start()
            self.y_copy(y).start()
            self.c_copy(y, c, 0).start()

        def relay_y(self):
            self.y_copy(1 - y).wait_recv()
            self.c_copy(1 - y, c, 1).start()

        def finish(self):
            self.c_copy(y, 1 - c, 0).wait_recv()
            self.c_copy(1 - y, 1 - c, 1).wait_recv()

        def sent(self):
            for dz in range(1, zs):
                self.z_copy(dz).wait_send()
            self.y_copy(y).wait_send()
            self.c_copy(y, c, 0).wait_send()
            self.c_copy(1 - y, c, 1).wait_send()

    class GatherHalf(Gather):
        def __init__(self, ref, r, columns, others, base, own):
            super().__init__(ref, r, columns, base, own)
            self.others = others

        def x_copy(self, yy, columns, other):
            block = self.layer(yy, c, columns)
            return far_w(block, block, self.base + zs + 2 + other, x_peer)

        def c_other(self, yy, cc, other):
            block = self.layer(yy, cc, self.others)
            return far_w(block, block, self.base + zs + 4 + other, c_peer)

        def push_x(self):
            self.x_copy(y, self.columns, 0).start()

        def relay_y(self):
            super().relay_y()
            self.x_copy(1 - y, self.columns, 1).start()

        def relay_x(self):
            self.x_copy(y, self.others, 0).wait_recv()
            self.c_other(y, c, 0).start()
            self.x_copy(1 - y, self.others, 1).wait_recv()
            self.c_other(1 - y, c, 1).start()

        def finish(self):
            super().finish()
            self.c_other(y, 1 - c, 0).wait_recv()
            self.c_other(1 - y, 1 - c, 1).wait_recv()

        def sent(self):
            super().sent()
            self.x_copy(y, self.columns, 0).wait_send()
            self.x_copy(1 - y, self.columns, 1).wait_send()
            self.c_other(y, c, 0).wait_send()
            self.c_other(1 - y, c, 1).wait_send()

    steps = zs + 2
    base_q = number.take(pairs * steps)

    def gather_q(p):
        return Gather(wq, rq, pl.ds(pl.multiple_of(p * local, 128), local), base_q + p * steps)

    gather_o = Gather(wo, rq, pl.ds(0, width), number.take(steps), own_o)
    base_gu = number.take(tiles * steps)

    def tile_lanes(t):
        return pl.ds(pl.multiple_of(t * tile, 128), tile)

    def turn(i, zz):
        return lax.rem(zz + i + 1, zs)

    def gather_u(i):
        return Gather(
            wu, rq, tile_lanes(turn(i, z)), base_gu + i * steps, own_u,
            lambda dz: tile_lanes(turn(i, lax.rem(z + dz, zs))),
        )

    cuts = local // 128
    base_gd = number.take(cuts * (zs + 6))

    def gather_d(i):
        mine = pl.ds(pl.multiple_of(s * local + i * 128, 128), 128)
        others = pl.ds(pl.multiple_of((1 - s) * local + i * 128, 128), 128)
        return GatherHalf(wd, rd, mine, others, base_gd + i * (zs + 6), own_d)

    near_q = []
    for p in range(pairs):
        for part in range(3):
            start = pl.multiple_of(part * width + s * local + p * 128, 128)
            near_q.append(
                pltpu.make_async_copy(
                    own_q.at[:, pl.ds(start, 128)],
                    wq.at[z, block_rows(rq, y, c), pl.ds(p * local + part * 128, 128)],
                    near_sem.at[local_number.take(1)],
                )
            )
    near_rest = []
    half = pl.ds(pl.multiple_of(s * local, 128), local)
    for own, there in (
        (own_o, wo.at[z, block_rows(rq, y, c), :]),
        (own_u, wu.at[z, block_rows(rq, y, c), :]),
        (own_d.at[:, half], wd.at[z, block_rows(rd, y, c), half]),
    ):
        near_rest.append(
            pltpu.make_async_copy(own, there, near_sem.at[local_number.take(1)])
        )
    near_cot = pltpu.make_async_copy(cot, gout, near_sem.at[local_number.take(1)])
    near_tok = pltpu.make_async_copy(tok_own, tok, near_sem.at[local_number.take(1)])
    for copy in near_q + [near_tok] + near_rest + [near_cot]:
        copy.start()

    base_e = number.take(zs + 1)
    for dz in range(1, zs):
        far(table, e_z.at[dz - 1], base_e + dz - 1, z_peers[dz - 1]).start()
    send_tok = far(tok_own, tok_far, number.take(1), x_peer)
    send_tok.start()
    for copy in near_q:
        copy.wait()
    for p in range(pairs):
        gather_q(p).z_start()

    for dz in range(1, zs):
        far(table, e_z.at[dz - 1], base_e + dz - 1, z_peers[dz - 1]).wait_recv()
    total = table[...].astype(F32)
    for dz in range(1, zs):
        total = total + e_z[dz - 1].astype(F32)
    e_own[0] = total.astype(BF)
    y_table = far(e_own.at[0], e_y, base_e + zs - 1, y_peer)
    y_table.start()
    gather_q(0).relay(gather_o)

    ends = []
    end = jnp.int32(0)
    for j in range(lengths.shape[1]):
        end = end + lengths[0, j]
        ends.append(end)
    position = lax.broadcasted_iota(jnp.int32, (1, group), 1)
    start = jnp.zeros((1, group), jnp.int32)
    for end in ends[:-1]:
        start = jnp.where(position >= end, end, start)
    lower[...] = start
    last_valid = ends[-2]

    y_table.wait_recv()
    total = total + e_y[...].astype(F32)
    e_own[1] = total.astype(BF)
    c_table = far(e_own.at[1], e_c, base_e + zs, c_peer)
    c_table.start()
    gather_q(1).relay(gather_d(0))
    c_table.wait_recv()
    total = total + e_c[...].astype(F32)
    for i in range(TABLE):
        vec[i] = total[i : i + 1, :]

    def first_norm(source, at):
        def body(i):
            x = source[pl.ds(pl.multiple_of(i * 128, 128), 128), :].astype(F32)
            scaled, unused = normed(x)
            value = (scaled * vec[GAIN_1] + vec[SHIFT_1]).astype(BF)
            there = pl.ds(pl.multiple_of(at + i * 128, 128), 128)
            first[there, :] = value
            first_t[:, there] = value.T

        loop(rows // 128, body)

    near_tok.wait()
    first_norm(tok, s * rows)

    base_mixed = number.take(pairs)
    near_mixed = local_number.take(pairs)

    def lanes(p, part):
        return pl.ds(pl.multiple_of(p * local + part * 128, 128), 128)

    def send_mixed(p):
        there = pl.ds(pl.multiple_of(s * local + p * 128, 128), 128)
        here = pl.ds(pl.multiple_of(p * 128, 128), 128)
        away = pl.ds(pl.multiple_of((1 - s) * rows, 128), rows)
        return far(mixed_near.at[away, here], mixed.at[:, there], base_mixed + p, x_peer)

    def keep_mixed(p):
        there = pl.ds(pl.multiple_of(s * local + p * 128, 128), 128)
        here = pl.ds(pl.multiple_of(p * 128, 128), 128)
        stay = pl.ds(pl.multiple_of(s * rows, 128), rows)
        return pltpu.make_async_copy(
            mixed_near.at[stay, here], mixed.at[:, there], near_sem.at[near_mixed + p]
        )

    side = 256
    blocks = group // side
    key_at = lax.broadcasted_iota(jnp.int32, (side, side), 0)
    query_at = lax.broadcasted_iota(jnp.int32, (side, side), 1)
    lane = lax.broadcasted_iota(jnp.int32, (side, 128), 1)

    def head_lanes(value, h):
        inside = (lane >= h * HEAD_DIM) & (lane < h * HEAD_DIM + HEAD_DIM)
        return jnp.where(inside, value, 0.0).astype(BF)

    def scores(p, keys_block, query, qi, j):
        raw = mul_nt(keys_block, query)
        ok = key_at + j * side >= lower[:, qi * side : (qi + 1) * side]
        if j == qi:
            ok = ok & (key_at <= query_at)
        return jnp.where(ok, raw, MASKED)

    scale = HEAD_DIM ** (-0.5)

    def pass_on(k):
        @pl.when(k == 0)
        def _():
            gather_o.relay(gather_d(2))

        @pl.when(k == 2)
        def _():
            gather_d(0).relay(gather_u(0))
            gather_d(0).push_x()
            gather_o.relay_y()

        @pl.when(k == 3)
        def _():
            gather_d(1).relay(gather_u(1))
            gather_d(1).push_x()

        @pl.when(k == 4)
        def _():
            gather_d(2).relay(gather_u(2))

    def attend(p):
        def head(h):
            half = pl.ds(pl.multiple_of(h * HEAD_DIM, HEAD_DIM), HEAD_DIM)
            for qi in range(blocks):
                query = head_lanes(
                    qkv[qi * side : (qi + 1) * side, lanes(p, 0)].astype(F32) * scale, h
                )
                raw = []
                top = None
                for j in range(qi + 1):
                    block = scores(p, qkv[j * side : (j + 1) * side, lanes(p, 1)], query, qi, j)
                    raw.append(block)
                    high = jnp.max(block, axis=0, keepdims=True)
                    top = high if top is None else jnp.maximum(top, high)
                amount = jnp.zeros((1, side), F32)
                gathered = jnp.zeros((HEAD_DIM, side), F32)
                for j in range(qi + 1):
                    weight = jnp.exp(raw[j] - top)
                    amount = amount + column_sum(weight)
                    gathered = gathered + mul(
                        v_t[p, half, j * side : (j + 1) * side], weight.astype(BF)
                    )
                o_t[half, qi * side : (qi + 1) * side] = gathered / amount
                lse[p, h, :, qi * side : (qi + 1) * side] = top + jnp.log(amount)
            pass_on(p * 2 + h)

        loop(2, head)
        here = pl.ds(pl.multiple_of(p * 128, 128), 128)
        for qi in range(blocks):
            at = slice(qi * side, (qi + 1) * side)
            mixed_near[at, here] = o_t[:, at].T.astype(BF)

    def project(p, at_row):
        zero = jnp.zeros((1, 128), F32)
        there = pl.ds(pl.multiple_of(s * local + p * 128, 128), 128)
        bias = jnp.concatenate([vec[BIAS_Q, :, there], zero, vec[BIAS_V, :, there]], axis=1)
        weight = flat(wq[:, :, pl.ds(pl.multiple_of(p * local, 128), local)])

        def body(i):
            at = pl.ds(pl.multiple_of(at_row + i * side, side), side)
            value = (mul(first[at, :], weight) + bias).astype(BF)
            qkv[at, pl.ds(pl.multiple_of(p * local, 128), local)] = value
            k_t[p, :, at] = value[:, 128:256].T
            v_t[p, :, at] = value[:, 256:384].T

        loop(rows // side, body)

    gather_q(0).relay_y()
    gather_q(2).relay(gather_d(1))
    gather_q(0).finish()
    project(0, s * rows)
    gather_q(1).relay_y()
    for copy in near_rest:
        copy.wait()
    gather_q(2).relay_y()
    send_tok.wait_recv()
    first_norm(tok_far, (1 - s) * rows)

    def pair_forward(p):
        @pl.when(p > 0)
        def _():
            gather_q(p).finish()
            project(p, s * rows)

        project(p, (1 - s) * rows)
        attend(p)
        send_mixed(p).start()
        keep_mixed(p).start()

    loop(pairs, pair_forward)
    gather_d(0).relay_y()
    gather_d(1).relay_y()
    gather_d(2).push_x()
    gather_u(0).relay(gather_u(3))
    gather_d(2).relay_y()

    gather_o.finish()
    near_cot.wait()
    for p in range(pairs):
        keep_mixed(p).wait()
    for p in range(pairs):
        far(
            mixed_near.at[pl.ds(0, rows), pl.ds(0, 128)],
            mixed.at[:, pl.ds(pl.multiple_of((1 - s) * local + p * 128, 128), 128)],
            base_mixed + p, x_peer,
        ).wait_recv()

    def project_out(i):
        at = pl.ds(pl.multiple_of(i * 128, 128), 128)
        near = mixed[at, :]
        mixed_t[:, at] = near.T
        value = tok[at, :].astype(F32) + mul(near, flat(wo[...])) + vec[BIAS_OUT]
        middle[at, :] = value
        scaled, unused = normed(value)
        rounded = (scaled * vec[GAIN_2] + vec[SHIFT_2]).astype(BF)
        second[at, :] = rounded
        second_t[:, at] = rounded.T
        spot = s * rows + i * 128 + lax.broadcasted_iota(jnp.int32, (128, width), 0)
        gout[at, :] = jnp.where(spot < last_valid, gout[at, :].astype(F32), 0.0).astype(BF)

    loop(rows // 128, project_out)
    for p in range(pairs):
        send_mixed(p).wait_send()
    gather_d(0).relay_x()
    gather_u(1).relay()
    gather_u(0).relay_y()


    base_sib = number.take(tiles * 2)
    base_dx = number.take(tiles * 2)
    base_zd = number.take(zs - 1)
    base_xs = number.take(1)
    mine = pl.ds(pl.multiple_of(s * local, 128), local)
    others = pl.ds(pl.multiple_of((1 - s) * local, 128), local)

    def rows_y(r, yy):
        return pl.ds(pl.multiple_of(yy * r, r), r)

    def sib_d(t, yy):
        return far_g(
            gwd.at[t, block_rows(rd, yy, 1 - c), :], r1_d.at[t, rows_y(rd, yy), :],
            base_sib + t * 2 + yy, c_peer,
        )

    def sib_start_d(t):
        for yy in range(2):
            sib_d(t, yy).start()

    def x_d(t):
        return far_g(r1_d.at[t, :, others], rx_d.at[t], base_dx + t * 2, x_peer)

    def x_start_d(t):
        for yy in range(2):
            sib_d(t, yy).wait_recv()
            at = rows_y(rd, yy)
            r1_d[t, at, :] = (
                r1_d[t, at, :].astype(F32) + gwd[t, block_rows(rd, yy, c), :].astype(F32)
            ).astype(BF)
        x_d(t).start()

    def y_d(t):
        return far_g(rx_d.at[t, rows_y(rd, 1 - y), :], ry_d.at[t], base_dx + t * 2 + 1, y_peer)

    def y_start_d(t):
        x_d(t).wait_recv()
        rx_d[t] = (rx_d[t].astype(F32) + r1_d[t, :, mine].astype(F32)).astype(BF)
        y_d(t).start()

    def z_d(t, dz):
        return far_g(ry_d.at[t], rz_d.at[dz - 1], base_zd + dz - 1, (t * 4 + y * 2 + c, s))

    def z_start_d(t):
        y_d(t).wait_recv()
        ry_d[t] = (ry_d[t].astype(F32) + rx_d[t, rows_y(rd, y), :].astype(F32)).astype(BF)
        dz = lax.rem(t + zs - z, zs)

        @pl.when(dz > 0)
        def _():
            z_d(t, dz).start()

    class Pooled:
        def __init__(self, ref, start, span, parts, base):
            self.ref, self.base = ref, base
            self.r1, self.rx, self.ry, self.rz, self.r5 = parts
            half = span // 2
            self.full = pl.ds(pl.multiple_of(start, 128), span)
            self.mine = pl.ds(pl.multiple_of(start + s * half, 128), half)
            self.others = pl.ds(pl.multiple_of(start + (1 - s) * half, 128), half)
            self.narrow = pl.ds(pl.multiple_of((start - early * span) // 2, 128), half)

        def sib(self, yy):
            return far_g(
                self.ref.at[:, block_rows(rq, yy, 1 - c), self.full],
                self.r1.at[:, rows_y(rq, yy), self.full], self.base + yy, c_peer,
            )

        def sib_start(self):
            for yy in range(2):
                self.sib(yy).start()

        def along_x(self):
            return far_g(
                self.r1.at[:, :, self.others], self.rx.at[:, :, self.narrow], self.base + 2, x_peer
            )

        def x_start(self):
            for yy in range(2):
                self.sib(yy).wait_recv()
                at = rows_y(rq, yy)
                for zz in range(zs):
                    self.r1[zz, at, self.full] = (
                        self.r1[zz, at, self.full].astype(F32)
                        + self.ref[zz, block_rows(rq, yy, c), self.full].astype(F32)
                    ).astype(BF)
            self.along_x().start()

        def along_y(self):
            return far_g(
                self.rx.at[:, rows_y(rq, 1 - y), self.narrow], self.ry.at[:, :, self.narrow],
                self.base + 3, y_peer,
            )

        def y_start(self):
            self.along_x().wait_recv()
            for zz in range(zs):
                self.rx[zz, :, self.narrow] = (
                    self.rx[zz, :, self.narrow].astype(F32)
                    + self.r1[zz, :, self.mine].astype(F32)
                ).astype(BF)
            self.along_y().start()

        def along_z(self, dz):
            return far_g(
                self.ry.at[lax.rem(z + dz, zs), :, self.narrow],
                self.rz.at[dz - 1, :, self.narrow], self.base + 3 + dz, z_peers[dz - 1],
            )

        def z_start(self):
            self.along_y().wait_recv()
            at = rows_y(rq, y)
            for zz in range(zs):
                self.ry[zz, :, self.narrow] = (
                    self.ry[zz, :, self.narrow].astype(F32)
                    + self.rx[zz, at, self.narrow].astype(F32)
                ).astype(BF)
            for dz in range(1, zs):
                self.along_z(dz).start()

        def swap(self, half):
            block = self.r5.at[half, :, self.narrow]
            return far_g(block, block, self.base + 3 + zs, x_peer)

        def finish(self):
            total = self.ry[z, :, self.narrow].astype(F32)
            for dz in range(1, zs):
                self.along_z(dz).wait_recv()
                total = total + self.rz[dz - 1, :, self.narrow].astype(F32)
            self.r5[s, :, self.narrow] = total.astype(BF)
            self.swap(s).start()

        def sent(self):
            for yy in range(2):
                self.sib(yy).wait_send()
            self.along_x().wait_send()
            self.along_y().wait_send()
            for dz in range(1, zs):
                self.along_z(dz).wait_send()
            self.swap(s).wait_send()

    class Spread:
        def __init__(self, ref, columns, r1, r2, r3, base):
            self.ref, self.columns, self.r1, self.r2, self.r3 = ref, columns, r1, r2, r3
            self.base = base

        def sib(self, yy):
            return far_g(
                self.ref.at[:, block_rows(rq, yy, 1 - c), self.columns],
                self.r1.at[:, pl.ds(pl.multiple_of(yy * rq, rq), rq), self.columns],
                self.base + yy, c_peer,
            )

        def sib_start(self):
            self.sib(1 - y).start()
            self.sib(y).start()

        def along_y(self):
            return far_g(
                self.r1.at[:, pl.ds(pl.multiple_of((1 - y) * rq, rq), rq), self.columns],
                self.r2.at[:, :, self.columns], self.base + 2, y_peer,
            )

        def y_start(self):
            self.sib(1 - y).wait_recv()
            at = pl.ds(pl.multiple_of((1 - y) * rq, rq), rq)
            for zz in range(zs):
                self.r1[zz, at, self.columns] = (
                    self.r1[zz, at, self.columns].astype(F32)
                    + self.ref[zz, block_rows(rq, 1 - y, c), self.columns].astype(F32)
                ).astype(BF)
            self.along_y().start()

        def along_z(self, dz):
            return far_g(
                self.r2.at[lax.rem(z + dz, zs), :, self.columns],
                self.r3.at[dz - 1, :, self.columns], self.base + 2 + dz, z_peers[dz - 1],
            )

        def z_start(self):
            self.sib(y).wait_recv()
            self.along_y().wait_recv()
            at = pl.ds(pl.multiple_of(y * rq, rq), rq)
            for zz in range(zs):
                self.r2[zz, :, self.columns] = (
                    self.r2[zz, :, self.columns].astype(F32)
                    + self.r1[zz, at, self.columns].astype(F32)
                    + self.ref[zz, block_rows(rq, y, c), self.columns].astype(F32)
                ).astype(BF)
            for dz in range(1, zs):
                self.along_z(dz).start()

        def z_finish(self):
            total = self.r2[z, :, self.columns].astype(F32)
            for dz in range(1, zs):
                self.along_z(dz).wait_recv()
                total = total + self.r3[dz - 1, :, self.columns].astype(F32)
            return total

        def sent(self):
            self.sib(0).wait_send()
            self.sib(1).wait_send()
            self.along_y().wait_send()
            for dz in range(1, zs):
                self.along_z(dz).wait_send()

    def swap(parts, columns, slot):
        return far_g(parts.at[0, :, columns], parts.at[1, :, columns], slot, x_peer)

    early = tiles // 2
    spread_steps = zs + 2
    base_su = number.take(early * (spread_steps + 1))

    def sum_e(t):
        return Spread(
            wu, tile_lanes(t), r1_u, r2_u, r3_u, base_su + t * (spread_steps + 1)
        )

    def swap_e(t):
        return swap(r4_u, tile_lanes(t), base_su + t * (spread_steps + 1) + spread_steps)

    def finish_e(t):
        r4_u[0, :, tile_lanes(t)] = sum_e(t).z_finish().astype(BF)
        swap_e(t).start()

    whole = pl.ds(0, width)
    sum_o = Spread(wo, whole, r1_o, r2_o, r3_o, number.take(spread_steps))
    swap_o = swap(r4_o, whole, number.take(1))

    def finish_o():
        r4_o[0] = sum_o.z_finish().astype(BF)
        swap_o.start()

    pooled_steps = zs + 4
    base_pu = number.take(tiles * pooled_steps)

    def sum_u(t):
        return Pooled(wu, t * tile, tile, (r1_u, rx_u, ry_u, rz_u, r5_u), base_pu + t * pooled_steps)

    def pass_up(k):
        @pl.when(k == 0)
        def _():
            gather_d(1).relay_x()

        @pl.when(k == 1)
        def _():
            gather_u(2).relay()
            gather_u(1).relay_y()

        @pl.when(k == 2)
        def _():
            x_start_d(turn(0, z))

        @pl.when(k == 3)
        def _():
            gather_u(3).relay()
            gather_u(2).relay_y()

        @pl.when(k == 4)
        def _():
            gather_d(2).relay_x()
            x_start_d(turn(1, z))

        @pl.when(k == 5)
        def _():
            gather_u(3).relay_y()

        @pl.when(k == 6)
        def _():
            x_start_d(turn(2, z))

    def feed(i):
        t = turn(i, z)
        gather_u(i).finish()
        at = tile_lanes(t)
        pre = mul(second[...], flat(wu[:, :, at])) + vec[BIAS_UP + t]
        square = pre * pre
        bent = 0.5 * jnp.tanh(pre * (SLOPE + (SLOPE * CUBIC) * square)) + 0.5
        value = pre * bent
        bend = bent + value * (1.0 - bent) * (2.0 * SLOPE + (6.0 * SLOPE * CUBIC) * square)
        rounded = value.astype(BF)
        hidden[:, at] = rounded
        hidden_t[...] = rounded.T
        slope[:, at] = bend.astype(BF)
        pass_up(i * 2)
        gwd[t] = mul(hidden_t[...], gout[...]).astype(BF)
        sib_start_d(t)
        pass_up(i * 2 + 1)

    loop(tiles, feed)
    y_start_d(turn(0, z))
    for i in range(cuts):
        gather_d(i).finish()

    def slopes_back(t):
        at = tile_lanes(t)
        grad = (mul_nt(gout[...], wd[t]) * slope[:, at].astype(F32)).astype(BF)
        slope[:, at] = grad
        gvec[BIAS_UP + t] = column_sum(grad.astype(F32))

    loop(tiles, slopes_back)
    y_start_d(turn(1, z))
    z_start_d(turn(0, z))

    def grow(i):
        at = pl.ds(pl.multiple_of(i * side, side), side)
        gtok[at, :] = mul_nt(slope[at, :], flat(wu[...]))

    loop(rows // side, grow)

    for row in (BIAS_Q, BIAS_V, BIAS_OUT, BIAS_DOWN, GAIN_1, SHIFT_1, GAIN_2, SHIFT_2):
        gvec[row] = jnp.zeros((1, width), F32)
    gattn = mixed
    gmix = second

    def middle_back(i):
        at = pl.ds(pl.multiple_of(i * 128, 128), 128)
        grad = gtok[at, :]
        scaled, inverse = normed(middle[at, :])
        ahead = gout[at, :].astype(F32)
        gvec[GAIN_2] += column_sum(grad * scaled)
        gvec[SHIFT_2] += column_sum(grad)
        gvec[BIAS_DOWN] += column_sum(ahead)
        total = ahead + normed_back(grad, scaled, inverse, vec[GAIN_2])
        gtok[at, :] = total
        rounded = total.astype(BF)
        gattn[at, :] = rounded
        gvec[BIAS_OUT] += column_sum(rounded.astype(F32))
        gmix[at, :] = mul_nt(rounded, flat(wo[...])).astype(BF)

    loop(rows // 128, middle_back)

    class Vectors:
        def __init__(self, first_row, count, base):
            self.rows, self.base = range(first_row, first_row + count), base
            self.at = pl.ds(first_row, count)

        def copy(self, source, there, slot, device):
            return far(source.at[self.at], there.at[self.at], self.base + slot, device)

        def along_z(self, dz):
            return self.copy(gvec, v_z.at[dz - 1], dz - 1, z_peers[dz - 1])

        def step(self, k):
            there, device = ((v_y, y_peer), (v_c, c_peer), (v_x, x_peer))[k]
            return self.copy(v_sum.at[k], there, zs - 1 + k, device)

        def z_start(self):
            for dz in range(1, zs):
                self.along_z(dz).start()

        def y_start(self):
            for dz in range(1, zs):
                self.along_z(dz).wait_recv()
            for i in self.rows:
                total = gvec[i]
                for dz in range(1, zs):
                    total = total + v_z[dz - 1, i]
                v_sum[0, i] = total
            self.step(0).start()

        def next_start(self, k):
            self.step(k - 1).wait_recv()
            there = (v_y, v_c)[k - 1]
            v_sum[k, self.at] = v_sum[k - 1, self.at] + there[self.at]
            self.step(k).start()

        def finish(self):
            self.step(2).wait_recv()
            out_v[self.at] = v_sum[2, self.at] + v_x[self.at]

        def sent(self):
            for dz in range(1, zs):
                self.along_z(dz).wait_send()
            for k in range(3):
                self.step(k).wait_send()

    late_rows = Vectors(BIAS_Q, 4, number.take(zs + 2))
    early_rows = Vectors(BIAS_OUT, 4 + tiles, number.take(zs + 2))

    base_gmix = number.take(pairs)
    near_gmix = local_number.take(1)
    here_rows = pl.ds(pl.multiple_of(s * rows, 128), rows)
    there_rows = pl.ds(pl.multiple_of((1 - s) * rows, 128), rows)

    def send_gmix(p):
        lanes_p = pl.ds(pl.multiple_of((1 - s) * local + p * 128, 128), 128)
        at = pl.ds(pl.multiple_of(p * 128, 128), 128)
        return far(gmix.at[:, lanes_p], mixed_near.at[here_rows, at], base_gmix + p, x_peer)

    def take_gmix(p):
        at = pl.ds(pl.multiple_of(p * 128, 128), 128)
        return far(gmix.at[:, pl.ds(0, 128)], mixed_near.at[there_rows, at], base_gmix + p, x_peer)

    keep_gmix = pltpu.make_async_copy(
        gmix.at[:, mine], mixed_near.at[here_rows, :], near_sem.at[near_gmix]
    )
    send_gmix(0).start()
    keep_gmix.start()
    x_start_d(z)
    for p in range(1, pairs):
        send_gmix(p).start()
    early_rows.z_start()

    gather_o.sent()

    wo[...] = mul(mixed_t[...], gattn[...]).astype(BF).reshape(zs, 4 * rq, width)
    y_start_d(turn(2, z))
    z_start_d(turn(1, z))
    for t in range(tiles):
        gather_u(t).sent()

    base_sq = number.take(pairs * spread_steps)

    def sum_q(p):
        return Spread(
            gwq, pl.ds(pl.multiple_of(p * local, 128), local), r1_q, r2_q, r3_q,
            base_sq + p * spread_steps,
        )

    sum_o.sib_start()

    def weigh_up_tile(t):
        at = tile_lanes(t)
        wu[:, :, at] = mul(second_t[...], slope[:, at]).astype(BF).reshape(zs, 4 * rq, tile)
        @pl.when(t < early)
        def _():
            sum_e(t).sib_start()

        @pl.when(t >= early)
        def _():
            sum_u(t).sib_start()

        @pl.when(t == 0)
        def _():
            sum_o.y_start()

        @pl.when(t == 1)
        def _():
            early_rows.y_start()

        @pl.when((t > 0) & (t <= early))
        def _():
            sum_e(t - 1).y_start()

        @pl.when(t > early)
        def _():
            sum_u(t - 1).x_start()

    loop(tiles, weigh_up_tile)
    z_start_d(turn(2, z))
    sum_u(tiles - 1).x_start()
    keep_gmix.wait()

    xd = far_g(r5_d.at[s], r5_d.at[s], base_xs, x_peer)

    def finish_d():
        total = ry_d[z].astype(F32)
        for dz in range(1, zs):
            far_g(ry_d.at[0], rz_d.at[dz - 1], base_zd + dz - 1, z_peers[dz - 1]).wait_recv()
            total = total + rz_d[dz - 1].astype(F32)
        r5_d[s] = total.astype(BF)
        xd.start()

    def serve(k):
        @pl.when(k == 0)
        def _():
            early_rows.next_start(1)
            sum_o.z_start()
            y_start_d(z)

        @pl.when(k == 1)
        def _():
            early_rows.next_start(2)

        @pl.when(k == 2)
        def _():
            sum_e(0).z_start()
            sum_q(0).y_start()

        @pl.when(k == 3)
        def _():
            sum_e(1).z_start()
            finish_o()

        @pl.when(k == 4)
        def _():
            sum_u(2).y_start()
            sum_q(1).y_start()
            z_start_d(z)

        @pl.when(k == 5)
        def _():
            sum_u(3).y_start()
            sum_q(0).z_start()
            finish_e(0)

    per_piece = rows // side

    def dk_at(j):
        return (j // per_piece, slice(j % per_piece * side, (j % per_piece + 1) * side))

    def dv_at(j):
        return dk_at(j + blocks)

    def attend_back(p):
        for i in range(2 * group // rows):
            pieces[i] = jnp.zeros((rows, 128), F32)

        def head(h):
            half = pl.ds(pl.multiple_of(h * HEAD_DIM, HEAD_DIM), HEAD_DIM)
            here = pl.ds(pl.multiple_of(p * 128, 128), 128)
            for qi in range(blocks):
                at = slice(qi * side, (qi + 1) * side)
                query = head_lanes(qkv[at, lanes(p, 0)].astype(F32) * scale, h)
                grad = head_lanes(mixed_near[at, here].astype(F32), h)
                level = lse[p, h, :, at]
                weights, slopes = [], []
                centre = jnp.zeros((1, side), F32)
                for j in range(qi + 1):
                    there = slice(j * side, (j + 1) * side)
                    raw = scores(p, qkv[there, lanes(p, 1)], query, qi, j)
                    weight = jnp.exp(raw - level)
                    slope = mul_nt(qkv[there, lanes(p, 2)], grad)
                    centre = centre + column_sum(weight * slope)
                    weights.append(weight)
                    slopes.append(slope)
                total = jnp.zeros((HEAD_DIM, side), F32)
                for j in range(qi + 1):
                    there = slice(j * side, (j + 1) * side)
                    bend = (weights[j] * (slopes[j] - centre)).astype(BF)
                    pieces[dk_at(j)] += mul(bend, query)
                    pieces[dv_at(j)] += mul(weights[j].astype(BF), grad)
                    total = total + mul(k_t[p, half, there], bend)
                o_t[half, at] = total * scale
            serve(p * 2 + h)

        loop(2, head)
        for qi in range(blocks):
            at = slice(qi * side, (qi + 1) * side)
            qkv[at, lanes(p, 0)] = o_t[:, at].T.astype(BF)
            qkv[at, lanes(p, 1)] = pieces[dk_at(qi)].astype(BF)
            qkv[at, lanes(p, 2)] = pieces[dv_at(qi)].astype(BF)
        own = pl.ds(pl.multiple_of(s * local + p * 128, 128), 128)
        gvec[BIAS_Q, :, own] = column_sum(qkv[:, lanes(p, 0)].astype(F32))
        gvec[BIAS_V, :, own] = column_sum(qkv[:, lanes(p, 2)].astype(F32))
        both = pl.ds(pl.multiple_of(p * local, 128), local)

        gwq[:, :, both] = mul(first_t[...], qkv[:, both]).astype(BF).reshape(zs, 4 * rq, local)

    def pair_back(p):
        take_gmix(p).wait_recv()
        attend_back(p)
        sum_q(p).sib_start()

    loop(pairs, pair_back)

    base_gf = number.take(rows // side)

    def send_gf(i):
        at = pl.ds(pl.multiple_of(i * side, side), side)
        there = pl.ds(pl.multiple_of(rows + i * side, side), side)
        return far(first.at[at, :], first.at[there, :], base_gf + i, x_peer)

    def first_back(i, source, at):
        there = pl.ds(pl.multiple_of(at + i * side, side), side)
        grad = mul_nt(qkv[there, :], flat(wq[...]))
        scaled, unused = normed(source[pl.ds(pl.multiple_of(i * side, side), side), :].astype(F32))
        gvec[GAIN_1] += column_sum(grad * scaled)
        gvec[SHIFT_1] += column_sum(grad)
        return grad

    def away(i):
        grad = first_back(i, tok_far, (1 - s) * rows)
        first[pl.ds(pl.multiple_of(i * side, side), side), :] = grad.astype(BF)
        send_gf(i).start()

    loop(rows // side, away)
    sum_q(2).y_start()

    def stay(i):
        grad = first_back(i, tok, s * rows)
        at = pl.ds(pl.multiple_of(i * side, side), side)
        for j in range(width // 128):
            pieces[j, at, :] = grad[:, j * 128 : (j + 1) * 128]

    loop(rows // side, stay)

    late_rows.z_start()
    sum_u(2).z_start()
    sum_q(1).z_start()
    finish_d()
    sum_u(3).z_start()

    def fall(i):
        at = pl.ds(pl.multiple_of(i * side, side), side)
        middle[at, :] += mul(hidden[at, :], flat(wd[...]))

    loop(rows // side, fall)
    late_rows.y_start()
    sum_q(2).z_start()

    def finish_out(i):
        at = pl.ds(pl.multiple_of(i * 128, 128), 128)
        value = middle[at, :] + vec[BIAS_DOWN]
        spot = s * rows + i * 128 + lax.broadcasted_iota(jnp.int32, (128, width), 0)
        out[at, :] = jnp.where(spot < last_valid, value, 0.0).astype(BF)

    loop(rows // 128, finish_out)
    finish_e(1)
    sum_u(2).finish()

    slot_q = number.take(pairs)

    def swap_q(p, half):
        block = r5_q.at[half, :, pl.ds(p * local, local)]
        return far_g(block, block, slot_q + p, x_peer)

    def finish_q(p):
        r5_q[s, :, p * local : (p + 1) * local] = sum_q(p).z_finish().astype(BF)
        swap_q(p, s).start()

    finish_q(0)
    late_rows.next_start(1)
    finish_q(1)
    late_rows.next_start(2)
    sum_u(3).finish()

    def last(i):
        at = pl.ds(pl.multiple_of(i * side, side), side)
        send_gf(i).wait_recv()
        scaled, inverse = normed(tok[at, :].astype(F32))
        there = pl.ds(pl.multiple_of(rows + i * side, side), side)
        own = jnp.concatenate([pieces[j, at, :] for j in range(width // 128)], axis=1)
        grad = own + first[there, :].astype(F32)
        gtok[at, :] = gtok[at, :] + normed_back(grad, scaled, inverse, vec[GAIN_1])

        @pl.when(i == 0)
        def _():
            finish_q(2)

    loop(rows // side, last)

    late_rows.finish()
    early_rows.finish()
    for i in range(BIAS_UP + tiles, TABLE):
        out_v[i] = jnp.zeros((1, width), F32)
    far_g(r5_d.at[1 - s], r5_d.at[1 - s], base_xs, x_peer).wait_recv()
    for half in range(2):
        out_d[:, half * local : (half + 1) * local] = r5_d[half].astype(F32)
    for t in range(early):
        swap_e(t).wait_recv()
        at = slice(t * tile, (t + 1) * tile)
        out_u[:, at] = r4_u[0, :, at].astype(F32) + r4_u[1, :, at].astype(F32)
    for t in range(early, tiles):
        sum_u(t).swap(1 - s).wait_recv()
        for half in range(2):
            wide = t * tile + half * local
            out_u[:, wide : wide + local] = r5_u[
                half, :, (t - early) * local : (t - early + 1) * local
            ].astype(F32)
    swap_o.wait_recv()
    out_o[...] = r4_o[0].astype(F32) + r4_o[1].astype(F32)
    for p in range(pairs):
        swap_q(p, 1 - s).wait_recv()
    for half in range(2):
        for p in range(pairs):
            for part in range(3):
                at = part * width + half * local + p * 128
                out_q[:, at : at + 128] = r5_q[
                    half, :, p * local + part * 128 : p * local + part * 128 + 128
                ].astype(F32)

    for dz in range(1, zs):
        far(table, e_z.at[dz - 1], base_e + dz - 1, z_peers[dz - 1]).wait_send()
        far_g(ry_d.at[0], rz_d.at[dz - 1], base_zd + dz - 1, z_peers[dz - 1]).wait_send()
    late_rows.sent()
    early_rows.sent()
    for copy in (y_table, c_table, send_tok, xd):
        copy.wait_send()
    for p in range(pairs):
        gather_q(p).sent()
        sum_q(p).sent()
        swap_q(p, s).wait_send()
    sum_o.sent()
    for i in range(cuts):
        gather_d(i).sent()
    for p in range(pairs):
        send_gmix(p).wait_send()
    for t in range(tiles):
        for yy in range(2):
            sib_d(t, yy).wait_send()
        x_d(t).wait_send()
        y_d(t).wait_send()
    for t in range(early):
        sum_e(t).sent()
        swap_e(t).wait_send()
    for t in range(early, tiles):
        sum_u(t).sent()
    swap_o.wait_send()
    for i in range(rows // side):
        send_gf(i).wait_send()


def fused_fits(tokens, lengths, own_q, own_d, shards, pair):
    rows, width = tokens.shape
    return (
        shards == 16
        and pair == 2
        and rows % 256 == 0
        and (width // pair) % 128 == 0
        and own_q.shape[0] % 16 == 0
        and own_d.shape[0] % 64 == 0
        and own_d.shape[0] * shards == 4 * width
    )


def fused(tokens, lengths, w_qkv, w_out, w_up, w_down, small, bias_up, cotangent):
    rows, width = tokens.shape
    shards = lax.axis_size("dp")
    zs = shards // 4
    d = lax.axis_index("dp")
    rq, rd = w_qkv.shape[0], w_down.shape[0]
    deep = 4 * rd * zs
    group = 2 * rows
    local = width // 2
    pairs = local // 128
    lane = jnp.arange(width)
    own = jnp.where(lane // rq == d, jnp.tile(jnp.stack(small), (1, shards)), 0)
    at = jnp.arange(zs)[:, None] * width + lane[None, :]
    up = jnp.where(at // rd == d, jnp.tile(bias_up, (width // rd,))[None, :], 0)
    table = jnp.concatenate([own, up, jnp.zeros((TABLE - 8 - zs, width), own.dtype)], axis=0)

    def vm(shape, kind=BF):
        return pltpu.VMEM(shape, kind)

    scratch = [
        vm((zs, 4 * rq, 3 * local)), vm((zs, 4 * rq, width)), vm((zs, 4 * rq, deep)),
        vm((zs, 4 * rd, width)), vm((zs, 4 * rq, 3 * local)), vm((zs, 4 * rd, width)),
        vm((rows, width)), vm((rows, width)), vm((group, width)), vm((width, group)), vm((group, 3 * local)),
        vm((pairs, 128, group)), vm((pairs, 128, group)), vm((1, group), jnp.int32),
        vm((pairs, 2, 1, group), F32), vm((128, group), F32),
        vm((group, local)), vm((rows, width)), vm((width, rows)), vm((rows, width), F32),
        vm((rows, width)), vm((width, rows)), vm((rows, width)),
        vm((rows, deep)), vm((4 * rd, rows)), vm((rows, deep)),
        vm((width // 128, rows, 128), F32),
        vm((2, TABLE, width)), vm((zs - 1, TABLE, width)), vm((TABLE, width)), vm((TABLE, width)),
        vm((TABLE, 1, width), F32), vm((TABLE, 1, width), F32), vm((zs - 1, TABLE, 1, width), F32),
        vm((TABLE, 1, width), F32), vm((TABLE, 1, width), F32), vm((TABLE, 1, width), F32),
        vm((3, TABLE, 1, width), F32),
        vm((zs, 2 * rd, width)), vm((zs, 2 * rd, local)), vm((zs, rd, local)),
        vm((zs - 1, rd, local)), vm((2, rd, local)),
        vm((zs, 2 * rq, deep)), vm((zs, 2 * rq, deep // 4)), vm((zs, rq, deep // 4)),
        vm((zs - 1, rq, deep // 4)), vm((2, rq, deep // 4)),
        vm((zs, rq, deep // 2)), vm((zs - 1, rq, deep // 2)), vm((2, rq, deep // 2)),
        vm((zs, 2 * rq, width)), vm((zs, rq, width)), vm((zs - 1, rq, width)), vm((2, rq, width)),
        vm((zs, 2 * rq, 3 * local)), vm((zs, rq, 3 * local)), vm((zs - 1, rq, 3 * local)),
        vm((2, rq, 3 * local)),
        pltpu.SemaphoreType.DMA((NEAR_COUNT,)),
        pltpu.SemaphoreType.DMA((FAR_COUNT,)),
        pltpu.SemaphoreType.DMA((FAR_COUNT,)),
    ]
    here = pl.BlockSpec(memory_space=pltpu.VMEM)
    away = pl.BlockSpec(memory_space=pl.ANY)
    return pl.pallas_call(
        fused_kernel,
        out_shape=(
            jax.ShapeDtypeStruct((rows, width), BF),
            jax.ShapeDtypeStruct((rows, width), F32),
            jax.ShapeDtypeStruct((rq, 3 * width), F32),
            jax.ShapeDtypeStruct((rq, width), F32),
            jax.ShapeDtypeStruct((rq, deep), F32),
            jax.ShapeDtypeStruct((rd, width), F32),
            jax.ShapeDtypeStruct((TABLE, 1, width), F32),
        ),
        in_specs=[pl.BlockSpec(memory_space=pltpu.SMEM), here, away, away, away, away, away, away],
        out_specs=[here] * 7,
        scratch_shapes=scratch,
        compiler_params=pltpu.CompilerParams(
            collective_id=0, has_side_effects=True, vmem_limit_bytes=67_043_328
        ),
        name="block",
    )(lengths, table, tokens, cotangent, w_qkv, w_out, w_up, w_down)


def per_device(
    tokens, lengths, w_qkv, w_out, w_up, w_down, bias_q, bias_v, bias_out, bias_up, bias_down,
    gain_one, shift_one, gain_two, shift_two, cotangent,
):
    if not fused_fits(
        tokens, lengths, w_qkv, w_down, lax.axis_size("dp"), lax.axis_size("seq")
    ):
        return per_device_plain(
            tokens, lengths, w_qkv, w_out, w_up, w_down, bias_q, bias_v, bias_out, bias_up,
            bias_down, gain_one, shift_one, gain_two, shift_two, cotangent,
        )
    small = [bias_q, bias_v, gain_one, shift_one, bias_out, bias_down, gain_two, shift_two]
    out, gtok, gq, go, gu, gd, table = fused(
        tokens, lengths, w_qkv, w_out, w_up, w_down, small, bias_up, cotangent
    )
    d = lax.axis_index("dp")
    width = tokens.shape[1]
    rq, rd = w_qkv.shape[0], w_down.shape[0]
    own = lax.dynamic_slice_in_dim(table[:8, 0], d * rq, rq, axis=1)
    up = lax.dynamic_slice_in_dim(
        table[8:].reshape((TABLE - 8) * width), d * rd, rd, axis=0
    )
    return (
        out, gtok, gq, go, gu, gd,
        own[0], own[1], own[4], up, own[5], own[2], own[3], own[6], own[7],
    )


def solution(mesh):
    return jax.shard_map(
        per_device,
        mesh=mesh,
        in_specs=(
            P(("dp", "seq"), None),
            P("dp", None),
            P("dp", None),
            P("dp", None),
            P("dp", None),
            P("dp", None),
            P("dp"),
            P("dp"),
            P("dp"),
            P("dp"),
            P("dp"),
            P("dp"),
            P("dp"),
            P("dp"),
            P("dp"),
            P(("dp", "seq"), None),
        ),
        out_specs=(
            P(("dp", "seq"), None),
            P(("dp", "seq"), None),
            P("dp", None),
            P("dp", None),
            P("dp", None),
            P("dp", None),
            P("dp"),
            P("dp"),
            P("dp"),
            P("dp"),
            P("dp"),
            P("dp"),
            P("dp"),
            P("dp"),
            P("dp"),
        ),
        check_vma=False,
    )
```

```python
import jax
import jax.numpy as jnp
from jax import lax
from jax.experimental import pallas as pl
from jax.experimental.pallas import tpu as pltpu
from jax.sharding import PartitionSpec as P

HEAD_DIM = 64


EPSILON = 1e-05
MASKED = -1e30
SLOPE = 0.7978845608028654
CUBIC = 0.044715


def as_sent(array):
    return jax.tree.map(lambda a: a.astype(jnp.bfloat16) if a.dtype == jnp.float32 else a, array)


def dense(left, right):
    return jnp.dot(left, right, preferred_element_type=jnp.float32)


def dense_left(left, right):
    return lax.dot_general(
        left, right, (((0,), (0,)), ((), ())), preferred_element_type=jnp.float32
    )


def dense_right(left, right):
    return lax.dot_general(
        left, right, (((1,), (1,)), ((), ())), preferred_element_type=jnp.float32
    )


def norm_parts(value):
    mean = jnp.mean(value, axis=-1, keepdims=True)
    centred = value - mean
    inverse = lax.rsqrt(jnp.mean(centred * centred, axis=-1, keepdims=True) + EPSILON)
    return (centred * inverse, inverse)


def norm_back(grad, scaled, inverse, gain):
    shaped = grad * gain
    inner = jnp.mean(shaped * scaled, axis=-1, keepdims=True)
    return inverse * (shaped - jnp.mean(shaped, axis=-1, keepdims=True) - scaled * inner)


def gelu_value(value):
    return 0.5 * value * (1.0 + jnp.tanh(SLOPE * (value + CUBIC * value * value * value)))


def gelu_slope(value):
    bent = jnp.tanh(SLOPE * (value + CUBIC * value * value * value))
    return 0.5 * (1.0 + bent) + 0.5 * value * (1.0 - bent * bent) * SLOPE * (
        1.0 + 3.0 * CUBIC * value * value
    )


def per_device_plain(
    tokens,
    lengths,
    w_qkv,
    w_out,
    w_up,
    w_down,
    bias_q,
    bias_v,
    bias_out,
    bias_up,
    bias_down,
    gain_one,
    shift_one,
    gain_two,
    shift_two,
    cotangent,
):
    width = tokens.shape[1]
    rows = tokens.shape[0]
    pair = lax.axis_size("seq")
    rank = lax.axis_index("seq")
    group = rows * pair
    local = width // pair
    heads = local // HEAD_DIM
    scale = HEAD_DIM ** (-0.5)
    block = 512
    blocks = group // block
    whole = (
        lax.all_gather(w_qkv, "dp", axis=0, tiled=True),
        lax.all_gather(w_out, "dp", axis=0, tiled=True),
        lax.all_gather(w_up, "dp", axis=0, tiled=True),
        lax.all_gather(w_down, "dp", axis=0, tiled=True),
        lax.all_gather(bias_q, "dp", axis=0, tiled=True),
        lax.all_gather(bias_v, "dp", axis=0, tiled=True),
        lax.all_gather(bias_out, "dp", axis=0, tiled=True),
        lax.all_gather(bias_up, "dp", axis=0, tiled=True),
        lax.all_gather(bias_down, "dp", axis=0, tiled=True),
        lax.all_gather(gain_one, "dp", axis=0, tiled=True),
        lax.all_gather(shift_one, "dp", axis=0, tiled=True),
        lax.all_gather(gain_two, "dp", axis=0, tiled=True),
        lax.all_gather(shift_two, "dp", axis=0, tiled=True),
    )
    weight_qkv, weight_out, weight_up, weight_down = whole[0:4]
    add_q, add_v, add_out, add_up, add_down, scale_one, move_one, scale_two, move_two = [
        piece.astype(jnp.float32) for piece in whole[4:]
    ]
    slots = lengths.shape[1]
    position = jnp.arange(group, dtype=jnp.int32)
    ends = jnp.cumsum(lengths[0])
    segment = jnp.sum((position[:, None] >= ends[None, :]).astype(jnp.int32), axis=1)
    own_segment = lax.dynamic_slice_in_dim(segment, rank * rows, rows)
    valid = (own_segment < slots - 1)[:, None]
    inputs = tokens.astype(jnp.float32)
    scaled_one, inverse_one = norm_parts(inputs)
    first = (scaled_one * scale_one + move_one).astype(jnp.bfloat16)
    bias_qkv = jnp.concatenate([add_q, jnp.zeros_like(add_q), add_v])
    qkv = (dense(first, weight_qkv) + bias_qkv).astype(jnp.bfloat16)
    head_side = lax.all_to_all(
        qkv.reshape(rows, 3, pair, local), "seq", split_axis=2, concat_axis=0, tiled=True
    )
    query = head_side[:, 0, 0].reshape(group, heads, HEAD_DIM)
    keys = head_side[:, 1, 0].reshape(group, heads, HEAD_DIM)
    values = head_side[:, 2, 0].reshape(group, heads, HEAD_DIM)

    def block_scores(index):
        start = index * block
        query_rows = lax.dynamic_slice_in_dim(query, start, block)
        raw = (
            jnp.einsum("qhd,khd->hqk", query_rows, keys, preferred_element_type=jnp.float32) * scale
        )
        row_segment = lax.dynamic_slice_in_dim(segment, start, block)
        row_position = lax.dynamic_slice_in_dim(position, start, block)
        allowed = (row_segment[:, None] == segment[None, :]) & (
            position[None, :] <= row_position[:, None]
        )
        return (jnp.where(allowed[None], raw, MASKED), query_rows)

    def attend(index):
        scores, unused = block_scores(index)
        top = jnp.max(scores, axis=-1, keepdims=True)
        weights = jnp.exp(scores - top)
        total = jnp.sum(weights, axis=-1, keepdims=True)
        probs = (weights / total).astype(jnp.bfloat16)
        mixed_rows = jnp.einsum("hqk,khd->qhd", probs, values, preferred_element_type=jnp.float32)
        return (
            mixed_rows.reshape(block, local).astype(jnp.bfloat16),
            (top + jnp.log(total))[:, :, 0],
        )

    mixed_blocks, log_totals = lax.map(attend, jnp.arange(blocks))
    mixed_head = mixed_blocks.reshape(group, 1, local)
    mixed = lax.all_to_all(mixed_head, "seq", split_axis=0, concat_axis=1, tiled=True).reshape(
        rows, width
    )
    middle = inputs + dense(mixed, weight_out) + add_out
    scaled_two, inverse_two = norm_parts(middle)
    second = (scaled_two * scale_two + move_two).astype(jnp.bfloat16)
    pre = dense(second, weight_up) + add_up
    hidden = gelu_value(pre).astype(jnp.bfloat16)
    result = middle + dense(hidden, weight_down) + add_down
    block_out = jnp.where(valid, result, 0.0).astype(jnp.bfloat16)
    grad_out = jnp.where(valid, cotangent, jnp.zeros_like(cotangent))
    grad_weight_down = dense_left(hidden, grad_out)
    grad_add_down = jnp.sum(grad_out.astype(jnp.float32), axis=0)
    grad_pre = (dense_right(grad_out, weight_down) * gelu_slope(pre)).astype(jnp.bfloat16)
    grad_weight_up = dense_left(second, grad_pre)
    grad_add_up = jnp.sum(grad_pre.astype(jnp.float32), axis=0)
    grad_second = dense_right(grad_pre, weight_up)
    grad_scale_two = jnp.sum(grad_second * scaled_two, axis=0)
    grad_move_two = jnp.sum(grad_second, axis=0)
    grad_middle = grad_out.astype(jnp.float32) + norm_back(
        grad_second, scaled_two, inverse_two, scale_two
    )
    grad_attn = grad_middle.astype(jnp.bfloat16)
    grad_weight_out = dense_left(mixed, grad_attn)
    grad_add_out = jnp.sum(grad_attn.astype(jnp.float32), axis=0)
    grad_mixed = dense_right(grad_attn, weight_out).astype(jnp.bfloat16)
    branch_grads = (
        grad_weight_out,
        grad_weight_up,
        grad_weight_down,
        grad_add_out,
        grad_add_up,
        grad_add_down,
        grad_scale_two,
        grad_move_two,
    )
    grad_head = lax.all_to_all(
        grad_mixed.reshape(rows, pair, local), "seq", split_axis=1, concat_axis=0, tiled=True
    )
    grad_head = grad_head.reshape(group, heads, HEAD_DIM)

    def attend_back(carry, index):
        grad_keys, grad_values = carry
        scores, query_rows = block_scores(index)
        probs = jnp.exp(scores - log_totals[index][:, :, None])
        grad_rows = lax.dynamic_slice_in_dim(grad_head, index * block, block)
        grad_probs = jnp.einsum(
            "qhd,khd->hqk", grad_rows, values, preferred_element_type=jnp.float32
        )
        centre = jnp.sum(probs * grad_probs, axis=-1, keepdims=True)
        grad_scores = (probs * (grad_probs - centre)).astype(jnp.bfloat16)
        grad_values = grad_values + jnp.einsum(
            "hqk,qhd->khd",
            probs.astype(jnp.bfloat16),
            grad_rows,
            preferred_element_type=jnp.float32,
        )
        grad_keys = (
            grad_keys
            + jnp.einsum(
                "hqk,qhd->khd", grad_scores, query_rows, preferred_element_type=jnp.float32
            )
            * scale
        )
        grad_query = (
            jnp.einsum("hqk,khd->qhd", grad_scores, keys, preferred_element_type=jnp.float32)
            * scale
        )
        return ((grad_keys, grad_values), grad_query)

    empty = jnp.zeros((group, heads, HEAD_DIM), jnp.float32)
    (grad_keys, grad_values), grad_queries = lax.scan(
        attend_back, (empty, empty), jnp.arange(blocks)
    )
    grad_side = jnp.stack(
        [
            grad_queries.reshape(group, local),
            grad_keys.reshape(group, local),
            grad_values.reshape(group, local),
        ],
        axis=1,
    ).astype(jnp.bfloat16)
    grad_qkv = lax.all_to_all(
        grad_side.reshape(group, 3, 1, local), "seq", split_axis=0, concat_axis=2, tiled=True
    )
    grad_qkv = grad_qkv.reshape(rows, 3 * width)
    grad_weight_qkv = dense_left(first, grad_qkv)
    column_sums = jnp.sum(grad_qkv.astype(jnp.float32), axis=0)
    grad_add_q = column_sums[:width]
    grad_add_v = column_sums[2 * width :]
    grad_first = dense_right(grad_qkv, weight_qkv)
    grad_scale_one = jnp.sum(grad_first * scaled_one, axis=0)
    grad_move_one = jnp.sum(grad_first, axis=0)
    grad_tokens = grad_middle + norm_back(grad_first, scaled_one, inverse_one, scale_one)
    stem_grads = (grad_weight_qkv, grad_add_q, grad_add_v, grad_scale_one, grad_move_one)
    halves = lax.psum_scatter(
        stem_grads + branch_grads, ("dp", "seq"), scatter_dimension=0, tiled=True
    )
    shares = jax.tree.map(
        lambda part, own: part.astype(own.dtype),
        lax.all_gather(as_sent(halves), "seq", axis=0, tiled=True),
        halves,
    )
    stem_shares = shares[0:5]
    branch_shares = shares[5:13]
    return (
        block_out,
        grad_tokens,
        stem_shares[0],
        branch_shares[0],
        branch_shares[1],
        branch_shares[2],
        stem_shares[1],
        stem_shares[2],
        branch_shares[3],
        branch_shares[4],
        branch_shares[5],
        stem_shares[3],
        stem_shares[4],
        branch_shares[6],
        branch_shares[7],
    )


FAR = pl.DeviceIdType.MESH
NT = (((1,), (1,)), ((), ()))
BF = jnp.bfloat16
F32 = jnp.float32


def mul(left, right):
    return jnp.dot(left, right, preferred_element_type=F32)


def mul_nt(left, right):
    return lax.dot_general(left, right, NT, preferred_element_type=F32)


def flat(blocks):
    return blocks.reshape(blocks.shape[0] * blocks.shape[1], blocks.shape[2])


def normed(value):
    width = value.shape[1]
    mean = jnp.sum(value, axis=1, keepdims=True) * (1.0 / width)
    centred = value - mean
    spread = jnp.sum(centred * centred, axis=1, keepdims=True) * (1.0 / width)
    inverse = lax.rsqrt(spread + EPSILON)
    return (centred * inverse, inverse)


def normed_back(grad, scaled, inverse, gain):
    width = grad.shape[1]
    shaped = grad * gain
    inner = jnp.sum(shaped * scaled, axis=1, keepdims=True) * (1.0 / width)
    outer = jnp.sum(shaped, axis=1, keepdims=True) * (1.0 / width)
    return inverse * (shaped - outer - scaled * inner)


def column_sum(value):
    return jnp.sum(value, axis=0, keepdims=True)


class Numbers:
    def __init__(self):
        self.used = 0

    def take(self, count):
        start = self.used
        self.used = start + count
        return start


BIAS_Q, BIAS_V, GAIN_1, SHIFT_1, BIAS_OUT, BIAS_DOWN, GAIN_2, SHIFT_2, BIAS_UP = range(9)
TABLE = 16
FAR_COUNT = 240
NEAR_COUNT = 32


def fused_kernel(
    lengths, table, tok_own, cot, own_q, own_o, own_u, own_d,
    out, gtok, out_q, out_o, out_u, out_d, out_v,
    wq, wo, wu, wd, gwq, gwd,
    tok, tok_far, first, first_t, qkv, k_t, v_t, lower, lse, o_t,
    mixed_near, mixed, mixed_t, middle, second, second_t, gout,
    hidden, hidden_t, slope, pieces,
    e_own, e_z, e_y, e_c, vec, gvec, v_z, v_y, v_c, v_x, v_sum,
    r1_d, rx_d, ry_d, rz_d, r5_d, r1_u, rx_u, ry_u, rz_u, r5_u,
    r2_u, r3_u, r4_u, r1_o, r2_o, r3_o, r4_o, r1_q, r2_q, r3_q, r5_q,
    near_sem, send_sem, recv_sem,
):
    d = lax.axis_index("dp")
    s = lax.axis_index("seq")
    z = lax.div(d, 4)
    y = lax.rem(lax.div(d, 2), 2)
    c = lax.rem(d, 2)
    zs = wq.shape[0]
    rows, width = tok_own.shape
    group = 2 * rows
    local = width // 2
    pairs = local // 128
    rq = width // (4 * zs)
    rd = own_d.shape[0]
    tile = 4 * rd
    tiles = zs
    z_peers = [(lax.rem(z + dz, zs) * 4 + y * 2 + c, s) for dz in range(1, zs)]
    y_peer = (z * 4 + (1 - y) * 2 + c, s)
    c_peer = (z * 4 + y * 2 + (1 - c), s)
    x_peer = (d, 1 - s)
    number = Numbers()
    local_number = Numbers()

    def far(src, dst, slot, device):
        return pltpu.make_async_remote_copy(
            src_ref=src, dst_ref=dst, send_sem=send_sem.at[slot], recv_sem=recv_sem.at[slot],
            device_id=device, device_id_type=FAR,
        )

    far_w, far_g = far, far

    def z_at(dz):
        return lax.rem(z + zs - dz, zs)

    def loop(count, body):
        lax.fori_loop(0, count, lambda i, carry: (body(i), carry)[1], 0)

    def block_rows(r, yy, cc):
        return pl.ds(pl.multiple_of((yy * 2 + cc) * r, r), r)

    barrier = pltpu.get_barrier_semaphore()
    everyone = z_peers + [y_peer, c_peer, x_peer]
    for peer in everyone:
        pl.semaphore_signal(barrier, inc=1, device_id=peer, device_id_type=FAR)
    pl.semaphore_wait(barrier, len(everyone))

    class Gather:
        def __init__(self, ref, r, columns, base, own=None, columns_at=None):
            self.ref, self.r, self.columns, self.base, self.own = ref, r, columns, base, own
            self.columns_at = columns_at

        def part(self, zz, yy, cc):
            return self.ref.at[zz, block_rows(self.r, yy, cc), self.columns]

        def layer(self, yy, cc, columns=None):
            columns = self.columns if columns is None else columns
            return self.ref.at[:, block_rows(self.r, yy, cc), columns]

        def z_copy(self, dz):
            columns = self.columns if self.columns_at is None else self.columns_at(dz)
            there = self.ref.at[z, block_rows(self.r, y, c), columns]
            here = there if self.own is None else self.own.at[:, columns]
            return far_w(here, there, self.base + dz - 1, z_peers[dz - 1])

        def z_start(self):
            for dz in range(1, zs):
                self.z_copy(dz).start()

        def z_wait(self):
            for dz in range(1, zs):
                block = self.part(z_at(dz), y, c)
                far_w(block, block, self.base + dz - 1, z_peers[dz - 1]).wait_recv()

        def y_copy(self, yy):
            return far_w(self.layer(yy, c), self.layer(yy, c), self.base + zs - 1, y_peer)

        def c_copy(self, yy, cc, other):
            return far_w(self.layer(yy, cc), self.layer(yy, cc), self.base + zs + other, c_peer)

        def relay(self, *following):
            self.z_wait()
            for other in following:
                other.z_start()
            self.y_copy(y).start()
            self.c_copy(y, c, 0).start()

        def relay_y(self):
            self.y_copy(1 - y).wait_recv()
            self.c_copy(1 - y, c, 1).start()

        def finish(self):
            self.c_copy(y, 1 - c, 0).wait_recv()
            self.c_copy(1 - y, 1 - c, 1).wait_recv()

        def sent(self):
            for dz in range(1, zs):
                self.z_copy(dz).wait_send()
            self.y_copy(y).wait_send()
            self.c_copy(y, c, 0).wait_send()
            self.c_copy(1 - y, c, 1).wait_send()

    class GatherHalf(Gather):
        def __init__(self, ref, r, columns, others, base, own):
            super().__init__(ref, r, columns, base, own)
            self.others = others

        def x_copy(self, yy, columns, other):
            block = self.layer(yy, c, columns)
            return far_w(block, block, self.base + zs + 2 + other, x_peer)

        def c_other(self, yy, cc, other):
            block = self.layer(yy, cc, self.others)
            return far_w(block, block, self.base + zs + 4 + other, c_peer)

        def push_x(self):
            self.x_copy(y, self.columns, 0).start()

        def relay_y(self):
            super().relay_y()
            self.x_copy(1 - y, self.columns, 1).start()

        def relay_x(self):
            self.x_copy(y, self.others, 0).wait_recv()
            self.c_other(y, c, 0).start()
            self.x_copy(1 - y, self.others, 1).wait_recv()
            self.c_other(1 - y, c, 1).start()

        def finish(self):
            super().finish()
            self.c_other(y, 1 - c, 0).wait_recv()
            self.c_other(1 - y, 1 - c, 1).wait_recv()

        def sent(self):
            super().sent()
            self.x_copy(y, self.columns, 0).wait_send()
            self.x_copy(1 - y, self.columns, 1).wait_send()
            self.c_other(y, c, 0).wait_send()
            self.c_other(1 - y, c, 1).wait_send()

    steps = zs + 2
    base_q = number.take(pairs * steps)

    def gather_q(p):
        return Gather(wq, rq, pl.ds(pl.multiple_of(p * local, 128), local), base_q + p * steps)

    gather_o = Gather(wo, rq, pl.ds(0, width), number.take(steps), own_o)
    base_gu = number.take(tiles * steps)

    def tile_lanes(t):
        return pl.ds(pl.multiple_of(t * tile, 128), tile)

    def turn(i, zz):
        return lax.rem(zz + i + 1, zs)

    def gather_u(i):
        return Gather(
            wu, rq, tile_lanes(turn(i, z)), base_gu + i * steps, own_u,
            lambda dz: tile_lanes(turn(i, lax.rem(z + dz, zs))),
        )

    cuts = local // 128
    base_gd = number.take(cuts * (zs + 6))

    def gather_d(i):
        mine = pl.ds(pl.multiple_of(s * local + i * 128, 128), 128)
        others = pl.ds(pl.multiple_of((1 - s) * local + i * 128, 128), 128)
        return GatherHalf(wd, rd, mine, others, base_gd + i * (zs + 6), own_d)

    near_q = []
    for p in range(pairs):
        for part in range(3):
            start = pl.multiple_of(part * width + s * local + p * 128, 128)
            near_q.append(
                pltpu.make_async_copy(
                    own_q.at[:, pl.ds(start, 128)],
                    wq.at[z, block_rows(rq, y, c), pl.ds(p * local + part * 128, 128)],
                    near_sem.at[local_number.take(1)],
                )
            )
    near_rest = []
    half = pl.ds(pl.multiple_of(s * local, 128), local)
    for own, there in (
        (own_o, wo.at[z, block_rows(rq, y, c), :]),
        (own_u, wu.at[z, block_rows(rq, y, c), :]),
        (own_d.at[:, half], wd.at[z, block_rows(rd, y, c), half]),
    ):
        near_rest.append(
            pltpu.make_async_copy(own, there, near_sem.at[local_number.take(1)])
        )
    near_cot = pltpu.make_async_copy(cot, gout, near_sem.at[local_number.take(1)])
    near_tok = pltpu.make_async_copy(tok_own, tok, near_sem.at[local_number.take(1)])
    for copy in near_q + [near_tok] + near_rest + [near_cot]:
        copy.start()

    base_e = number.take(zs + 1)
    for dz in range(1, zs):
        far(table, e_z.at[dz - 1], base_e + dz - 1, z_peers[dz - 1]).start()
    send_tok = far(tok_own, tok_far, number.take(1), x_peer)
    send_tok.start()
    for copy in near_q:
        copy.wait()
    for p in range(pairs):
        gather_q(p).z_start()

    for dz in range(1, zs):
        far(table, e_z.at[dz - 1], base_e + dz - 1, z_peers[dz - 1]).wait_recv()
    total = table[...].astype(F32)
    for dz in range(1, zs):
        total = total + e_z[dz - 1].astype(F32)
    e_own[0] = total.astype(BF)
    y_table = far(e_own.at[0], e_y, base_e + zs - 1, y_peer)
    y_table.start()
    gather_q(0).relay(gather_o)

    ends = []
    end = jnp.int32(0)
    for j in range(lengths.shape[1]):
        end = end + lengths[0, j]
        ends.append(end)
    position = lax.broadcasted_iota(jnp.int32, (1, group), 1)
    start = jnp.zeros((1, group), jnp.int32)
    for end in ends[:-1]:
        start = jnp.where(position >= end, end, start)
    lower[...] = start
    last_valid = ends[-2]

    y_table.wait_recv()
    total = total + e_y[...].astype(F32)
    e_own[1] = total.astype(BF)
    c_table = far(e_own.at[1], e_c, base_e + zs, c_peer)
    c_table.start()
    gather_q(1).relay(gather_d(0))
    c_table.wait_recv()
    total = total + e_c[...].astype(F32)
    for i in range(TABLE):
        vec[i] = total[i : i + 1, :]

    def first_norm(source, at):
        def body(i):
            x = source[pl.ds(pl.multiple_of(i * 128, 128), 128), :].astype(F32)
            scaled, unused = normed(x)
            value = (scaled * vec[GAIN_1] + vec[SHIFT_1]).astype(BF)
            there = pl.ds(pl.multiple_of(at + i * 128, 128), 128)
            first[there, :] = value
            first_t[:, there] = value.T

        loop(rows // 128, body)

    near_tok.wait()
    first_norm(tok, s * rows)

    base_mixed = number.take(pairs)
    near_mixed = local_number.take(pairs)

    def lanes(p, part):
        return pl.ds(pl.multiple_of(p * local + part * 128, 128), 128)

    def send_mixed(p):
        there = pl.ds(pl.multiple_of(s * local + p * 128, 128), 128)
        here = pl.ds(pl.multiple_of(p * 128, 128), 128)
        away = pl.ds(pl.multiple_of((1 - s) * rows, 128), rows)
        return far(mixed_near.at[away, here], mixed.at[:, there], base_mixed + p, x_peer)

    def keep_mixed(p):
        there = pl.ds(pl.multiple_of(s * local + p * 128, 128), 128)
        here = pl.ds(pl.multiple_of(p * 128, 128), 128)
        stay = pl.ds(pl.multiple_of(s * rows, 128), rows)
        return pltpu.make_async_copy(
            mixed_near.at[stay, here], mixed.at[:, there], near_sem.at[near_mixed + p]
        )

    side = 256
    blocks = group // side
    key_at = lax.broadcasted_iota(jnp.int32, (side, side), 0)
    query_at = lax.broadcasted_iota(jnp.int32, (side, side), 1)
    lane = lax.broadcasted_iota(jnp.int32, (side, 128), 1)

    def head_lanes(value, h):
        inside = (lane >= h * HEAD_DIM) & (lane < h * HEAD_DIM + HEAD_DIM)
        return jnp.where(inside, value, 0.0).astype(BF)

    def scores(p, keys_block, query, qi, j):
        raw = mul_nt(keys_block, query)
        ok = key_at + j * side >= lower[:, qi * side : (qi + 1) * side]
        if j == qi:
            ok = ok & (key_at <= query_at)
        return jnp.where(ok, raw, MASKED)

    scale = HEAD_DIM ** (-0.5)

    def pass_on(k):
        @pl.when(k == 0)
        def _():
            gather_o.relay(gather_d(2))

        @pl.when(k == 2)
        def _():
            gather_d(0).relay(gather_u(0))
            gather_d(0).push_x()
            gather_o.relay_y()

        @pl.when(k == 3)
        def _():
            gather_d(1).relay(gather_u(1))
            gather_d(1).push_x()

        @pl.when(k == 4)
        def _():
            gather_d(2).relay(gather_u(2))

    def attend(p):
        def head(h):
            half = pl.ds(pl.multiple_of(h * HEAD_DIM, HEAD_DIM), HEAD_DIM)
            for qi in range(blocks):
                query = head_lanes(
                    qkv[qi * side : (qi + 1) * side, lanes(p, 0)].astype(F32) * scale, h
                )
                raw = []
                top = None
                for j in range(qi + 1):
                    block = scores(p, qkv[j * side : (j + 1) * side, lanes(p, 1)], query, qi, j)
                    raw.append(block)
                    high = jnp.max(block, axis=0, keepdims=True)
                    top = high if top is None else jnp.maximum(top, high)
                amount = jnp.zeros((1, side), F32)
                gathered = jnp.zeros((HEAD_DIM, side), F32)
                for j in range(qi + 1):
                    weight = jnp.exp(raw[j] - top)
                    amount = amount + column_sum(weight)
                    gathered = gathered + mul(
                        v_t[p, half, j * side : (j + 1) * side], weight.astype(BF)
                    )
                o_t[half, qi * side : (qi + 1) * side] = gathered / amount
                lse[p, h, :, qi * side : (qi + 1) * side] = top + jnp.log(amount)
            pass_on(p * 2 + h)

        loop(2, head)
        here = pl.ds(pl.multiple_of(p * 128, 128), 128)
        for qi in range(blocks):
            at = slice(qi * side, (qi + 1) * side)
            mixed_near[at, here] = o_t[:, at].T.astype(BF)

    def project(p, at_row):
        zero = jnp.zeros((1, 128), F32)
        there = pl.ds(pl.multiple_of(s * local + p * 128, 128), 128)
        bias = jnp.concatenate([vec[BIAS_Q, :, there], zero, vec[BIAS_V, :, there]], axis=1)
        weight = flat(wq[:, :, pl.ds(pl.multiple_of(p * local, 128), local)])

        def body(i):
            at = pl.ds(pl.multiple_of(at_row + i * side, side), side)
            value = (mul(first[at, :], weight) + bias).astype(BF)
            qkv[at, pl.ds(pl.multiple_of(p * local, 128), local)] = value
            k_t[p, :, at] = value[:, 128:256].T
            v_t[p, :, at] = value[:, 256:384].T

        loop(rows // side, body)

    gather_q(0).relay_y()
    gather_q(2).relay(gather_d(1))
    gather_q(0).finish()
    project(0, s * rows)
    gather_q(1).relay_y()
    for copy in near_rest:
        copy.wait()
    gather_q(2).relay_y()
    send_tok.wait_recv()
    first_norm(tok_far, (1 - s) * rows)

    def pair_forward(p):
        @pl.when(p > 0)
        def _():
            gather_q(p).finish()
            project(p, s * rows)

        project(p, (1 - s) * rows)
        attend(p)
        send_mixed(p).start()
        keep_mixed(p).start()

    loop(pairs, pair_forward)
    gather_d(0).relay_y()
    gather_d(1).relay_y()
    gather_d(2).push_x()
    gather_u(0).relay(gather_u(3))
    gather_d(2).relay_y()

    gather_o.finish()
    near_cot.wait()
    for p in range(pairs):
        keep_mixed(p).wait()
    for p in range(pairs):
        far(
            mixed_near.at[pl.ds(0, rows), pl.ds(0, 128)],
            mixed.at[:, pl.ds(pl.multiple_of((1 - s) * local + p * 128, 128), 128)],
            base_mixed + p, x_peer,
        ).wait_recv()

    def project_out(i):
        at = pl.ds(pl.multiple_of(i * 128, 128), 128)
        near = mixed[at, :]
        mixed_t[:, at] = near.T
        value = tok[at, :].astype(F32) + mul(near, flat(wo[...])) + vec[BIAS_OUT]
        middle[at, :] = value
        scaled, unused = normed(value)
        rounded = (scaled * vec[GAIN_2] + vec[SHIFT_2]).astype(BF)
        second[at, :] = rounded
        second_t[:, at] = rounded.T
        spot = s * rows + i * 128 + lax.broadcasted_iota(jnp.int32, (128, width), 0)
        gout[at, :] = jnp.where(spot < last_valid, gout[at, :].astype(F32), 0.0).astype(BF)

    loop(rows // 128, project_out)
    for p in range(pairs):
        send_mixed(p).wait_send()
    gather_d(0).relay_x()
    gather_u(1).relay()
    gather_u(0).relay_y()


    base_sib = number.take(tiles * 2)
    base_dx = number.take(tiles * 2)
    base_zd = number.take(zs - 1)
    base_xs = number.take(1)
    mine = pl.ds(pl.multiple_of(s * local, 128), local)
    others = pl.ds(pl.multiple_of((1 - s) * local, 128), local)

    def rows_y(r, yy):
        return pl.ds(pl.multiple_of(yy * r, r), r)

    def sib_d(t, yy):
        return far_g(
            gwd.at[t, block_rows(rd, yy, 1 - c), :], r1_d.at[t, rows_y(rd, yy), :],
            base_sib + t * 2 + yy, c_peer,
        )

    def sib_start_d(t):
        for yy in range(2):
            sib_d(t, yy).start()

    def x_d(t):
        return far_g(r1_d.at[t, :, others], rx_d.at[t], base_dx + t * 2, x_peer)

    def x_start_d(t):
        for yy in range(2):
            sib_d(t, yy).wait_recv()
            at = rows_y(rd, yy)
            r1_d[t, at, :] = (
                r1_d[t, at, :].astype(F32) + gwd[t, block_rows(rd, yy, c), :].astype(F32)
            ).astype(BF)
        x_d(t).start()

    def y_d(t):
        return far_g(rx_d.at[t, rows_y(rd, 1 - y), :], ry_d.at[t], base_dx + t * 2 + 1, y_peer)

    def y_start_d(t):
        x_d(t).wait_recv()
        rx_d[t] = (rx_d[t].astype(F32) + r1_d[t, :, mine].astype(F32)).astype(BF)
        y_d(t).start()

    def z_d(t, dz):
        return far_g(ry_d.at[t], rz_d.at[dz - 1], base_zd + dz - 1, (t * 4 + y * 2 + c, s))

    def z_start_d(t):
        y_d(t).wait_recv()
        ry_d[t] = (ry_d[t].astype(F32) + rx_d[t, rows_y(rd, y), :].astype(F32)).astype(BF)
        dz = lax.rem(t + zs - z, zs)

        @pl.when(dz > 0)
        def _():
            z_d(t, dz).start()

    class Pooled:
        def __init__(self, ref, start, span, parts, base):
            self.ref, self.base = ref, base
            self.r1, self.rx, self.ry, self.rz, self.r5 = parts
            half = span // 2
            self.full = pl.ds(pl.multiple_of(start, 128), span)
            self.mine = pl.ds(pl.multiple_of(start + s * half, 128), half)
            self.others = pl.ds(pl.multiple_of(start + (1 - s) * half, 128), half)
            self.narrow = pl.ds(pl.multiple_of((start - early * span) // 2, 128), half)

        def sib(self, yy):
            return far_g(
                self.ref.at[:, block_rows(rq, yy, 1 - c), self.full],
                self.r1.at[:, rows_y(rq, yy), self.full], self.base + yy, c_peer,
            )

        def sib_start(self):
            for yy in range(2):
                self.sib(yy).start()

        def along_x(self):
            return far_g(
                self.r1.at[:, :, self.others], self.rx.at[:, :, self.narrow], self.base + 2, x_peer
            )

        def x_start(self):
            for yy in range(2):
                self.sib(yy).wait_recv()
                at = rows_y(rq, yy)
                for zz in range(zs):
                    self.r1[zz, at, self.full] = (
                        self.r1[zz, at, self.full].astype(F32)
                        + self.ref[zz, block_rows(rq, yy, c), self.full].astype(F32)
                    ).astype(BF)
            self.along_x().start()

        def along_y(self):
            return far_g(
                self.rx.at[:, rows_y(rq, 1 - y), self.narrow], self.ry.at[:, :, self.narrow],
                self.base + 3, y_peer,
            )

        def y_start(self):
            self.along_x().wait_recv()
            for zz in range(zs):
                self.rx[zz, :, self.narrow] = (
                    self.rx[zz, :, self.narrow].astype(F32)
                    + self.r1[zz, :, self.mine].astype(F32)
                ).astype(BF)
            self.along_y().start()

        def along_z(self, dz):
            return far_g(
                self.ry.at[lax.rem(z + dz, zs), :, self.narrow],
                self.rz.at[dz - 1, :, self.narrow], self.base + 3 + dz, z_peers[dz - 1],
            )

        def z_start(self):
            self.along_y().wait_recv()
            at = rows_y(rq, y)
            for zz in range(zs):
                self.ry[zz, :, self.narrow] = (
                    self.ry[zz, :, self.narrow].astype(F32)
                    + self.rx[zz, at, self.narrow].astype(F32)
                ).astype(BF)
            for dz in range(1, zs):
                self.along_z(dz).start()

        def swap(self, half):
            block = self.r5.at[half, :, self.narrow]
            return far_g(block, block, self.base + 3 + zs, x_peer)

        def finish(self):
            total = self.ry[z, :, self.narrow].astype(F32)
            for dz in range(1, zs):
                self.along_z(dz).wait_recv()
                total = total + self.rz[dz - 1, :, self.narrow].astype(F32)
            self.r5[s, :, self.narrow] = total.astype(BF)
            self.swap(s).start()

        def sent(self):
            for yy in range(2):
                self.sib(yy).wait_send()
            self.along_x().wait_send()
            self.along_y().wait_send()
            for dz in range(1, zs):
                self.along_z(dz).wait_send()
            self.swap(s).wait_send()

    class Spread:
        def __init__(self, ref, columns, r1, r2, r3, base):
            self.ref, self.columns, self.r1, self.r2, self.r3 = ref, columns, r1, r2, r3
            self.base = base

        def sib(self, yy):
            return far_g(
                self.ref.at[:, block_rows(rq, yy, 1 - c), self.columns],
                self.r1.at[:, pl.ds(pl.multiple_of(yy * rq, rq), rq), self.columns],
                self.base + yy, c_peer,
            )

        def sib_start(self):
            self.sib(1 - y).start()
            self.sib(y).start()

        def along_y(self):
            return far_g(
                self.r1.at[:, pl.ds(pl.multiple_of((1 - y) * rq, rq), rq), self.columns],
                self.r2.at[:, :, self.columns], self.base + 2, y_peer,
            )

        def y_start(self):
            self.sib(1 - y).wait_recv()
            at = pl.ds(pl.multiple_of((1 - y) * rq, rq), rq)
            for zz in range(zs):
                self.r1[zz, at, self.columns] = (
                    self.r1[zz, at, self.columns].astype(F32)
                    + self.ref[zz, block_rows(rq, 1 - y, c), self.columns].astype(F32)
                ).astype(BF)
            self.along_y().start()

        def along_z(self, dz):
            return far_g(
                self.r2.at[lax.rem(z + dz, zs), :, self.columns],
                self.r3.at[dz - 1, :, self.columns], self.base + 2 + dz, z_peers[dz - 1],
            )

        def z_start(self):
            self.sib(y).wait_recv()
            self.along_y().wait_recv()
            at = pl.ds(pl.multiple_of(y * rq, rq), rq)
            for zz in range(zs):
                self.r2[zz, :, self.columns] = (
                    self.r2[zz, :, self.columns].astype(F32)
                    + self.r1[zz, at, self.columns].astype(F32)
                    + self.ref[zz, block_rows(rq, y, c), self.columns].astype(F32)
                ).astype(BF)
            for dz in range(1, zs):
                self.along_z(dz).start()

        def z_finish(self):
            total = self.r2[z, :, self.columns].astype(F32)
            for dz in range(1, zs):
                self.along_z(dz).wait_recv()
                total = total + self.r3[dz - 1, :, self.columns].astype(F32)
            return total

        def sent(self):
            self.sib(0).wait_send()
            self.sib(1).wait_send()
            self.along_y().wait_send()
            for dz in range(1, zs):
                self.along_z(dz).wait_send()

    def swap(parts, columns, slot):
        return far_g(parts.at[0, :, columns], parts.at[1, :, columns], slot, x_peer)

    early = tiles // 2
    spread_steps = zs + 2
    base_su = number.take(early * (spread_steps + 1))

    def sum_e(t):
        return Spread(
            wu, tile_lanes(t), r1_u, r2_u, r3_u, base_su + t * (spread_steps + 1)
        )

    def swap_e(t):
        return swap(r4_u, tile_lanes(t), base_su + t * (spread_steps + 1) + spread_steps)

    def finish_e(t):
        r4_u[0, :, tile_lanes(t)] = sum_e(t).z_finish().astype(BF)
        swap_e(t).start()

    whole = pl.ds(0, width)
    sum_o = Spread(wo, whole, r1_o, r2_o, r3_o, number.take(spread_steps))
    swap_o = swap(r4_o, whole, number.take(1))

    def finish_o():
        r4_o[0] = sum_o.z_finish().astype(BF)
        swap_o.start()

    pooled_steps = zs + 4
    base_pu = number.take(tiles * pooled_steps)

    def sum_u(t):
        return Pooled(wu, t * tile, tile, (r1_u, rx_u, ry_u, rz_u, r5_u), base_pu + t * pooled_steps)

    def pass_up(k):
        @pl.when(k == 0)
        def _():
            gather_d(1).relay_x()

        @pl.when(k == 1)
        def _():
            gather_u(2).relay()
            gather_u(1).relay_y()

        @pl.when(k == 2)
        def _():
            x_start_d(turn(0, z))

        @pl.when(k == 3)
        def _():
            gather_u(3).relay()
            gather_u(2).relay_y()

        @pl.when(k == 4)
        def _():
            gather_d(2).relay_x()
            x_start_d(turn(1, z))

        @pl.when(k == 5)
        def _():
            gather_u(3).relay_y()

        @pl.when(k == 6)
        def _():
            x_start_d(turn(2, z))

    def feed(i):
        t = turn(i, z)
        gather_u(i).finish()
        at = tile_lanes(t)
        pre = mul(second[...], flat(wu[:, :, at])) + vec[BIAS_UP + t]
        square = pre * pre
        bent = 0.5 * jnp.tanh(pre * (SLOPE + (SLOPE * CUBIC) * square)) + 0.5
        value = pre * bent
        bend = bent + value * (1.0 - bent) * (2.0 * SLOPE + (6.0 * SLOPE * CUBIC) * square)
        rounded = value.astype(BF)
        hidden[:, at] = rounded
        hidden_t[...] = rounded.T
        slope[:, at] = bend.astype(BF)
        pass_up(i * 2)
        gwd[t] = mul(hidden_t[...], gout[...]).astype(BF)
        sib_start_d(t)
        pass_up(i * 2 + 1)

    loop(tiles, feed)
    y_start_d(turn(0, z))
    for i in range(cuts):
        gather_d(i).finish()

    def slopes_back(t):
        at = tile_lanes(t)
        grad = (mul_nt(gout[...], wd[t]) * slope[:, at].astype(F32)).astype(BF)
        slope[:, at] = grad
        gvec[BIAS_UP + t] = column_sum(grad.astype(F32))

    loop(tiles, slopes_back)
    y_start_d(turn(1, z))
    z_start_d(turn(0, z))

    def grow(i):
        at = pl.ds(pl.multiple_of(i * side, side), side)
        gtok[at, :] = mul_nt(slope[at, :], flat(wu[...]))

    loop(rows // side, grow)

    for row in (BIAS_Q, BIAS_V, BIAS_OUT, BIAS_DOWN, GAIN_1, SHIFT_1, GAIN_2, SHIFT_2):
        gvec[row] = jnp.zeros((1, width), F32)
    gattn = mixed
    gmix = second

    def middle_back(i):
        at = pl.ds(pl.multiple_of(i * 128, 128), 128)
        grad = gtok[at, :]
        scaled, inverse = normed(middle[at, :])
        ahead = gout[at, :].astype(F32)
        gvec[GAIN_2] += column_sum(grad * scaled)
        gvec[SHIFT_2] += column_sum(grad)
        gvec[BIAS_DOWN] += column_sum(ahead)
        total = ahead + normed_back(grad, scaled, inverse, vec[GAIN_2])
        gtok[at, :] = total
        rounded = total.astype(BF)
        gattn[at, :] = rounded
        gvec[BIAS_OUT] += column_sum(rounded.astype(F32))
        gmix[at, :] = mul_nt(rounded, flat(wo[...])).astype(BF)

    loop(rows // 128, middle_back)

    class Vectors:
        def __init__(self, first_row, count, base):
            self.rows, self.base = range(first_row, first_row + count), base
            self.at = pl.ds(first_row, count)

        def copy(self, source, there, slot, device):
            return far(source.at[self.at], there.at[self.at], self.base + slot, device)

        def along_z(self, dz):
            return self.copy(gvec, v_z.at[dz - 1], dz - 1, z_peers[dz - 1])

        def step(self, k):
            there, device = ((v_y, y_peer), (v_c, c_peer), (v_x, x_peer))[k]
            return self.copy(v_sum.at[k], there, zs - 1 + k, device)

        def z_start(self):
            for dz in range(1, zs):
                self.along_z(dz).start()

        def y_start(self):
            for dz in range(1, zs):
                self.along_z(dz).wait_recv()
            for i in self.rows:
                total = gvec[i]
                for dz in range(1, zs):
                    total = total + v_z[dz - 1, i]
                v_sum[0, i] = total
            self.step(0).start()

        def next_start(self, k):
            self.step(k - 1).wait_recv()
            there = (v_y, v_c)[k - 1]
            v_sum[k, self.at] = v_sum[k - 1, self.at] + there[self.at]
            self.step(k).start()

        def finish(self):
            self.step(2).wait_recv()
            out_v[self.at] = v_sum[2, self.at] + v_x[self.at]

        def sent(self):
            for dz in range(1, zs):
                self.along_z(dz).wait_send()
            for k in range(3):
                self.step(k).wait_send()

    late_rows = Vectors(BIAS_Q, 4, number.take(zs + 2))
    early_rows = Vectors(BIAS_OUT, 4 + tiles, number.take(zs + 2))

    base_gmix = number.take(pairs)
    near_gmix = local_number.take(1)
    here_rows = pl.ds(pl.multiple_of(s * rows, 128), rows)
    there_rows = pl.ds(pl.multiple_of((1 - s) * rows, 128), rows)

    def send_gmix(p):
        lanes_p = pl.ds(pl.multiple_of((1 - s) * local + p * 128, 128), 128)
        at = pl.ds(pl.multiple_of(p * 128, 128), 128)
        return far(gmix.at[:, lanes_p], mixed_near.at[here_rows, at], base_gmix + p, x_peer)

    def take_gmix(p):
        at = pl.ds(pl.multiple_of(p * 128, 128), 128)
        return far(gmix.at[:, pl.ds(0, 128)], mixed_near.at[there_rows, at], base_gmix + p, x_peer)

    keep_gmix = pltpu.make_async_copy(
        gmix.at[:, mine], mixed_near.at[here_rows, :], near_sem.at[near_gmix]
    )
    send_gmix(0).start()
    keep_gmix.start()
    x_start_d(z)
    for p in range(1, pairs):
        send_gmix(p).start()
    early_rows.z_start()

    gather_o.sent()

    wo[...] = mul(mixed_t[...], gattn[...]).astype(BF).reshape(zs, 4 * rq, width)
    y_start_d(turn(2, z))
    z_start_d(turn(1, z))
    for t in range(tiles):
        gather_u(t).sent()

    base_sq = number.take(pairs * spread_steps)

    def sum_q(p):
        return Spread(
            gwq, pl.ds(pl.multiple_of(p * local, 128), local), r1_q, r2_q, r3_q,
            base_sq + p * spread_steps,
        )

    sum_o.sib_start()

    def weigh_up_tile(t):
        at = tile_lanes(t)
        wu[:, :, at] = mul(second_t[...], slope[:, at]).astype(BF).reshape(zs, 4 * rq, tile)
        @pl.when(t < early)
        def _():
            sum_e(t).sib_start()

        @pl.when(t >= early)
        def _():
            sum_u(t).sib_start()

        @pl.when(t == 0)
        def _():
            sum_o.y_start()

        @pl.when(t == 1)
        def _():
            early_rows.y_start()

        @pl.when((t > 0) & (t < early))
        def _():
            sum_e(t - 1).y_start()

        @pl.when(t > early)
        def _():
            sum_u(t - 1).x_start()

    loop(tiles, weigh_up_tile)
    z_start_d(turn(2, z))
    sum_u(tiles - 1).x_start()
    keep_gmix.wait()

    xd = far_g(r5_d.at[s], r5_d.at[s], base_xs, x_peer)

    def finish_d():
        total = ry_d[z].astype(F32)
        for dz in range(1, zs):
            far_g(ry_d.at[0], rz_d.at[dz - 1], base_zd + dz - 1, z_peers[dz - 1]).wait_recv()
            total = total + rz_d[dz - 1].astype(F32)
        r5_d[s] = total.astype(BF)
        xd.start()

    def serve(k):
        @pl.when(k == 0)
        def _():
            early_rows.next_start(1)
            sum_o.z_start()
            y_start_d(z)
            sum_e(early - 1).y_start()

        @pl.when(k == 1)
        def _():
            early_rows.next_start(2)

        @pl.when(k == 2)
        def _():
            z_start_d(z)
            sum_e(0).z_start()
            sum_q(0).y_start()

        @pl.when(k == 3)
        def _():
            finish_o()

        @pl.when(k == 4)
        def _():
            sum_e(early - 1).z_start()
            sum_u(2).y_start()
            sum_q(1).y_start()
            finish_d()

        @pl.when(k == 5)
        def _():
            sum_u(3).y_start()
            sum_q(0).z_start()
            finish_e(0)

    per_piece = rows // side

    def dk_at(j):
        return (j // per_piece, slice(j % per_piece * side, (j % per_piece + 1) * side))

    def dv_at(j):
        return dk_at(j + blocks)

    def attend_back(p):
        for i in range(2 * group // rows):
            pieces[i] = jnp.zeros((rows, 128), F32)

        def head(h):
            half = pl.ds(pl.multiple_of(h * HEAD_DIM, HEAD_DIM), HEAD_DIM)
            here = pl.ds(pl.multiple_of(p * 128, 128), 128)
            for qi in range(blocks):
                at = slice(qi * side, (qi + 1) * side)
                query = head_lanes(qkv[at, lanes(p, 0)].astype(F32) * scale, h)
                grad = head_lanes(mixed_near[at, here].astype(F32), h)
                level = lse[p, h, :, at]
                weights, slopes = [], []
                centre = jnp.zeros((1, side), F32)
                for j in range(qi + 1):
                    there = slice(j * side, (j + 1) * side)
                    raw = scores(p, qkv[there, lanes(p, 1)], query, qi, j)
                    weight = jnp.exp(raw - level)
                    slope = mul_nt(qkv[there, lanes(p, 2)], grad)
                    centre = centre + column_sum(weight * slope)
                    weights.append(weight)
                    slopes.append(slope)
                total = jnp.zeros((HEAD_DIM, side), F32)
                for j in range(qi + 1):
                    there = slice(j * side, (j + 1) * side)
                    bend = (weights[j] * (slopes[j] - centre)).astype(BF)
                    pieces[dk_at(j)] += mul(bend, query)
                    pieces[dv_at(j)] += mul(weights[j].astype(BF), grad)
                    total = total + mul(k_t[p, half, there], bend)
                o_t[half, at] = total * scale
            serve(p * 2 + h)

        loop(2, head)
        for qi in range(blocks):
            at = slice(qi * side, (qi + 1) * side)
            qkv[at, lanes(p, 0)] = o_t[:, at].T.astype(BF)
            qkv[at, lanes(p, 1)] = pieces[dk_at(qi)].astype(BF)
            qkv[at, lanes(p, 2)] = pieces[dv_at(qi)].astype(BF)
        own = pl.ds(pl.multiple_of(s * local + p * 128, 128), 128)
        gvec[BIAS_Q, :, own] = column_sum(qkv[:, lanes(p, 0)].astype(F32))
        gvec[BIAS_V, :, own] = column_sum(qkv[:, lanes(p, 2)].astype(F32))
        both = pl.ds(pl.multiple_of(p * local, 128), local)

        gwq[:, :, both] = mul(first_t[...], qkv[:, both]).astype(BF).reshape(zs, 4 * rq, local)

    def pair_back(p):
        take_gmix(p).wait_recv()
        attend_back(p)
        sum_q(p).sib_start()

    loop(pairs, pair_back)

    base_gf = number.take(rows // side)

    def send_gf(i):
        at = pl.ds(pl.multiple_of(i * side, side), side)
        there = pl.ds(pl.multiple_of(rows + i * side, side), side)
        return far(first.at[at, :], first.at[there, :], base_gf + i, x_peer)

    def first_back(i, source, at):
        there = pl.ds(pl.multiple_of(at + i * side, side), side)
        grad = mul_nt(qkv[there, :], flat(wq[...]))
        scaled, unused = normed(source[pl.ds(pl.multiple_of(i * side, side), side), :].astype(F32))
        gvec[GAIN_1] += column_sum(grad * scaled)
        gvec[SHIFT_1] += column_sum(grad)
        return grad

    def away(i):
        grad = first_back(i, tok_far, (1 - s) * rows)
        first[pl.ds(pl.multiple_of(i * side, side), side), :] = grad.astype(BF)
        send_gf(i).start()

    loop(rows // side, away)
    sum_q(2).y_start()

    def stay(i):
        grad = first_back(i, tok, s * rows)
        at = pl.ds(pl.multiple_of(i * side, side), side)
        for j in range(width // 128):
            pieces[j, at, :] = grad[:, j * 128 : (j + 1) * 128]

    loop(rows // side, stay)

    late_rows.z_start()
    sum_u(2).z_start()
    sum_q(1).z_start()
    sum_u(3).z_start()

    def fall(i):
        at = pl.ds(pl.multiple_of(i * side, side), side)
        middle[at, :] += mul(hidden[at, :], flat(wd[...]))

    loop(rows // side, fall)
    late_rows.y_start()
    sum_q(2).z_start()

    def finish_out(i):
        at = pl.ds(pl.multiple_of(i * 128, 128), 128)
        value = middle[at, :] + vec[BIAS_DOWN]
        spot = s * rows + i * 128 + lax.broadcasted_iota(jnp.int32, (128, width), 0)
        out[at, :] = jnp.where(spot < last_valid, value, 0.0).astype(BF)

    loop(rows // 128, finish_out)
    finish_e(1)
    sum_u(2).finish()

    slot_q = number.take(pairs)

    def swap_q(p, half):
        block = r5_q.at[half, :, pl.ds(p * local, local)]
        return far_g(block, block, slot_q + p, x_peer)

    def finish_q(p):
        r5_q[s, :, p * local : (p + 1) * local] = sum_q(p).z_finish().astype(BF)
        swap_q(p, s).start()

    finish_q(0)
    late_rows.next_start(1)
    finish_q(1)
    late_rows.next_start(2)
    sum_u(3).finish()

    def last(i):
        at = pl.ds(pl.multiple_of(i * side, side), side)
        send_gf(i).wait_recv()
        scaled, inverse = normed(tok[at, :].astype(F32))
        there = pl.ds(pl.multiple_of(rows + i * side, side), side)
        own = jnp.concatenate([pieces[j, at, :] for j in range(width // 128)], axis=1)
        grad = own + first[there, :].astype(F32)
        gtok[at, :] = gtok[at, :] + normed_back(grad, scaled, inverse, vec[GAIN_1])

        @pl.when(i == 0)
        def _():
            finish_q(2)

    loop(rows // side, last)

    late_rows.finish()
    early_rows.finish()
    for i in range(BIAS_UP + tiles, TABLE):
        out_v[i] = jnp.zeros((1, width), F32)
    far_g(r5_d.at[1 - s], r5_d.at[1 - s], base_xs, x_peer).wait_recv()
    for half in range(2):
        out_d[:, half * local : (half + 1) * local] = r5_d[half].astype(F32)
    for t in range(early):
        swap_e(t).wait_recv()
        at = slice(t * tile, (t + 1) * tile)
        out_u[:, at] = r4_u[0, :, at].astype(F32) + r4_u[1, :, at].astype(F32)
    for t in range(early, tiles):
        sum_u(t).swap(1 - s).wait_recv()
        for half in range(2):
            wide = t * tile + half * local
            out_u[:, wide : wide + local] = r5_u[
                half, :, (t - early) * local : (t - early + 1) * local
            ].astype(F32)
    swap_o.wait_recv()
    out_o[...] = r4_o[0].astype(F32) + r4_o[1].astype(F32)
    for p in range(pairs):
        swap_q(p, 1 - s).wait_recv()
    for half in range(2):
        for p in range(pairs):
            for part in range(3):
                at = part * width + half * local + p * 128
                out_q[:, at : at + 128] = r5_q[
                    half, :, p * local + part * 128 : p * local + part * 128 + 128
                ].astype(F32)

    for dz in range(1, zs):
        far(table, e_z.at[dz - 1], base_e + dz - 1, z_peers[dz - 1]).wait_send()
        far_g(ry_d.at[0], rz_d.at[dz - 1], base_zd + dz - 1, z_peers[dz - 1]).wait_send()
    late_rows.sent()
    early_rows.sent()
    for copy in (y_table, c_table, send_tok, xd):
        copy.wait_send()
    for p in range(pairs):
        gather_q(p).sent()
        sum_q(p).sent()
        swap_q(p, s).wait_send()
    sum_o.sent()
    for i in range(cuts):
        gather_d(i).sent()
    for p in range(pairs):
        send_gmix(p).wait_send()
    for t in range(tiles):
        for yy in range(2):
            sib_d(t, yy).wait_send()
        x_d(t).wait_send()
        y_d(t).wait_send()
    for t in range(early):
        sum_e(t).sent()
        swap_e(t).wait_send()
    for t in range(early, tiles):
        sum_u(t).sent()
    swap_o.wait_send()
    for i in range(rows // side):
        send_gf(i).wait_send()


def fused_fits(tokens, lengths, own_q, own_d, shards, pair):
    rows, width = tokens.shape
    return (
        shards == 16
        and pair == 2
        and rows % 256 == 0
        and (width // pair) % 128 == 0
        and own_q.shape[0] % 16 == 0
        and own_d.shape[0] % 64 == 0
        and own_d.shape[0] * shards == 4 * width
    )


def fused(tokens, lengths, w_qkv, w_out, w_up, w_down, small, bias_up, cotangent):
    rows, width = tokens.shape
    shards = lax.axis_size("dp")
    zs = shards // 4
    d = lax.axis_index("dp")
    rq, rd = w_qkv.shape[0], w_down.shape[0]
    deep = 4 * rd * zs
    group = 2 * rows
    local = width // 2
    pairs = local // 128
    lane = jnp.arange(width)
    own = jnp.where(lane // rq == d, jnp.tile(jnp.stack(small), (1, shards)), 0)
    at = jnp.arange(zs)[:, None] * width + lane[None, :]
    up = jnp.where(at // rd == d, jnp.tile(bias_up, (width // rd,))[None, :], 0)
    table = jnp.concatenate([own, up, jnp.zeros((TABLE - 8 - zs, width), own.dtype)], axis=0)

    def vm(shape, kind=BF):
        return pltpu.VMEM(shape, kind)

    scratch = [
        vm((zs, 4 * rq, 3 * local)), vm((zs, 4 * rq, width)), vm((zs, 4 * rq, deep)),
        vm((zs, 4 * rd, width)), vm((zs, 4 * rq, 3 * local)), vm((zs, 4 * rd, width)),
        vm((rows, width)), vm((rows, width)), vm((group, width)), vm((width, group)), vm((group, 3 * local)),
        vm((pairs, 128, group)), vm((pairs, 128, group)), vm((1, group), jnp.int32),
        vm((pairs, 2, 1, group), F32), vm((128, group), F32),
        vm((group, local)), vm((rows, width)), vm((width, rows)), vm((rows, width), F32),
        vm((rows, width)), vm((width, rows)), vm((rows, width)),
        vm((rows, deep)), vm((4 * rd, rows)), vm((rows, deep)),
        vm((width // 128, rows, 128), F32),
        vm((2, TABLE, width)), vm((zs - 1, TABLE, width)), vm((TABLE, width)), vm((TABLE, width)),
        vm((TABLE, 1, width), F32), vm((TABLE, 1, width), F32), vm((zs - 1, TABLE, 1, width), F32),
        vm((TABLE, 1, width), F32), vm((TABLE, 1, width), F32), vm((TABLE, 1, width), F32),
        vm((3, TABLE, 1, width), F32),
        vm((zs, 2 * rd, width)), vm((zs, 2 * rd, local)), vm((zs, rd, local)),
        vm((zs - 1, rd, local)), vm((2, rd, local)),
        vm((zs, 2 * rq, deep)), vm((zs, 2 * rq, deep // 4)), vm((zs, rq, deep // 4)),
        vm((zs - 1, rq, deep // 4)), vm((2, rq, deep // 4)),
        vm((zs, rq, deep // 2)), vm((zs - 1, rq, deep // 2)), vm((2, rq, deep // 2)),
        vm((zs, 2 * rq, width)), vm((zs, rq, width)), vm((zs - 1, rq, width)), vm((2, rq, width)),
        vm((zs, 2 * rq, 3 * local)), vm((zs, rq, 3 * local)), vm((zs - 1, rq, 3 * local)),
        vm((2, rq, 3 * local)),
        pltpu.SemaphoreType.DMA((NEAR_COUNT,)),
        pltpu.SemaphoreType.DMA((FAR_COUNT,)),
        pltpu.SemaphoreType.DMA((FAR_COUNT,)),
    ]
    here = pl.BlockSpec(memory_space=pltpu.VMEM)
    away = pl.BlockSpec(memory_space=pl.ANY)
    return pl.pallas_call(
        fused_kernel,
        out_shape=(
            jax.ShapeDtypeStruct((rows, width), BF),
            jax.ShapeDtypeStruct((rows, width), F32),
            jax.ShapeDtypeStruct((rq, 3 * width), F32),
            jax.ShapeDtypeStruct((rq, width), F32),
            jax.ShapeDtypeStruct((rq, deep), F32),
            jax.ShapeDtypeStruct((rd, width), F32),
            jax.ShapeDtypeStruct((TABLE, 1, width), F32),
        ),
        in_specs=[pl.BlockSpec(memory_space=pltpu.SMEM), here, away, away, away, away, away, away],
        out_specs=[here] * 7,
        scratch_shapes=scratch,
        compiler_params=pltpu.CompilerParams(
            collective_id=0, has_side_effects=True, vmem_limit_bytes=67_043_328
        ),
        name="block",
    )(lengths, table, tokens, cotangent, w_qkv, w_out, w_up, w_down)


def closing_kernel(*refs):
    given, table, taken = refs[:6], refs[6], refs[7:]
    d = lax.axis_index("dp")
    for source, there in zip(given, taken[:6]):
        there[...] = source[...]
    own, up = taken[6:14], taken[14]
    width = table.shape[2]
    rq, rd = own[0].shape[1], up.shape[1]
    rows = jnp.concatenate([table[i] for i in range(8)], axis=0)
    moved = pltpu.roll(rows, lax.rem(width - d * rq, width), 1)
    for i in range(8):
        own[i][...] = moved[i : i + 1, :rq]
    row = jnp.broadcast_to(table[BIAS_UP + lax.div(d * rd, width)], (8, width))
    moved = pltpu.roll(row, lax.rem(width - lax.rem(d * rd, width), width), 1)
    up[...] = moved[0:1, :rd]


def per_device(
    tokens, lengths, w_qkv, w_out, w_up, w_down, bias_q, bias_v, bias_out, bias_up, bias_down,
    gain_one, shift_one, gain_two, shift_two, cotangent,
):
    if not fused_fits(
        tokens, lengths, w_qkv, w_down, lax.axis_size("dp"), lax.axis_size("seq")
    ):
        return per_device_plain(
            tokens, lengths, w_qkv, w_out, w_up, w_down, bias_q, bias_v, bias_out, bias_up,
            bias_down, gain_one, shift_one, gain_two, shift_two, cotangent,
        )
    small = [bias_q, bias_v, gain_one, shift_one, bias_out, bias_down, gain_two, shift_two]
    results = fused(
        tokens, lengths, w_qkv, w_out, w_up, w_down, small, bias_up, cotangent
    )
    rq, rd = w_qkv.shape[0], w_down.shape[0]
    here = pl.BlockSpec(memory_space=pltpu.VMEM)
    out, gtok, gq, go, gu, gd, *own, up = pl.pallas_call(
        closing_kernel,
        out_shape=tuple(jax.ShapeDtypeStruct(a.shape, a.dtype) for a in results[:6])
        + (jax.ShapeDtypeStruct((1, rq), F32),) * 8 + (jax.ShapeDtypeStruct((1, rd), F32),),
        in_specs=[here] * 7,
        out_specs=[here] * 15,
        name="closing",
    )(*results)
    own, up = [piece[0] for piece in own], up[0]
    return (
        out, gtok, gq, go, gu, gd,
        own[0], own[1], own[4], up, own[5], own[2], own[3], own[6], own[7],
    )


def solution(mesh):
    return jax.shard_map(
        per_device,
        mesh=mesh,
        in_specs=(
            P(("dp", "seq"), None),
            P("dp", None),
            P("dp", None),
            P("dp", None),
            P("dp", None),
            P("dp", None),
            P("dp"),
            P("dp"),
            P("dp"),
            P("dp"),
            P("dp"),
            P("dp"),
            P("dp"),
            P("dp"),
            P("dp"),
            P(("dp", "seq"), None),
        ),
        out_specs=(
            P(("dp", "seq"), None),
            P(("dp", "seq"), None),
            P("dp", None),
            P("dp", None),
            P("dp", None),
            P("dp", None),
            P("dp"),
            P("dp"),
            P("dp"),
            P("dp"),
            P("dp"),
            P("dp"),
            P("dp"),
            P("dp"),
            P("dp"),
        ),
        check_vma=False,
    )
```

```python
import jax
import jax.numpy as jnp
from jax import lax
from jax.experimental import pallas as pl
from jax.experimental.pallas import tpu as pltpu
from jax.sharding import PartitionSpec as P

HEAD_DIM = 64


EPSILON = 1e-05
MASKED = -1e30
SLOPE = 0.7978845608028654
CUBIC = 0.044715


def as_sent(array):
    return jax.tree.map(lambda a: a.astype(jnp.bfloat16) if a.dtype == jnp.float32 else a, array)


def dense(left, right):
    return jnp.dot(left, right, preferred_element_type=jnp.float32)


def dense_left(left, right):
    return lax.dot_general(
        left, right, (((0,), (0,)), ((), ())), preferred_element_type=jnp.float32
    )


def dense_right(left, right):
    return lax.dot_general(
        left, right, (((1,), (1,)), ((), ())), preferred_element_type=jnp.float32
    )


def norm_parts(value):
    mean = jnp.mean(value, axis=-1, keepdims=True)
    centred = value - mean
    inverse = lax.rsqrt(jnp.mean(centred * centred, axis=-1, keepdims=True) + EPSILON)
    return (centred * inverse, inverse)


def norm_back(grad, scaled, inverse, gain):
    shaped = grad * gain
    inner = jnp.mean(shaped * scaled, axis=-1, keepdims=True)
    return inverse * (shaped - jnp.mean(shaped, axis=-1, keepdims=True) - scaled * inner)


def gelu_value(value):
    return 0.5 * value * (1.0 + jnp.tanh(SLOPE * (value + CUBIC * value * value * value)))


def gelu_slope(value):
    bent = jnp.tanh(SLOPE * (value + CUBIC * value * value * value))
    return 0.5 * (1.0 + bent) + 0.5 * value * (1.0 - bent * bent) * SLOPE * (
        1.0 + 3.0 * CUBIC * value * value
    )


def per_device_plain(
    tokens,
    lengths,
    w_qkv,
    w_out,
    w_up,
    w_down,
    bias_q,
    bias_v,
    bias_out,
    bias_up,
    bias_down,
    gain_one,
    shift_one,
    gain_two,
    shift_two,
    cotangent,
):
    width = tokens.shape[1]
    rows = tokens.shape[0]
    pair = lax.axis_size("seq")
    rank = lax.axis_index("seq")
    group = rows * pair
    local = width // pair
    heads = local // HEAD_DIM
    scale = HEAD_DIM ** (-0.5)
    block = 512
    blocks = group // block
    whole = (
        lax.all_gather(w_qkv, "dp", axis=0, tiled=True),
        lax.all_gather(w_out, "dp", axis=0, tiled=True),
        lax.all_gather(w_up, "dp", axis=0, tiled=True),
        lax.all_gather(w_down, "dp", axis=0, tiled=True),
        lax.all_gather(bias_q, "dp", axis=0, tiled=True),
        lax.all_gather(bias_v, "dp", axis=0, tiled=True),
        lax.all_gather(bias_out, "dp", axis=0, tiled=True),
        lax.all_gather(bias_up, "dp", axis=0, tiled=True),
        lax.all_gather(bias_down, "dp", axis=0, tiled=True),
        lax.all_gather(gain_one, "dp", axis=0, tiled=True),
        lax.all_gather(shift_one, "dp", axis=0, tiled=True),
        lax.all_gather(gain_two, "dp", axis=0, tiled=True),
        lax.all_gather(shift_two, "dp", axis=0, tiled=True),
    )
    weight_qkv, weight_out, weight_up, weight_down = whole[0:4]
    add_q, add_v, add_out, add_up, add_down, scale_one, move_one, scale_two, move_two = [
        piece.astype(jnp.float32) for piece in whole[4:]
    ]
    slots = lengths.shape[1]
    position = jnp.arange(group, dtype=jnp.int32)
    ends = jnp.cumsum(lengths[0])
    segment = jnp.sum((position[:, None] >= ends[None, :]).astype(jnp.int32), axis=1)
    own_segment = lax.dynamic_slice_in_dim(segment, rank * rows, rows)
    valid = (own_segment < slots - 1)[:, None]
    inputs = tokens.astype(jnp.float32)
    scaled_one, inverse_one = norm_parts(inputs)
    first = (scaled_one * scale_one + move_one).astype(jnp.bfloat16)
    bias_qkv = jnp.concatenate([add_q, jnp.zeros_like(add_q), add_v])
    qkv = (dense(first, weight_qkv) + bias_qkv).astype(jnp.bfloat16)
    head_side = lax.all_to_all(
        qkv.reshape(rows, 3, pair, local), "seq", split_axis=2, concat_axis=0, tiled=True
    )
    query = head_side[:, 0, 0].reshape(group, heads, HEAD_DIM)
    keys = head_side[:, 1, 0].reshape(group, heads, HEAD_DIM)
    values = head_side[:, 2, 0].reshape(group, heads, HEAD_DIM)

    def block_scores(index):
        start = index * block
        query_rows = lax.dynamic_slice_in_dim(query, start, block)
        raw = (
            jnp.einsum("qhd,khd->hqk", query_rows, keys, preferred_element_type=jnp.float32) * scale
        )
        row_segment = lax.dynamic_slice_in_dim(segment, start, block)
        row_position = lax.dynamic_slice_in_dim(position, start, block)
        allowed = (row_segment[:, None] == segment[None, :]) & (
            position[None, :] <= row_position[:, None]
        )
        return (jnp.where(allowed[None], raw, MASKED), query_rows)

    def attend(index):
        scores, unused = block_scores(index)
        top = jnp.max(scores, axis=-1, keepdims=True)
        weights = jnp.exp(scores - top)
        total = jnp.sum(weights, axis=-1, keepdims=True)
        probs = (weights / total).astype(jnp.bfloat16)
        mixed_rows = jnp.einsum("hqk,khd->qhd", probs, values, preferred_element_type=jnp.float32)
        return (
            mixed_rows.reshape(block, local).astype(jnp.bfloat16),
            (top + jnp.log(total))[:, :, 0],
        )

    mixed_blocks, log_totals = lax.map(attend, jnp.arange(blocks))
    mixed_head = mixed_blocks.reshape(group, 1, local)
    mixed = lax.all_to_all(mixed_head, "seq", split_axis=0, concat_axis=1, tiled=True).reshape(
        rows, width
    )
    middle = inputs + dense(mixed, weight_out) + add_out
    scaled_two, inverse_two = norm_parts(middle)
    second = (scaled_two * scale_two + move_two).astype(jnp.bfloat16)
    pre = dense(second, weight_up) + add_up
    hidden = gelu_value(pre).astype(jnp.bfloat16)
    result = middle + dense(hidden, weight_down) + add_down
    block_out = jnp.where(valid, result, 0.0).astype(jnp.bfloat16)
    grad_out = jnp.where(valid, cotangent, jnp.zeros_like(cotangent))
    grad_weight_down = dense_left(hidden, grad_out)
    grad_add_down = jnp.sum(grad_out.astype(jnp.float32), axis=0)
    grad_pre = (dense_right(grad_out, weight_down) * gelu_slope(pre)).astype(jnp.bfloat16)
    grad_weight_up = dense_left(second, grad_pre)
    grad_add_up = jnp.sum(grad_pre.astype(jnp.float32), axis=0)
    grad_second = dense_right(grad_pre, weight_up)
    grad_scale_two = jnp.sum(grad_second * scaled_two, axis=0)
    grad_move_two = jnp.sum(grad_second, axis=0)
    grad_middle = grad_out.astype(jnp.float32) + norm_back(
        grad_second, scaled_two, inverse_two, scale_two
    )
    grad_attn = grad_middle.astype(jnp.bfloat16)
    grad_weight_out = dense_left(mixed, grad_attn)
    grad_add_out = jnp.sum(grad_attn.astype(jnp.float32), axis=0)
    grad_mixed = dense_right(grad_attn, weight_out).astype(jnp.bfloat16)
    branch_grads = (
        grad_weight_out,
        grad_weight_up,
        grad_weight_down,
        grad_add_out,
        grad_add_up,
        grad_add_down,
        grad_scale_two,
        grad_move_two,
    )
    grad_head = lax.all_to_all(
        grad_mixed.reshape(rows, pair, local), "seq", split_axis=1, concat_axis=0, tiled=True
    )
    grad_head = grad_head.reshape(group, heads, HEAD_DIM)

    def attend_back(carry, index):
        grad_keys, grad_values = carry
        scores, query_rows = block_scores(index)
        probs = jnp.exp(scores - log_totals[index][:, :, None])
        grad_rows = lax.dynamic_slice_in_dim(grad_head, index * block, block)
        grad_probs = jnp.einsum(
            "qhd,khd->hqk", grad_rows, values, preferred_element_type=jnp.float32
        )
        centre = jnp.sum(probs * grad_probs, axis=-1, keepdims=True)
        grad_scores = (probs * (grad_probs - centre)).astype(jnp.bfloat16)
        grad_values = grad_values + jnp.einsum(
            "hqk,qhd->khd",
            probs.astype(jnp.bfloat16),
            grad_rows,
            preferred_element_type=jnp.float32,
        )
        grad_keys = (
            grad_keys
            + jnp.einsum(
                "hqk,qhd->khd", grad_scores, query_rows, preferred_element_type=jnp.float32
            )
            * scale
        )
        grad_query = (
            jnp.einsum("hqk,khd->qhd", grad_scores, keys, preferred_element_type=jnp.float32)
            * scale
        )
        return ((grad_keys, grad_values), grad_query)

    empty = jnp.zeros((group, heads, HEAD_DIM), jnp.float32)
    (grad_keys, grad_values), grad_queries = lax.scan(
        attend_back, (empty, empty), jnp.arange(blocks)
    )
    grad_side = jnp.stack(
        [
            grad_queries.reshape(group, local),
            grad_keys.reshape(group, local),
            grad_values.reshape(group, local),
        ],
        axis=1,
    ).astype(jnp.bfloat16)
    grad_qkv = lax.all_to_all(
        grad_side.reshape(group, 3, 1, local), "seq", split_axis=0, concat_axis=2, tiled=True
    )
    grad_qkv = grad_qkv.reshape(rows, 3 * width)
    grad_weight_qkv = dense_left(first, grad_qkv)
    column_sums = jnp.sum(grad_qkv.astype(jnp.float32), axis=0)
    grad_add_q = column_sums[:width]
    grad_add_v = column_sums[2 * width :]
    grad_first = dense_right(grad_qkv, weight_qkv)
    grad_scale_one = jnp.sum(grad_first * scaled_one, axis=0)
    grad_move_one = jnp.sum(grad_first, axis=0)
    grad_tokens = grad_middle + norm_back(grad_first, scaled_one, inverse_one, scale_one)
    stem_grads = (grad_weight_qkv, grad_add_q, grad_add_v, grad_scale_one, grad_move_one)
    halves = lax.psum_scatter(
        stem_grads + branch_grads, ("dp", "seq"), scatter_dimension=0, tiled=True
    )
    shares = jax.tree.map(
        lambda part, own: part.astype(own.dtype),
        lax.all_gather(as_sent(halves), "seq", axis=0, tiled=True),
        halves,
    )
    stem_shares = shares[0:5]
    branch_shares = shares[5:13]
    return (
        block_out,
        grad_tokens,
        stem_shares[0],
        branch_shares[0],
        branch_shares[1],
        branch_shares[2],
        stem_shares[1],
        stem_shares[2],
        branch_shares[3],
        branch_shares[4],
        branch_shares[5],
        stem_shares[3],
        stem_shares[4],
        branch_shares[6],
        branch_shares[7],
    )


FAR = pl.DeviceIdType.MESH
NT = (((1,), (1,)), ((), ()))
BF = jnp.bfloat16
F32 = jnp.float32


def mul(left, right):
    return jnp.dot(left, right, preferred_element_type=F32)


def mul_nt(left, right):
    return lax.dot_general(left, right, NT, preferred_element_type=F32)


def flat(blocks):
    return blocks.reshape(blocks.shape[0] * blocks.shape[1], blocks.shape[2])


def normed(value):
    width = value.shape[1]
    mean = jnp.sum(value, axis=1, keepdims=True) * (1.0 / width)
    centred = value - mean
    spread = jnp.sum(centred * centred, axis=1, keepdims=True) * (1.0 / width)
    inverse = lax.rsqrt(spread + EPSILON)
    return (centred * inverse, inverse)


def normed_back(grad, scaled, inverse, gain):
    width = grad.shape[1]
    shaped = grad * gain
    inner = jnp.sum(shaped * scaled, axis=1, keepdims=True) * (1.0 / width)
    outer = jnp.sum(shaped, axis=1, keepdims=True) * (1.0 / width)
    return inverse * (shaped - outer - scaled * inner)


def column_sum(value):
    return jnp.sum(value, axis=0, keepdims=True)


class Numbers:
    def __init__(self):
        self.used = 0

    def take(self, count):
        start = self.used
        self.used = start + count
        return start


BIAS_Q, BIAS_V, GAIN_1, SHIFT_1, BIAS_OUT, BIAS_DOWN, GAIN_2, SHIFT_2, BIAS_UP = range(9)
TABLE = 16
FAR_COUNT = 240
NEAR_COUNT = 32


def fused_kernel(
    lengths, table, tok_own, cot, own_q, own_o, own_u, own_d,
    out, gtok, out_q, out_o, out_u, out_d, out_v,
    wq, wo, wu, wd, gwq, gwd,
    tok, tok_far, first, first_t, qkv, k_t, v_t, lower, lse, o_t,
    mixed_near, mixed, mixed_t, middle, second, second_t, gout,
    hidden, hidden_t, slope, pieces,
    e_own, e_z, e_y, e_c, vec, gvec, v_z, v_y, v_c, v_x, v_sum,
    r1_d, rx_d, ry_d, rz_d, r5_d, r1_u, rx_u, ry_u, rz_u, r5_u,
    r2_u, r3_u, r4_u, r1_o, r2_o, r3_o, r4_o, r1_q, r2_q, r3_q, r5_q,
    near_sem, send_sem, recv_sem,
):
    d = lax.axis_index("dp")
    s = lax.axis_index("seq")
    z = lax.div(d, 4)
    y = lax.rem(lax.div(d, 2), 2)
    c = lax.rem(d, 2)
    zs = wq.shape[0]
    rows, width = tok_own.shape
    group = 2 * rows
    local = width // 2
    pairs = local // 128
    rq = width // (4 * zs)
    rd = own_d.shape[0]
    tile = 4 * rd
    tiles = zs
    z_peers = [(lax.rem(z + dz, zs) * 4 + y * 2 + c, s) for dz in range(1, zs)]
    y_peer = (z * 4 + (1 - y) * 2 + c, s)
    c_peer = (z * 4 + y * 2 + (1 - c), s)
    x_peer = (d, 1 - s)
    number = Numbers()
    local_number = Numbers()

    def far(src, dst, slot, device):
        return pltpu.make_async_remote_copy(
            src_ref=src, dst_ref=dst, send_sem=send_sem.at[slot], recv_sem=recv_sem.at[slot],
            device_id=device, device_id_type=FAR,
        )

    far_w, far_g = far, far

    def z_at(dz):
        return lax.rem(z + zs - dz, zs)

    def loop(count, body):
        lax.fori_loop(0, count, lambda i, carry: (body(i), carry)[1], 0)

    def block_rows(r, yy, cc):
        return pl.ds(pl.multiple_of((yy * 2 + cc) * r, r), r)

    barrier = pltpu.get_barrier_semaphore()
    everyone = z_peers + [y_peer, c_peer, x_peer]
    for peer in everyone:
        pl.semaphore_signal(barrier, inc=1, device_id=peer, device_id_type=FAR)
    pl.semaphore_wait(barrier, len(everyone))

    class Gather:
        def __init__(self, ref, r, columns, base, own=None, columns_at=None):
            self.ref, self.r, self.columns, self.base, self.own = ref, r, columns, base, own
            self.columns_at = columns_at

        def part(self, zz, yy, cc):
            return self.ref.at[zz, block_rows(self.r, yy, cc), self.columns]

        def layer(self, yy, cc, columns=None):
            columns = self.columns if columns is None else columns
            return self.ref.at[:, block_rows(self.r, yy, cc), columns]

        def z_copy(self, dz):
            columns = self.columns if self.columns_at is None else self.columns_at(dz)
            there = self.ref.at[z, block_rows(self.r, y, c), columns]
            here = there if self.own is None else self.own.at[:, columns]
            return far_w(here, there, self.base + dz - 1, z_peers[dz - 1])

        def z_start(self):
            for dz in range(1, zs):
                self.z_copy(dz).start()

        def z_wait(self):
            for dz in range(1, zs):
                block = self.part(z_at(dz), y, c)
                far_w(block, block, self.base + dz - 1, z_peers[dz - 1]).wait_recv()

        def y_copy(self, yy):
            return far_w(self.layer(yy, c), self.layer(yy, c), self.base + zs - 1, y_peer)

        def c_copy(self, yy, cc, other):
            return far_w(self.layer(yy, cc), self.layer(yy, cc), self.base + zs + other, c_peer)

        def relay(self, *following):
            self.z_wait()
            for other in following:
                other.z_start()
            self.y_copy(y).start()
            self.c_copy(y, c, 0).start()

        def relay_y(self):
            self.y_copy(1 - y).wait_recv()
            self.c_copy(1 - y, c, 1).start()

        def finish(self):
            self.c_copy(y, 1 - c, 0).wait_recv()
            self.c_copy(1 - y, 1 - c, 1).wait_recv()

        def sent(self):
            for dz in range(1, zs):
                self.z_copy(dz).wait_send()
            self.y_copy(y).wait_send()
            self.c_copy(y, c, 0).wait_send()
            self.c_copy(1 - y, c, 1).wait_send()

    class GatherHalf(Gather):
        def __init__(self, ref, r, columns, others, base, own):
            super().__init__(ref, r, columns, base, own)
            self.others = others

        def x_copy(self, yy, columns, other):
            block = self.layer(yy, c, columns)
            return far_w(block, block, self.base + zs + 2 + other, x_peer)

        def c_other(self, yy, cc, other):
            block = self.layer(yy, cc, self.others)
            return far_w(block, block, self.base + zs + 4 + other, c_peer)

        def push_x(self):
            self.x_copy(y, self.columns, 0).start()

        def relay_y(self):
            super().relay_y()
            self.x_copy(1 - y, self.columns, 1).start()

        def relay_x(self):
            self.x_copy(y, self.others, 0).wait_recv()
            self.c_other(y, c, 0).start()
            self.x_copy(1 - y, self.others, 1).wait_recv()
            self.c_other(1 - y, c, 1).start()

        def finish(self):
            super().finish()
            self.c_other(y, 1 - c, 0).wait_recv()
            self.c_other(1 - y, 1 - c, 1).wait_recv()

        def sent(self):
            super().sent()
            self.x_copy(y, self.columns, 0).wait_send()
            self.x_copy(1 - y, self.columns, 1).wait_send()
            self.c_other(y, c, 0).wait_send()
            self.c_other(1 - y, c, 1).wait_send()

    steps = zs + 2
    base_q = number.take(pairs * steps)

    def gather_q(p):
        return Gather(wq, rq, pl.ds(pl.multiple_of(p * local, 128), local), base_q + p * steps)

    gather_o = Gather(wo, rq, pl.ds(0, width), number.take(steps), own_o)
    base_gu = number.take(tiles * steps)

    def tile_lanes(t):
        return pl.ds(pl.multiple_of(t * tile, 128), tile)

    def turn(i, zz):
        return lax.rem(zz + i + 1, zs)

    def gather_u(i):
        return Gather(
            wu, rq, tile_lanes(turn(i, z)), base_gu + i * steps, own_u,
            lambda dz: tile_lanes(turn(i, lax.rem(z + dz, zs))),
        )

    cuts = local // 128
    base_gd = number.take(cuts * (zs + 6))

    def gather_d(i):
        mine = pl.ds(pl.multiple_of(s * local + i * 128, 128), 128)
        others = pl.ds(pl.multiple_of((1 - s) * local + i * 128, 128), 128)
        return GatherHalf(wd, rd, mine, others, base_gd + i * (zs + 6), own_d)

    near_q = []
    for p in range(pairs):
        for part in range(3):
            start = pl.multiple_of(part * width + s * local + p * 128, 128)
            near_q.append(
                pltpu.make_async_copy(
                    own_q.at[:, pl.ds(start, 128)],
                    wq.at[z, block_rows(rq, y, c), pl.ds(p * local + part * 128, 128)],
                    near_sem.at[local_number.take(1)],
                )
            )
    near_rest = []
    half = pl.ds(pl.multiple_of(s * local, 128), local)
    for own, there in (
        (own_o, wo.at[z, block_rows(rq, y, c), :]),
        (own_u, wu.at[z, block_rows(rq, y, c), :]),
        (own_d.at[:, half], wd.at[z, block_rows(rd, y, c), half]),
    ):
        near_rest.append(
            pltpu.make_async_copy(own, there, near_sem.at[local_number.take(1)])
        )
    near_cot = pltpu.make_async_copy(cot, gout, near_sem.at[local_number.take(1)])
    near_tok = pltpu.make_async_copy(tok_own, tok, near_sem.at[local_number.take(1)])
    for copy in near_q + [near_tok] + near_rest + [near_cot]:
        copy.start()

    base_e = number.take(zs + 1)
    for dz in range(1, zs):
        far(table, e_z.at[dz - 1], base_e + dz - 1, z_peers[dz - 1]).start()
    send_tok = far(tok_own, tok_far, number.take(1), x_peer)
    send_tok.start()
    for copy in near_q:
        copy.wait()
    for p in range(pairs):
        gather_q(p).z_start()

    for dz in range(1, zs):
        far(table, e_z.at[dz - 1], base_e + dz - 1, z_peers[dz - 1]).wait_recv()
    total = table[...].astype(F32)
    for dz in range(1, zs):
        total = total + e_z[dz - 1].astype(F32)
    e_own[0] = total.astype(BF)
    y_table = far(e_own.at[0], e_y, base_e + zs - 1, y_peer)
    y_table.start()
    gather_q(0).relay(gather_o)

    ends = []
    end = jnp.int32(0)
    for j in range(lengths.shape[1]):
        end = end + lengths[0, j]
        ends.append(end)
    position = lax.broadcasted_iota(jnp.int32, (1, group), 1)
    start = jnp.zeros((1, group), jnp.int32)
    for end in ends[:-1]:
        start = jnp.where(position >= end, end, start)
    lower[...] = start
    last_valid = ends[-2]

    y_table.wait_recv()
    total = total + e_y[...].astype(F32)
    e_own[1] = total.astype(BF)
    c_table = far(e_own.at[1], e_c, base_e + zs, c_peer)
    c_table.start()
    gather_q(1).relay(gather_d(0))
    c_table.wait_recv()
    total = total + e_c[...].astype(F32)
    for i in range(TABLE):
        vec[i] = total[i : i + 1, :]

    def first_norm(source, at):
        def body(i):
            x = source[pl.ds(pl.multiple_of(i * 128, 128), 128), :].astype(F32)
            scaled, unused = normed(x)
            value = (scaled * vec[GAIN_1] + vec[SHIFT_1]).astype(BF)
            there = pl.ds(pl.multiple_of(at + i * 128, 128), 128)
            first[there, :] = value
            first_t[:, there] = value.T

        loop(rows // 128, body)

    near_tok.wait()
    first_norm(tok, s * rows)

    base_mixed = number.take(pairs)
    near_mixed = local_number.take(pairs)

    def lanes(p, part):
        return pl.ds(pl.multiple_of(p * local + part * 128, 128), 128)

    def send_mixed(p):
        there = pl.ds(pl.multiple_of(s * local + p * 128, 128), 128)
        here = pl.ds(pl.multiple_of(p * 128, 128), 128)
        away = pl.ds(pl.multiple_of((1 - s) * rows, 128), rows)
        return far(mixed_near.at[away, here], mixed.at[:, there], base_mixed + p, x_peer)

    def keep_mixed(p):
        there = pl.ds(pl.multiple_of(s * local + p * 128, 128), 128)
        here = pl.ds(pl.multiple_of(p * 128, 128), 128)
        stay = pl.ds(pl.multiple_of(s * rows, 128), rows)
        return pltpu.make_async_copy(
            mixed_near.at[stay, here], mixed.at[:, there], near_sem.at[near_mixed + p]
        )

    side = 256
    blocks = group // side
    key_at = lax.broadcasted_iota(jnp.int32, (side, side), 0)
    query_at = lax.broadcasted_iota(jnp.int32, (side, side), 1)
    lane = lax.broadcasted_iota(jnp.int32, (side, 128), 1)

    def head_lanes(value, h):
        inside = (lane >= h * HEAD_DIM) & (lane < h * HEAD_DIM + HEAD_DIM)
        return jnp.where(inside, value, 0.0).astype(BF)

    def scores(p, keys_block, query, qi, j):
        raw = mul_nt(keys_block, query)
        ok = key_at + j * side >= lower[:, qi * side : (qi + 1) * side]
        if j == qi:
            ok = ok & (key_at <= query_at)
        return jnp.where(ok, raw, MASKED)

    scale = HEAD_DIM ** (-0.5)

    def pass_on(k):
        @pl.when(k == 0)
        def _():
            gather_o.relay(gather_d(2))

        @pl.when(k == 2)
        def _():
            gather_d(0).relay(gather_u(0))
            gather_d(0).push_x()
            gather_o.relay_y()

        @pl.when(k == 3)
        def _():
            gather_d(1).relay(gather_u(1))
            gather_d(1).push_x()

        @pl.when(k == 4)
        def _():
            gather_d(2).relay(gather_u(2))

    def attend(p):
        def head(h):
            half = pl.ds(pl.multiple_of(h * HEAD_DIM, HEAD_DIM), HEAD_DIM)
            for qi in range(blocks):
                query = head_lanes(
                    qkv[qi * side : (qi + 1) * side, lanes(p, 0)].astype(F32) * scale, h
                )
                raw = []
                top = None
                for j in range(qi + 1):
                    block = scores(p, qkv[j * side : (j + 1) * side, lanes(p, 1)], query, qi, j)
                    raw.append(block)
                    high = jnp.max(block, axis=0, keepdims=True)
                    top = high if top is None else jnp.maximum(top, high)
                amount = jnp.zeros((1, side), F32)
                gathered = jnp.zeros((HEAD_DIM, side), F32)
                for j in range(qi + 1):
                    weight = jnp.exp(raw[j] - top)
                    amount = amount + column_sum(weight)
                    gathered = gathered + mul(
                        v_t[p, half, j * side : (j + 1) * side], weight.astype(BF)
                    )
                o_t[half, qi * side : (qi + 1) * side] = gathered / amount
                lse[p, h, :, qi * side : (qi + 1) * side] = top + jnp.log(amount)
            pass_on(p * 2 + h)

        loop(2, head)
        here = pl.ds(pl.multiple_of(p * 128, 128), 128)
        for qi in range(blocks):
            at = slice(qi * side, (qi + 1) * side)
            mixed_near[at, here] = o_t[:, at].T.astype(BF)

    def project(p, at_row):
        zero = jnp.zeros((1, 128), F32)
        there = pl.ds(pl.multiple_of(s * local + p * 128, 128), 128)
        bias = jnp.concatenate([vec[BIAS_Q, :, there], zero, vec[BIAS_V, :, there]], axis=1)
        weight = flat(wq[:, :, pl.ds(pl.multiple_of(p * local, 128), local)])

        def body(i):
            at = pl.ds(pl.multiple_of(at_row + i * side, side), side)
            value = (mul(first[at, :], weight) + bias).astype(BF)
            qkv[at, pl.ds(pl.multiple_of(p * local, 128), local)] = value
            k_t[p, :, at] = value[:, 128:256].T
            v_t[p, :, at] = value[:, 256:384].T

        loop(rows // side, body)

    gather_q(0).relay_y()
    gather_q(2).relay(gather_d(1))
    gather_q(0).finish()
    project(0, s * rows)
    gather_q(1).relay_y()
    for copy in near_rest:
        copy.wait()
    gather_q(2).relay_y()
    send_tok.wait_recv()
    first_norm(tok_far, (1 - s) * rows)

    def pair_forward(p):
        @pl.when(p > 0)
        def _():
            gather_q(p).finish()
            project(p, s * rows)

        project(p, (1 - s) * rows)
        attend(p)
        send_mixed(p).start()
        keep_mixed(p).start()

    loop(pairs, pair_forward)
    gather_d(0).relay_y()
    gather_d(1).relay_y()
    gather_d(2).push_x()
    gather_u(0).relay(gather_u(3))
    gather_d(2).relay_y()

    gather_o.finish()
    near_cot.wait()
    for p in range(pairs):
        keep_mixed(p).wait()
    for p in range(pairs):
        far(
            mixed_near.at[pl.ds(0, rows), pl.ds(0, 128)],
            mixed.at[:, pl.ds(pl.multiple_of((1 - s) * local + p * 128, 128), 128)],
            base_mixed + p, x_peer,
        ).wait_recv()

    def project_out(i):
        at = pl.ds(pl.multiple_of(i * 128, 128), 128)
        near = mixed[at, :]
        mixed_t[:, at] = near.T
        value = tok[at, :].astype(F32) + mul(near, flat(wo[...])) + vec[BIAS_OUT]
        middle[at, :] = value
        scaled, unused = normed(value)
        rounded = (scaled * vec[GAIN_2] + vec[SHIFT_2]).astype(BF)
        second[at, :] = rounded
        second_t[:, at] = rounded.T
        spot = s * rows + i * 128 + lax.broadcasted_iota(jnp.int32, (128, width), 0)
        gout[at, :] = jnp.where(spot < last_valid, gout[at, :].astype(F32), 0.0).astype(BF)

    loop(rows // 128, project_out)
    for p in range(pairs):
        send_mixed(p).wait_send()
    gather_d(0).relay_x()
    gather_u(1).relay()
    gather_u(0).relay_y()


    base_sib = number.take(tiles * 2)
    base_dx = number.take(tiles * 2)
    base_zd = number.take(zs - 1)
    base_xs = number.take(1)
    mine = pl.ds(pl.multiple_of(s * local, 128), local)
    others = pl.ds(pl.multiple_of((1 - s) * local, 128), local)

    def rows_y(r, yy):
        return pl.ds(pl.multiple_of(yy * r, r), r)

    def sib_d(t, yy):
        return far_g(
            gwd.at[t, block_rows(rd, yy, 1 - c), :], r1_d.at[t, rows_y(rd, yy), :],
            base_sib + t * 2 + yy, c_peer,
        )

    def sib_start_d(t):
        for yy in range(2):
            sib_d(t, yy).start()

    def x_d(t):
        return far_g(r1_d.at[t, :, others], rx_d.at[t], base_dx + t * 2, x_peer)

    def x_start_d(t):
        for yy in range(2):
            sib_d(t, yy).wait_recv()
            at = rows_y(rd, yy)
            r1_d[t, at, :] = (
                r1_d[t, at, :].astype(F32) + gwd[t, block_rows(rd, yy, c), :].astype(F32)
            ).astype(BF)
        x_d(t).start()

    def y_d(t):
        return far_g(rx_d.at[t, rows_y(rd, 1 - y), :], ry_d.at[t], base_dx + t * 2 + 1, y_peer)

    def y_start_d(t):
        x_d(t).wait_recv()
        rx_d[t] = (rx_d[t].astype(F32) + r1_d[t, :, mine].astype(F32)).astype(BF)
        y_d(t).start()

    def z_d(t, dz):
        return far_g(ry_d.at[t], rz_d.at[dz - 1], base_zd + dz - 1, (t * 4 + y * 2 + c, s))

    def z_start_d(t):
        y_d(t).wait_recv()
        ry_d[t] = (ry_d[t].astype(F32) + rx_d[t, rows_y(rd, y), :].astype(F32)).astype(BF)
        dz = lax.rem(t + zs - z, zs)

        @pl.when(dz > 0)
        def _():
            z_d(t, dz).start()

    class Pooled:
        def __init__(self, ref, start, span, parts, base):
            self.ref, self.base = ref, base
            self.r1, self.rx, self.ry, self.rz, self.r5 = parts
            half = span // 2
            self.full = pl.ds(pl.multiple_of(start, 128), span)
            self.mine = pl.ds(pl.multiple_of(start + s * half, 128), half)
            self.others = pl.ds(pl.multiple_of(start + (1 - s) * half, 128), half)
            self.narrow = pl.ds(pl.multiple_of((start - early * span) // 2, 128), half)

        def sib(self, yy):
            return far_g(
                self.ref.at[:, block_rows(rq, yy, 1 - c), self.full],
                self.r1.at[:, rows_y(rq, yy), self.full], self.base + yy, c_peer,
            )

        def sib_start(self):
            for yy in range(2):
                self.sib(yy).start()

        def along_x(self):
            return far_g(
                self.r1.at[:, :, self.others], self.rx.at[:, :, self.narrow], self.base + 2, x_peer
            )

        def x_start(self):
            for yy in range(2):
                self.sib(yy).wait_recv()
                at = rows_y(rq, yy)
                for zz in range(zs):
                    self.r1[zz, at, self.full] = (
                        self.r1[zz, at, self.full].astype(F32)
                        + self.ref[zz, block_rows(rq, yy, c), self.full].astype(F32)
                    ).astype(BF)
            self.along_x().start()

        def along_y(self):
            return far_g(
                self.rx.at[:, rows_y(rq, 1 - y), self.narrow], self.ry.at[:, :, self.narrow],
                self.base + 3, y_peer,
            )

        def y_start(self):
            self.along_x().wait_recv()
            for zz in range(zs):
                self.rx[zz, :, self.narrow] = (
                    self.rx[zz, :, self.narrow].astype(F32)
                    + self.r1[zz, :, self.mine].astype(F32)
                ).astype(BF)
            self.along_y().start()

        def along_z(self, dz):
            return far_g(
                self.ry.at[lax.rem(z + dz, zs), :, self.narrow],
                self.rz.at[dz - 1, :, self.narrow], self.base + 3 + dz, z_peers[dz - 1],
            )

        def z_start(self):
            self.along_y().wait_recv()
            at = rows_y(rq, y)
            for zz in range(zs):
                self.ry[zz, :, self.narrow] = (
                    self.ry[zz, :, self.narrow].astype(F32)
                    + self.rx[zz, at, self.narrow].astype(F32)
                ).astype(BF)
            for dz in range(1, zs):
                self.along_z(dz).start()

        def swap(self, half):
            block = self.r5.at[half, :, self.narrow]
            return far_g(block, block, self.base + 3 + zs, x_peer)

        def finish(self):
            total = self.ry[z, :, self.narrow].astype(F32)
            for dz in range(1, zs):
                self.along_z(dz).wait_recv()
                total = total + self.rz[dz - 1, :, self.narrow].astype(F32)
            self.r5[s, :, self.narrow] = total.astype(BF)
            self.swap(s).start()

        def sent(self):
            for yy in range(2):
                self.sib(yy).wait_send()
            self.along_x().wait_send()
            self.along_y().wait_send()
            for dz in range(1, zs):
                self.along_z(dz).wait_send()
            self.swap(s).wait_send()

    class Spread:
        def __init__(self, ref, columns, r1, r2, r3, base):
            self.ref, self.columns, self.r1, self.r2, self.r3 = ref, columns, r1, r2, r3
            self.base = base

        def sib(self, yy):
            return far_g(
                self.ref.at[:, block_rows(rq, yy, 1 - c), self.columns],
                self.r1.at[:, pl.ds(pl.multiple_of(yy * rq, rq), rq), self.columns],
                self.base + yy, c_peer,
            )

        def sib_start(self):
            self.sib(1 - y).start()
            self.sib(y).start()

        def along_y(self):
            return far_g(
                self.r1.at[:, pl.ds(pl.multiple_of((1 - y) * rq, rq), rq), self.columns],
                self.r2.at[:, :, self.columns], self.base + 2, y_peer,
            )

        def y_start(self):
            self.sib(1 - y).wait_recv()
            at = pl.ds(pl.multiple_of((1 - y) * rq, rq), rq)
            for zz in range(zs):
                self.r1[zz, at, self.columns] = (
                    self.r1[zz, at, self.columns].astype(F32)
                    + self.ref[zz, block_rows(rq, 1 - y, c), self.columns].astype(F32)
                ).astype(BF)
            self.along_y().start()

        def along_z(self, dz):
            return far_g(
                self.r2.at[lax.rem(z + dz, zs), :, self.columns],
                self.r3.at[dz - 1, :, self.columns], self.base + 2 + dz, z_peers[dz - 1],
            )

        def z_start(self):
            self.sib(y).wait_recv()
            self.along_y().wait_recv()
            at = pl.ds(pl.multiple_of(y * rq, rq), rq)
            for zz in range(zs):
                self.r2[zz, :, self.columns] = (
                    self.r2[zz, :, self.columns].astype(F32)
                    + self.r1[zz, at, self.columns].astype(F32)
                    + self.ref[zz, block_rows(rq, y, c), self.columns].astype(F32)
                ).astype(BF)
            for dz in range(1, zs):
                self.along_z(dz).start()

        def z_finish(self):
            total = self.r2[z, :, self.columns].astype(F32)
            for dz in range(1, zs):
                self.along_z(dz).wait_recv()
                total = total + self.r3[dz - 1, :, self.columns].astype(F32)
            return total

        def sent(self):
            self.sib(0).wait_send()
            self.sib(1).wait_send()
            self.along_y().wait_send()
            for dz in range(1, zs):
                self.along_z(dz).wait_send()

    def swap(parts, columns, slot):
        return far_g(parts.at[0, :, columns], parts.at[1, :, columns], slot, x_peer)

    early = tiles // 2
    spread_steps = zs + 2
    base_su = number.take(early * (spread_steps + 1))

    def sum_e(t):
        return Spread(
            wu, tile_lanes(t), r1_u, r2_u, r3_u, base_su + t * (spread_steps + 1)
        )

    def swap_e(t):
        return swap(r4_u, tile_lanes(t), base_su + t * (spread_steps + 1) + spread_steps)

    def finish_e(t):
        r4_u[0, :, tile_lanes(t)] = sum_e(t).z_finish().astype(BF)
        swap_e(t).start()

    whole = pl.ds(0, width)
    sum_o = Spread(wo, whole, r1_o, r2_o, r3_o, number.take(spread_steps))
    swap_o = swap(r4_o, whole, number.take(1))

    def finish_o():
        r4_o[0] = sum_o.z_finish().astype(BF)
        swap_o.start()

    pooled_steps = zs + 4
    base_pu = number.take(tiles * pooled_steps)

    def sum_u(t):
        return Pooled(wu, t * tile, tile, (r1_u, rx_u, ry_u, rz_u, r5_u), base_pu + t * pooled_steps)

    def pass_up(k):
        @pl.when(k == 0)
        def _():
            gather_d(1).relay_x()

        @pl.when(k == 1)
        def _():
            gather_u(2).relay()
            gather_u(1).relay_y()

        @pl.when(k == 2)
        def _():
            x_start_d(turn(0, z))

        @pl.when(k == 3)
        def _():
            gather_u(3).relay()
            gather_u(2).relay_y()

        @pl.when(k == 4)
        def _():
            gather_d(2).relay_x()
            x_start_d(turn(1, z))

        @pl.when(k == 5)
        def _():
            gather_u(3).relay_y()

        @pl.when(k == 6)
        def _():
            x_start_d(turn(2, z))

    def weigh_down(t):
        def part(m):
            at = pl.ds(pl.multiple_of(m * 2 * rd, 2 * rd), 2 * rd)
            gwd[t, at, :] = mul(hidden_t[at, :], gout[...]).astype(BF)

        loop(2, part)
        sib_start_d(t)

    def feed(i):
        t = turn(i, z)
        gather_u(i).finish()
        at = tile_lanes(t)
        pre = mul(second[...], flat(wu[:, :, at])) + vec[BIAS_UP + t]
        square = pre * pre
        bent = 0.5 * jnp.tanh(pre * (SLOPE + (SLOPE * CUBIC) * square)) + 0.5
        value = pre * bent
        bend = bent + value * (1.0 - bent) * (2.0 * SLOPE + (6.0 * SLOPE * CUBIC) * square)
        rounded = value.astype(BF)
        hidden[:, at] = rounded
        hidden_t[...] = rounded.T
        slope[:, at] = bend.astype(BF)
        pass_up(i * 2)

        @pl.when(i < tiles - 1)
        def _():
            weigh_down(t)

        pass_up(i * 2 + 1)

    loop(tiles, feed)
    y_start_d(turn(0, z))
    for i in range(cuts):
        gather_d(i).finish()

    def slopes_back(t):
        at = tile_lanes(t)
        grad = (mul_nt(gout[...], wd[t]) * slope[:, at].astype(F32)).astype(BF)
        slope[:, at] = grad
        gvec[BIAS_UP + t] = column_sum(grad.astype(F32))

    loop(tiles, slopes_back)

    def grow(i):
        at = pl.ds(pl.multiple_of(i * side, side), side)
        gtok[at, :] = mul_nt(slope[at, :], flat(wu[...]))

    loop(rows // side, grow)
    y_start_d(turn(1, z))

    for row in (BIAS_Q, BIAS_V, BIAS_OUT, BIAS_DOWN, GAIN_1, SHIFT_1, GAIN_2, SHIFT_2):
        gvec[row] = jnp.zeros((1, width), F32)
    gattn = mixed
    gmix = second

    def middle_back(i):
        at = pl.ds(pl.multiple_of(i * 128, 128), 128)
        grad = gtok[at, :]
        scaled, inverse = normed(middle[at, :])
        ahead = gout[at, :].astype(F32)
        gvec[GAIN_2] += column_sum(grad * scaled)
        gvec[SHIFT_2] += column_sum(grad)
        gvec[BIAS_DOWN] += column_sum(ahead)
        total = ahead + normed_back(grad, scaled, inverse, vec[GAIN_2])
        gtok[at, :] = total
        rounded = total.astype(BF)
        gattn[at, :] = rounded
        gvec[BIAS_OUT] += column_sum(rounded.astype(F32))
        gmix[at, :] = mul_nt(rounded, flat(wo[...])).astype(BF)

    loop(rows // 128, middle_back)

    class Vectors:
        def __init__(self, first_row, count, base):
            self.rows, self.base = range(first_row, first_row + count), base
            self.at = pl.ds(first_row, count)

        def copy(self, source, there, slot, device):
            return far(source.at[self.at], there.at[self.at], self.base + slot, device)

        def along_z(self, dz):
            return self.copy(gvec, v_z.at[dz - 1], dz - 1, z_peers[dz - 1])

        def step(self, k):
            there, device = ((v_y, y_peer), (v_c, c_peer), (v_x, x_peer))[k]
            return self.copy(v_sum.at[k], there, zs - 1 + k, device)

        def z_start(self):
            for dz in range(1, zs):
                self.along_z(dz).start()

        def y_start(self):
            for dz in range(1, zs):
                self.along_z(dz).wait_recv()
            for i in self.rows:
                total = gvec[i]
                for dz in range(1, zs):
                    total = total + v_z[dz - 1, i]
                v_sum[0, i] = total
            self.step(0).start()

        def next_start(self, k):
            self.step(k - 1).wait_recv()
            there = (v_y, v_c)[k - 1]
            v_sum[k, self.at] = v_sum[k - 1, self.at] + there[self.at]
            self.step(k).start()

        def finish(self):
            self.step(2).wait_recv()
            out_v[self.at] = v_sum[2, self.at] + v_x[self.at]

        def sent(self):
            for dz in range(1, zs):
                self.along_z(dz).wait_send()
            for k in range(3):
                self.step(k).wait_send()

    late_rows = Vectors(BIAS_Q, 4, number.take(zs + 2))
    early_rows = Vectors(BIAS_OUT, 4 + tiles, number.take(zs + 2))

    base_gmix = number.take(pairs)
    near_gmix = local_number.take(1)
    here_rows = pl.ds(pl.multiple_of(s * rows, 128), rows)
    there_rows = pl.ds(pl.multiple_of((1 - s) * rows, 128), rows)

    def send_gmix(p):
        lanes_p = pl.ds(pl.multiple_of((1 - s) * local + p * 128, 128), 128)
        at = pl.ds(pl.multiple_of(p * 128, 128), 128)
        return far(gmix.at[:, lanes_p], mixed_near.at[here_rows, at], base_gmix + p, x_peer)

    def take_gmix(p):
        at = pl.ds(pl.multiple_of(p * 128, 128), 128)
        return far(gmix.at[:, pl.ds(0, 128)], mixed_near.at[there_rows, at], base_gmix + p, x_peer)

    keep_gmix = pltpu.make_async_copy(
        gmix.at[:, mine], mixed_near.at[here_rows, :], near_sem.at[near_gmix]
    )
    send_gmix(0).start()
    keep_gmix.start()
    early_rows.z_start()
    weigh_down(z)

    gather_o.sent()

    wo[...] = mul(mixed_t[...], gattn[...]).astype(BF).reshape(zs, 4 * rq, width)
    x_start_d(z)
    for p in range(1, pairs):
        send_gmix(p).start()
    z_start_d(turn(0, z))
    y_start_d(turn(2, z))
    z_start_d(turn(1, z))
    for t in range(tiles):
        gather_u(t).sent()

    base_sq = number.take(pairs * spread_steps)

    def sum_q(p):
        return Spread(
            gwq, pl.ds(pl.multiple_of(p * local, 128), local), r1_q, r2_q, r3_q,
            base_sq + p * spread_steps,
        )

    sum_o.sib_start()

    def weigh_up_tile(t):
        at = tile_lanes(t)
        wu[:, :, at] = mul(second_t[...], slope[:, at]).astype(BF).reshape(zs, 4 * rq, tile)
        @pl.when(t < early)
        def _():
            sum_e(t).sib_start()

        @pl.when(t >= early)
        def _():
            sum_u(t).sib_start()

        @pl.when(t == 0)
        def _():
            sum_o.y_start()

        @pl.when(t == 1)
        def _():
            early_rows.y_start()

        @pl.when((t > 0) & (t < early))
        def _():
            sum_e(t - 1).y_start()

        @pl.when(t > early)
        def _():
            sum_u(t - 1).x_start()

    loop(tiles, weigh_up_tile)
    z_start_d(turn(2, z))
    sum_u(tiles - 1).x_start()
    keep_gmix.wait()

    xd = far_g(r5_d.at[s], r5_d.at[s], base_xs, x_peer)

    def finish_d():
        total = ry_d[z].astype(F32)
        for dz in range(1, zs):
            far_g(ry_d.at[0], rz_d.at[dz - 1], base_zd + dz - 1, z_peers[dz - 1]).wait_recv()
            total = total + rz_d[dz - 1].astype(F32)
        r5_d[s] = total.astype(BF)
        xd.start()

    def serve(k):
        @pl.when(k == 0)
        def _():
            early_rows.next_start(1)
            sum_o.z_start()
            y_start_d(z)
            sum_e(early - 1).y_start()

        @pl.when(k == 1)
        def _():
            early_rows.next_start(2)

        @pl.when(k == 2)
        def _():
            z_start_d(z)
            sum_e(0).z_start()
            sum_q(0).y_start()

        @pl.when(k == 3)
        def _():
            finish_o()

        @pl.when(k == 4)
        def _():
            sum_e(early - 1).z_start()
            sum_u(2).y_start()
            sum_q(1).y_start()
            finish_d()

        @pl.when(k == 5)
        def _():
            sum_u(3).y_start()
            sum_q(0).z_start()
            finish_e(0)

    per_piece = rows // side

    def dk_at(j):
        return (j // per_piece, slice(j % per_piece * side, (j % per_piece + 1) * side))

    def dv_at(j):
        return dk_at(j + blocks)

    def attend_back(p):
        for i in range(2 * group // rows):
            pieces[i] = jnp.zeros((rows, 128), F32)

        def head(h):
            half = pl.ds(pl.multiple_of(h * HEAD_DIM, HEAD_DIM), HEAD_DIM)
            here = pl.ds(pl.multiple_of(p * 128, 128), 128)
            for qi in range(blocks):
                at = slice(qi * side, (qi + 1) * side)
                query = head_lanes(qkv[at, lanes(p, 0)].astype(F32) * scale, h)
                grad = head_lanes(mixed_near[at, here].astype(F32), h)
                level = lse[p, h, :, at]
                weights, slopes = [], []
                centre = jnp.zeros((1, side), F32)
                for j in range(qi + 1):
                    there = slice(j * side, (j + 1) * side)
                    raw = scores(p, qkv[there, lanes(p, 1)], query, qi, j)
                    weight = jnp.exp(raw - level)
                    slope = mul_nt(qkv[there, lanes(p, 2)], grad)
                    centre = centre + column_sum(weight * slope)
                    weights.append(weight)
                    slopes.append(slope)
                total = jnp.zeros((HEAD_DIM, side), F32)
                for j in range(qi + 1):
                    there = slice(j * side, (j + 1) * side)
                    bend = (weights[j] * (slopes[j] - centre)).astype(BF)
                    pieces[dk_at(j)] += mul(bend, query)
                    pieces[dv_at(j)] += mul(weights[j].astype(BF), grad)
                    total = total + mul(k_t[p, half, there], bend)
                o_t[half, at] = total * scale
            serve(p * 2 + h)

        loop(2, head)
        for qi in range(blocks):
            at = slice(qi * side, (qi + 1) * side)
            qkv[at, lanes(p, 0)] = o_t[:, at].T.astype(BF)
            qkv[at, lanes(p, 1)] = pieces[dk_at(qi)].astype(BF)
            qkv[at, lanes(p, 2)] = pieces[dv_at(qi)].astype(BF)
        own = pl.ds(pl.multiple_of(s * local + p * 128, 128), 128)
        gvec[BIAS_Q, :, own] = column_sum(qkv[:, lanes(p, 0)].astype(F32))
        gvec[BIAS_V, :, own] = column_sum(qkv[:, lanes(p, 2)].astype(F32))
        both = pl.ds(pl.multiple_of(p * local, 128), local)

        gwq[:, :, both] = mul(first_t[...], qkv[:, both]).astype(BF).reshape(zs, 4 * rq, local)

    def pair_back(p):
        take_gmix(p).wait_recv()
        attend_back(p)
        sum_q(p).sib_start()

    loop(pairs, pair_back)

    base_gf = number.take(rows // side)

    def send_gf(i):
        at = pl.ds(pl.multiple_of(i * side, side), side)
        there = pl.ds(pl.multiple_of(rows + i * side, side), side)
        return far(first.at[at, :], first.at[there, :], base_gf + i, x_peer)

    def first_back(i, source, at):
        there = pl.ds(pl.multiple_of(at + i * side, side), side)
        grad = mul_nt(qkv[there, :], flat(wq[...]))
        scaled, unused = normed(source[pl.ds(pl.multiple_of(i * side, side), side), :].astype(F32))
        gvec[GAIN_1] += column_sum(grad * scaled)
        gvec[SHIFT_1] += column_sum(grad)
        return grad

    def away(i):
        grad = first_back(i, tok_far, (1 - s) * rows)
        first[pl.ds(pl.multiple_of(i * side, side), side), :] = grad.astype(BF)
        send_gf(i).start()

    loop(rows // side, away)
    sum_q(2).y_start()

    def stay(i):
        grad = first_back(i, tok, s * rows)
        at = pl.ds(pl.multiple_of(i * side, side), side)
        for j in range(width // 128):
            pieces[j, at, :] = grad[:, j * 128 : (j + 1) * 128]

    loop(rows // side, stay)

    late_rows.z_start()
    sum_u(2).z_start()
    sum_q(1).z_start()
    sum_u(3).z_start()

    def fall(i):
        at = pl.ds(pl.multiple_of(i * side, side), side)
        middle[at, :] += mul(hidden[at, :], flat(wd[...]))

    loop(rows // side, fall)
    late_rows.y_start()
    sum_q(2).z_start()

    def finish_out(i):
        at = pl.ds(pl.multiple_of(i * 128, 128), 128)
        value = middle[at, :] + vec[BIAS_DOWN]
        spot = s * rows + i * 128 + lax.broadcasted_iota(jnp.int32, (128, width), 0)
        out[at, :] = jnp.where(spot < last_valid, value, 0.0).astype(BF)

    loop(rows // 128, finish_out)
    finish_e(1)
    sum_u(2).finish()

    slot_q = number.take(pairs)

    def swap_q(p, half):
        block = r5_q.at[half, :, pl.ds(p * local, local)]
        return far_g(block, block, slot_q + p, x_peer)

    def finish_q(p):
        r5_q[s, :, p * local : (p + 1) * local] = sum_q(p).z_finish().astype(BF)
        swap_q(p, s).start()

    finish_q(0)
    late_rows.next_start(1)
    finish_q(1)
    late_rows.next_start(2)
    sum_u(3).finish()

    def last(i):
        at = pl.ds(pl.multiple_of(i * side, side), side)
        send_gf(i).wait_recv()
        scaled, inverse = normed(tok[at, :].astype(F32))
        there = pl.ds(pl.multiple_of(rows + i * side, side), side)
        own = jnp.concatenate([pieces[j, at, :] for j in range(width // 128)], axis=1)
        grad = own + first[there, :].astype(F32)
        gtok[at, :] = gtok[at, :] + normed_back(grad, scaled, inverse, vec[GAIN_1])

        @pl.when(i == 0)
        def _():
            finish_q(2)

    loop(rows // side, last)

    late_rows.finish()
    early_rows.finish()
    for i in range(BIAS_UP + tiles, TABLE):
        out_v[i] = jnp.zeros((1, width), F32)
    far_g(r5_d.at[1 - s], r5_d.at[1 - s], base_xs, x_peer).wait_recv()
    for half in range(2):
        out_d[:, half * local : (half + 1) * local] = r5_d[half].astype(F32)
    for t in range(early):
        swap_e(t).wait_recv()
        at = slice(t * tile, (t + 1) * tile)
        out_u[:, at] = r4_u[0, :, at].astype(F32) + r4_u[1, :, at].astype(F32)
    for t in range(early, tiles):
        sum_u(t).swap(1 - s).wait_recv()
        for half in range(2):
            wide = t * tile + half * local
            out_u[:, wide : wide + local] = r5_u[
                half, :, (t - early) * local : (t - early + 1) * local
            ].astype(F32)
    swap_o.wait_recv()
    out_o[...] = r4_o[0].astype(F32) + r4_o[1].astype(F32)
    for p in range(pairs):
        swap_q(p, 1 - s).wait_recv()
    for half in range(2):
        for p in range(pairs):
            for part in range(3):
                at = part * width + half * local + p * 128
                out_q[:, at : at + 128] = r5_q[
                    half, :, p * local + part * 128 : p * local + part * 128 + 128
                ].astype(F32)

    for dz in range(1, zs):
        far(table, e_z.at[dz - 1], base_e + dz - 1, z_peers[dz - 1]).wait_send()
        far_g(ry_d.at[0], rz_d.at[dz - 1], base_zd + dz - 1, z_peers[dz - 1]).wait_send()
    late_rows.sent()
    early_rows.sent()
    for copy in (y_table, c_table, send_tok, xd):
        copy.wait_send()
    for p in range(pairs):
        gather_q(p).sent()
        sum_q(p).sent()
        swap_q(p, s).wait_send()
    sum_o.sent()
    for i in range(cuts):
        gather_d(i).sent()
    for p in range(pairs):
        send_gmix(p).wait_send()
    for t in range(tiles):
        for yy in range(2):
            sib_d(t, yy).wait_send()
        x_d(t).wait_send()
        y_d(t).wait_send()
    for t in range(early):
        sum_e(t).sent()
        swap_e(t).wait_send()
    for t in range(early, tiles):
        sum_u(t).sent()
    swap_o.wait_send()
    for i in range(rows // side):
        send_gf(i).wait_send()


def fused_fits(tokens, lengths, own_q, own_d, shards, pair):
    rows, width = tokens.shape
    return (
        shards == 16
        and pair == 2
        and rows % 256 == 0
        and (width // pair) % 128 == 0
        and own_q.shape[0] % 16 == 0
        and own_d.shape[0] % 64 == 0
        and own_d.shape[0] * shards == 4 * width
    )


def fused(tokens, lengths, w_qkv, w_out, w_up, w_down, small, bias_up, cotangent):
    rows, width = tokens.shape
    shards = lax.axis_size("dp")
    zs = shards // 4
    d = lax.axis_index("dp")
    rq, rd = w_qkv.shape[0], w_down.shape[0]
    deep = 4 * rd * zs
    group = 2 * rows
    local = width // 2
    pairs = local // 128
    lane = jnp.arange(width)
    own = jnp.where(lane // rq == d, jnp.tile(jnp.stack(small), (1, shards)), 0)
    at = jnp.arange(zs)[:, None] * width + lane[None, :]
    up = jnp.where(at // rd == d, jnp.tile(bias_up, (width // rd,))[None, :], 0)
    table = jnp.concatenate([own, up, jnp.zeros((TABLE - 8 - zs, width), own.dtype)], axis=0)

    def vm(shape, kind=BF):
        return pltpu.VMEM(shape, kind)

    scratch = [
        vm((zs, 4 * rq, 3 * local)), vm((zs, 4 * rq, width)), vm((zs, 4 * rq, deep)),
        vm((zs, 4 * rd, width)), vm((zs, 4 * rq, 3 * local)), vm((zs, 4 * rd, width)),
        vm((rows, width)), vm((rows, width)), vm((group, width)), vm((width, group)), vm((group, 3 * local)),
        vm((pairs, 128, group)), vm((pairs, 128, group)), vm((1, group), jnp.int32),
        vm((pairs, 2, 1, group), F32), vm((128, group), F32),
        vm((group, local)), vm((rows, width)), vm((width, rows)), vm((rows, width), F32),
        vm((rows, width)), vm((width, rows)), vm((rows, width)),
        vm((rows, deep)), vm((4 * rd, rows)), vm((rows, deep)),
        vm((width // 128, rows, 128), F32),
        vm((2, TABLE, width)), vm((zs - 1, TABLE, width)), vm((TABLE, width)), vm((TABLE, width)),
        vm((TABLE, 1, width), F32), vm((TABLE, 1, width), F32), vm((zs - 1, TABLE, 1, width), F32),
        vm((TABLE, 1, width), F32), vm((TABLE, 1, width), F32), vm((TABLE, 1, width), F32),
        vm((3, TABLE, 1, width), F32),
        vm((zs, 2 * rd, width)), vm((zs, 2 * rd, local)), vm((zs, rd, local)),
        vm((zs - 1, rd, local)), vm((2, rd, local)),
        vm((zs, 2 * rq, deep)), vm((zs, 2 * rq, deep // 4)), vm((zs, rq, deep // 4)),
        vm((zs - 1, rq, deep // 4)), vm((2, rq, deep // 4)),
        vm((zs, rq, deep // 2)), vm((zs - 1, rq, deep // 2)), vm((2, rq, deep // 2)),
        vm((zs, 2 * rq, width)), vm((zs, rq, width)), vm((zs - 1, rq, width)), vm((2, rq, width)),
        vm((zs, 2 * rq, 3 * local)), vm((zs, rq, 3 * local)), vm((zs - 1, rq, 3 * local)),
        vm((2, rq, 3 * local)),
        pltpu.SemaphoreType.DMA((NEAR_COUNT,)),
        pltpu.SemaphoreType.DMA((FAR_COUNT,)),
        pltpu.SemaphoreType.DMA((FAR_COUNT,)),
    ]
    here = pl.BlockSpec(memory_space=pltpu.VMEM)
    away = pl.BlockSpec(memory_space=pl.ANY)
    return pl.pallas_call(
        fused_kernel,
        out_shape=(
            jax.ShapeDtypeStruct((rows, width), BF),
            jax.ShapeDtypeStruct((rows, width), F32),
            jax.ShapeDtypeStruct((rq, 3 * width), F32),
            jax.ShapeDtypeStruct((rq, width), F32),
            jax.ShapeDtypeStruct((rq, deep), F32),
            jax.ShapeDtypeStruct((rd, width), F32),
            jax.ShapeDtypeStruct((TABLE, 1, width), F32),
        ),
        in_specs=[pl.BlockSpec(memory_space=pltpu.SMEM), here, away, away, away, away, away, away],
        out_specs=[here] * 7,
        scratch_shapes=scratch,
        compiler_params=pltpu.CompilerParams(
            collective_id=0, has_side_effects=True, vmem_limit_bytes=67_043_328
        ),
        name="block",
    )(lengths, table, tokens, cotangent, w_qkv, w_out, w_up, w_down)


def closing_kernel(*refs):
    given, table, taken = refs[:6], refs[6], refs[7:]
    d = lax.axis_index("dp")
    for source, there in zip(given, taken[:6]):
        there[...] = source[...]
    own, up = taken[6:14], taken[14]
    width = table.shape[2]
    rq, rd = own[0].shape[1], up.shape[1]
    rows = jnp.concatenate([table[i] for i in range(8)], axis=0)
    moved = pltpu.roll(rows, lax.rem(width - d * rq, width), 1)
    for i in range(8):
        own[i][...] = moved[i : i + 1, :rq]
    row = jnp.broadcast_to(table[BIAS_UP + lax.div(d * rd, width)], (8, width))
    moved = pltpu.roll(row, lax.rem(width - lax.rem(d * rd, width), width), 1)
    up[...] = moved[0:1, :rd]


def per_device(
    tokens, lengths, w_qkv, w_out, w_up, w_down, bias_q, bias_v, bias_out, bias_up, bias_down,
    gain_one, shift_one, gain_two, shift_two, cotangent,
):
    if not fused_fits(
        tokens, lengths, w_qkv, w_down, lax.axis_size("dp"), lax.axis_size("seq")
    ):
        return per_device_plain(
            tokens, lengths, w_qkv, w_out, w_up, w_down, bias_q, bias_v, bias_out, bias_up,
            bias_down, gain_one, shift_one, gain_two, shift_two, cotangent,
        )
    small = [bias_q, bias_v, gain_one, shift_one, bias_out, bias_down, gain_two, shift_two]
    results = fused(
        tokens, lengths, w_qkv, w_out, w_up, w_down, small, bias_up, cotangent
    )
    rq, rd = w_qkv.shape[0], w_down.shape[0]
    steps = 2

    def whole(shape):
        return pl.BlockSpec(shape, lambda i: (0,) * len(shape))

    cut = [pl.BlockSpec((a.shape[0] // steps, a.shape[1]), lambda i: (i, 0)) for a in results[:6]]
    out, gtok, gq, go, gu, gd, *own, up = pl.pallas_call(
        closing_kernel,
        grid=(steps,),
        out_shape=tuple(jax.ShapeDtypeStruct(a.shape, a.dtype) for a in results[:6])
        + (jax.ShapeDtypeStruct((1, rq), F32),) * 8 + (jax.ShapeDtypeStruct((1, rd), F32),),
        in_specs=cut + [whole(results[6].shape)],
        out_specs=cut + [whole((1, rq))] * 8 + [whole((1, rd))],
        name="closing",
    )(*results)
    own, up = [piece[0] for piece in own], up[0]
    return (
        out, gtok, gq, go, gu, gd,
        own[0], own[1], own[4], up, own[5], own[2], own[3], own[6], own[7],
    )


def solution(mesh):
    return jax.shard_map(
        per_device,
        mesh=mesh,
        in_specs=(
            P(("dp", "seq"), None),
            P("dp", None),
            P("dp", None),
            P("dp", None),
            P("dp", None),
            P("dp", None),
            P("dp"),
            P("dp"),
            P("dp"),
            P("dp"),
            P("dp"),
            P("dp"),
            P("dp"),
            P("dp"),
            P("dp"),
            P(("dp", "seq"), None),
        ),
        out_specs=(
            P(("dp", "seq"), None),
            P(("dp", "seq"), None),
            P("dp", None),
            P("dp", None),
            P("dp", None),
            P("dp", None),
            P("dp"),
            P("dp"),
            P("dp"),
            P("dp"),
            P("dp"),
            P("dp"),
            P("dp"),
            P("dp"),
            P("dp"),
        ),
        check_vma=False,
    )
```

```python
import jax
import jax.numpy as jnp
from jax import lax
from jax.experimental import pallas as pl
from jax.experimental.pallas import tpu as pltpu
from jax.sharding import PartitionSpec as P

HEAD_DIM = 64


EPSILON = 1e-05
MASKED = -1e30
SLOPE = 0.7978845608028654
CUBIC = 0.044715


def as_sent(array):
    return jax.tree.map(lambda a: a.astype(jnp.bfloat16) if a.dtype == jnp.float32 else a, array)


def dense(left, right):
    return jnp.dot(left, right, preferred_element_type=jnp.float32)


def dense_left(left, right):
    return lax.dot_general(
        left, right, (((0,), (0,)), ((), ())), preferred_element_type=jnp.float32
    )


def dense_right(left, right):
    return lax.dot_general(
        left, right, (((1,), (1,)), ((), ())), preferred_element_type=jnp.float32
    )


def norm_parts(value):
    mean = jnp.mean(value, axis=-1, keepdims=True)
    centred = value - mean
    inverse = lax.rsqrt(jnp.mean(centred * centred, axis=-1, keepdims=True) + EPSILON)
    return (centred * inverse, inverse)


def norm_back(grad, scaled, inverse, gain):
    shaped = grad * gain
    inner = jnp.mean(shaped * scaled, axis=-1, keepdims=True)
    return inverse * (shaped - jnp.mean(shaped, axis=-1, keepdims=True) - scaled * inner)


def gelu_value(value):
    return 0.5 * value * (1.0 + jnp.tanh(SLOPE * (value + CUBIC * value * value * value)))


def gelu_slope(value):
    bent = jnp.tanh(SLOPE * (value + CUBIC * value * value * value))
    return 0.5 * (1.0 + bent) + 0.5 * value * (1.0 - bent * bent) * SLOPE * (
        1.0 + 3.0 * CUBIC * value * value
    )


def per_device_plain(
    tokens,
    lengths,
    w_qkv,
    w_out,
    w_up,
    w_down,
    bias_q,
    bias_v,
    bias_out,
    bias_up,
    bias_down,
    gain_one,
    shift_one,
    gain_two,
    shift_two,
    cotangent,
):
    width = tokens.shape[1]
    rows = tokens.shape[0]
    pair = lax.axis_size("seq")
    rank = lax.axis_index("seq")
    group = rows * pair
    local = width // pair
    heads = local // HEAD_DIM
    scale = HEAD_DIM ** (-0.5)
    block = 512
    blocks = group // block
    whole = (
        lax.all_gather(w_qkv, "dp", axis=0, tiled=True),
        lax.all_gather(w_out, "dp", axis=0, tiled=True),
        lax.all_gather(w_up, "dp", axis=0, tiled=True),
        lax.all_gather(w_down, "dp", axis=0, tiled=True),
        lax.all_gather(bias_q, "dp", axis=0, tiled=True),
        lax.all_gather(bias_v, "dp", axis=0, tiled=True),
        lax.all_gather(bias_out, "dp", axis=0, tiled=True),
        lax.all_gather(bias_up, "dp", axis=0, tiled=True),
        lax.all_gather(bias_down, "dp", axis=0, tiled=True),
        lax.all_gather(gain_one, "dp", axis=0, tiled=True),
        lax.all_gather(shift_one, "dp", axis=0, tiled=True),
        lax.all_gather(gain_two, "dp", axis=0, tiled=True),
        lax.all_gather(shift_two, "dp", axis=0, tiled=True),
    )
    weight_qkv, weight_out, weight_up, weight_down = whole[0:4]
    add_q, add_v, add_out, add_up, add_down, scale_one, move_one, scale_two, move_two = [
        piece.astype(jnp.float32) for piece in whole[4:]
    ]
    slots = lengths.shape[1]
    position = jnp.arange(group, dtype=jnp.int32)
    ends = jnp.cumsum(lengths[0])
    segment = jnp.sum((position[:, None] >= ends[None, :]).astype(jnp.int32), axis=1)
    own_segment = lax.dynamic_slice_in_dim(segment, rank * rows, rows)
    valid = (own_segment < slots - 1)[:, None]
    inputs = tokens.astype(jnp.float32)
    scaled_one, inverse_one = norm_parts(inputs)
    first = (scaled_one * scale_one + move_one).astype(jnp.bfloat16)
    bias_qkv = jnp.concatenate([add_q, jnp.zeros_like(add_q), add_v])
    qkv = (dense(first, weight_qkv) + bias_qkv).astype(jnp.bfloat16)
    head_side = lax.all_to_all(
        qkv.reshape(rows, 3, pair, local), "seq", split_axis=2, concat_axis=0, tiled=True
    )
    query = head_side[:, 0, 0].reshape(group, heads, HEAD_DIM)
    keys = head_side[:, 1, 0].reshape(group, heads, HEAD_DIM)
    values = head_side[:, 2, 0].reshape(group, heads, HEAD_DIM)

    def block_scores(index):
        start = index * block
        query_rows = lax.dynamic_slice_in_dim(query, start, block)
        raw = (
            jnp.einsum("qhd,khd->hqk", query_rows, keys, preferred_element_type=jnp.float32) * scale
        )
        row_segment = lax.dynamic_slice_in_dim(segment, start, block)
        row_position = lax.dynamic_slice_in_dim(position, start, block)
        allowed = (row_segment[:, None] == segment[None, :]) & (
            position[None, :] <= row_position[:, None]
        )
        return (jnp.where(allowed[None], raw, MASKED), query_rows)

    def attend(index):
        scores, unused = block_scores(index)
        top = jnp.max(scores, axis=-1, keepdims=True)
        weights = jnp.exp(scores - top)
        total = jnp.sum(weights, axis=-1, keepdims=True)
        probs = (weights / total).astype(jnp.bfloat16)
        mixed_rows = jnp.einsum("hqk,khd->qhd", probs, values, preferred_element_type=jnp.float32)
        return (
            mixed_rows.reshape(block, local).astype(jnp.bfloat16),
            (top + jnp.log(total))[:, :, 0],
        )

    mixed_blocks, log_totals = lax.map(attend, jnp.arange(blocks))
    mixed_head = mixed_blocks.reshape(group, 1, local)
    mixed = lax.all_to_all(mixed_head, "seq", split_axis=0, concat_axis=1, tiled=True).reshape(
        rows, width
    )
    middle = inputs + dense(mixed, weight_out) + add_out
    scaled_two, inverse_two = norm_parts(middle)
    second = (scaled_two * scale_two + move_two).astype(jnp.bfloat16)
    pre = dense(second, weight_up) + add_up
    hidden = gelu_value(pre).astype(jnp.bfloat16)
    result = middle + dense(hidden, weight_down) + add_down
    block_out = jnp.where(valid, result, 0.0).astype(jnp.bfloat16)
    grad_out = jnp.where(valid, cotangent, jnp.zeros_like(cotangent))
    grad_weight_down = dense_left(hidden, grad_out)
    grad_add_down = jnp.sum(grad_out.astype(jnp.float32), axis=0)
    grad_pre = (dense_right(grad_out, weight_down) * gelu_slope(pre)).astype(jnp.bfloat16)
    grad_weight_up = dense_left(second, grad_pre)
    grad_add_up = jnp.sum(grad_pre.astype(jnp.float32), axis=0)
    grad_second = dense_right(grad_pre, weight_up)
    grad_scale_two = jnp.sum(grad_second * scaled_two, axis=0)
    grad_move_two = jnp.sum(grad_second, axis=0)
    grad_middle = grad_out.astype(jnp.float32) + norm_back(
        grad_second, scaled_two, inverse_two, scale_two
    )
    grad_attn = grad_middle.astype(jnp.bfloat16)
    grad_weight_out = dense_left(mixed, grad_attn)
    grad_add_out = jnp.sum(grad_attn.astype(jnp.float32), axis=0)
    grad_mixed = dense_right(grad_attn, weight_out).astype(jnp.bfloat16)
    branch_grads = (
        grad_weight_out,
        grad_weight_up,
        grad_weight_down,
        grad_add_out,
        grad_add_up,
        grad_add_down,
        grad_scale_two,
        grad_move_two,
    )
    grad_head = lax.all_to_all(
        grad_mixed.reshape(rows, pair, local), "seq", split_axis=1, concat_axis=0, tiled=True
    )
    grad_head = grad_head.reshape(group, heads, HEAD_DIM)

    def attend_back(carry, index):
        grad_keys, grad_values = carry
        scores, query_rows = block_scores(index)
        probs = jnp.exp(scores - log_totals[index][:, :, None])
        grad_rows = lax.dynamic_slice_in_dim(grad_head, index * block, block)
        grad_probs = jnp.einsum(
            "qhd,khd->hqk", grad_rows, values, preferred_element_type=jnp.float32
        )
        centre = jnp.sum(probs * grad_probs, axis=-1, keepdims=True)
        grad_scores = (probs * (grad_probs - centre)).astype(jnp.bfloat16)
        grad_values = grad_values + jnp.einsum(
            "hqk,qhd->khd",
            probs.astype(jnp.bfloat16),
            grad_rows,
            preferred_element_type=jnp.float32,
        )
        grad_keys = (
            grad_keys
            + jnp.einsum(
                "hqk,qhd->khd", grad_scores, query_rows, preferred_element_type=jnp.float32
            )
            * scale
        )
        grad_query = (
            jnp.einsum("hqk,khd->qhd", grad_scores, keys, preferred_element_type=jnp.float32)
            * scale
        )
        return ((grad_keys, grad_values), grad_query)

    empty = jnp.zeros((group, heads, HEAD_DIM), jnp.float32)
    (grad_keys, grad_values), grad_queries = lax.scan(
        attend_back, (empty, empty), jnp.arange(blocks)
    )
    grad_side = jnp.stack(
        [
            grad_queries.reshape(group, local),
            grad_keys.reshape(group, local),
            grad_values.reshape(group, local),
        ],
        axis=1,
    ).astype(jnp.bfloat16)
    grad_qkv = lax.all_to_all(
        grad_side.reshape(group, 3, 1, local), "seq", split_axis=0, concat_axis=2, tiled=True
    )
    grad_qkv = grad_qkv.reshape(rows, 3 * width)
    grad_weight_qkv = dense_left(first, grad_qkv)
    column_sums = jnp.sum(grad_qkv.astype(jnp.float32), axis=0)
    grad_add_q = column_sums[:width]
    grad_add_v = column_sums[2 * width :]
    grad_first = dense_right(grad_qkv, weight_qkv)
    grad_scale_one = jnp.sum(grad_first * scaled_one, axis=0)
    grad_move_one = jnp.sum(grad_first, axis=0)
    grad_tokens = grad_middle + norm_back(grad_first, scaled_one, inverse_one, scale_one)
    stem_grads = (grad_weight_qkv, grad_add_q, grad_add_v, grad_scale_one, grad_move_one)
    halves = lax.psum_scatter(
        stem_grads + branch_grads, ("dp", "seq"), scatter_dimension=0, tiled=True
    )
    shares = jax.tree.map(
        lambda part, own: part.astype(own.dtype),
        lax.all_gather(as_sent(halves), "seq", axis=0, tiled=True),
        halves,
    )
    stem_shares = shares[0:5]
    branch_shares = shares[5:13]
    return (
        block_out,
        grad_tokens,
        stem_shares[0],
        branch_shares[0],
        branch_shares[1],
        branch_shares[2],
        stem_shares[1],
        stem_shares[2],
        branch_shares[3],
        branch_shares[4],
        branch_shares[5],
        stem_shares[3],
        stem_shares[4],
        branch_shares[6],
        branch_shares[7],
    )


FAR = pl.DeviceIdType.MESH
NT = (((1,), (1,)), ((), ()))
BF = jnp.bfloat16
F32 = jnp.float32


def mul(left, right):
    return jnp.dot(left, right, preferred_element_type=F32)


def mul_nt(left, right):
    return lax.dot_general(left, right, NT, preferred_element_type=F32)


def flat(blocks):
    return blocks.reshape(blocks.shape[0] * blocks.shape[1], blocks.shape[2])


def normed(value):
    width = value.shape[1]
    mean = jnp.sum(value, axis=1, keepdims=True) * (1.0 / width)
    centred = value - mean
    spread = jnp.sum(centred * centred, axis=1, keepdims=True) * (1.0 / width)
    inverse = lax.rsqrt(spread + EPSILON)
    return (centred * inverse, inverse)


def normed_back(grad, scaled, inverse, gain):
    width = grad.shape[1]
    shaped = grad * gain
    inner = jnp.sum(shaped * scaled, axis=1, keepdims=True) * (1.0 / width)
    outer = jnp.sum(shaped, axis=1, keepdims=True) * (1.0 / width)
    return inverse * (shaped - outer - scaled * inner)


def column_sum(value):
    return jnp.sum(value, axis=0, keepdims=True)


class Numbers:
    def __init__(self):
        self.used = 0

    def take(self, count):
        start = self.used
        self.used = start + count
        return start


BIAS_Q, BIAS_V, GAIN_1, SHIFT_1, BIAS_OUT, BIAS_DOWN, GAIN_2, SHIFT_2, BIAS_UP = range(9)
TABLE = 16
FAR_COUNT = 240
NEAR_COUNT = 32


def fused_kernel(
    lengths, table, tok_own, cot, own_q, own_o, own_u, own_d,
    out, gtok, out_q, out_o, out_u, out_d, out_v,
    wq, wo, wu, wd, gwq, gwd,
    tok, tok_far, first, first_t, qkv, k_t, v_t, lower, lse, o_t,
    mixed_near, mixed, mixed_t, middle, second, second_t, gout,
    hidden, hidden_t, slope, pieces,
    e_own, e_z, e_y, e_c, vec, gvec, v_z, v_y, v_c, v_x, v_sum,
    r1_d, rx_d, ry_d, rz_d, r5_d, r1_u, rx_u, ry_u, rz_u, r5_u,
    r2_u, r3_u, r4_u, r1_o, r2_o, r3_o, r4_o, r1_q, r2_q, r3_q, r5_q,
    near_sem, send_sem, recv_sem,
):
    d = lax.axis_index("dp")
    s = lax.axis_index("seq")
    z = lax.div(d, 4)
    y = lax.rem(lax.div(d, 2), 2)
    c = lax.rem(d, 2)
    zs = wq.shape[0]
    rows, width = tok_own.shape
    group = 2 * rows
    local = width // 2
    pairs = local // 128
    rq = width // (4 * zs)
    rd = own_d.shape[0]
    tile = 4 * rd
    tiles = zs
    z_peers = [(lax.rem(z + dz, zs) * 4 + y * 2 + c, s) for dz in range(1, zs)]
    y_peer = (z * 4 + (1 - y) * 2 + c, s)
    c_peer = (z * 4 + y * 2 + (1 - c), s)
    x_peer = (d, 1 - s)
    number = Numbers()
    local_number = Numbers()

    def far(src, dst, slot, device):
        return pltpu.make_async_remote_copy(
            src_ref=src, dst_ref=dst, send_sem=send_sem.at[slot], recv_sem=recv_sem.at[slot],
            device_id=device, device_id_type=FAR,
        )

    far_w, far_g = far, far

    def z_at(dz):
        return lax.rem(z + zs - dz, zs)

    def loop(count, body):
        lax.fori_loop(0, count, lambda i, carry: (body(i), carry)[1], 0)

    def block_rows(r, yy, cc):
        return pl.ds(pl.multiple_of((yy * 2 + cc) * r, r), r)

    barrier = pltpu.get_barrier_semaphore()
    everyone = z_peers + [y_peer, c_peer, x_peer]
    for peer in everyone:
        pl.semaphore_signal(barrier, inc=1, device_id=peer, device_id_type=FAR)
    pl.semaphore_wait(barrier, len(everyone))

    class Gather:
        def __init__(self, ref, r, columns, base, own=None, columns_at=None):
            self.ref, self.r, self.columns, self.base, self.own = ref, r, columns, base, own
            self.columns_at = columns_at

        def part(self, zz, yy, cc):
            return self.ref.at[zz, block_rows(self.r, yy, cc), self.columns]

        def layer(self, yy, cc, columns=None):
            columns = self.columns if columns is None else columns
            return self.ref.at[:, block_rows(self.r, yy, cc), columns]

        def z_copy(self, dz):
            columns = self.columns if self.columns_at is None else self.columns_at(dz)
            there = self.ref.at[z, block_rows(self.r, y, c), columns]
            here = there if self.own is None else self.own.at[:, columns]
            return far_w(here, there, self.base + dz - 1, z_peers[dz - 1])

        def z_start(self):
            for dz in range(1, zs):
                self.z_copy(dz).start()

        def z_wait(self):
            for dz in range(1, zs):
                block = self.part(z_at(dz), y, c)
                far_w(block, block, self.base + dz - 1, z_peers[dz - 1]).wait_recv()

        def y_copy(self, yy):
            return far_w(self.layer(yy, c), self.layer(yy, c), self.base + zs - 1, y_peer)

        def c_copy(self, yy, cc, other):
            return far_w(self.layer(yy, cc), self.layer(yy, cc), self.base + zs + other, c_peer)

        def relay(self, *following):
            self.z_wait()
            for other in following:
                other.z_start()
            self.y_copy(y).start()
            self.c_copy(y, c, 0).start()

        def relay_y(self):
            self.y_copy(1 - y).wait_recv()
            self.c_copy(1 - y, c, 1).start()

        def finish(self):
            self.c_copy(y, 1 - c, 0).wait_recv()
            self.c_copy(1 - y, 1 - c, 1).wait_recv()

        def sent(self):
            for dz in range(1, zs):
                self.z_copy(dz).wait_send()
            self.y_copy(y).wait_send()
            self.c_copy(y, c, 0).wait_send()
            self.c_copy(1 - y, c, 1).wait_send()

    class GatherHalf(Gather):
        def __init__(self, ref, r, columns, others, base, own):
            super().__init__(ref, r, columns, base, own)
            self.others = others

        def x_copy(self, yy, columns, other):
            block = self.layer(yy, c, columns)
            return far_w(block, block, self.base + zs + 2 + other, x_peer)

        def c_other(self, yy, cc, other):
            block = self.layer(yy, cc, self.others)
            return far_w(block, block, self.base + zs + 4 + other, c_peer)

        def push_x(self):
            self.x_copy(y, self.columns, 0).start()

        def relay_y(self):
            super().relay_y()
            self.x_copy(1 - y, self.columns, 1).start()

        def relay_x(self):
            self.x_copy(y, self.others, 0).wait_recv()
            self.c_other(y, c, 0).start()
            self.x_copy(1 - y, self.others, 1).wait_recv()
            self.c_other(1 - y, c, 1).start()

        def finish(self):
            super().finish()
            self.c_other(y, 1 - c, 0).wait_recv()
            self.c_other(1 - y, 1 - c, 1).wait_recv()

        def sent(self):
            super().sent()
            self.x_copy(y, self.columns, 0).wait_send()
            self.x_copy(1 - y, self.columns, 1).wait_send()
            self.c_other(y, c, 0).wait_send()
            self.c_other(1 - y, c, 1).wait_send()

    steps = zs + 2
    base_q = number.take(pairs * steps)

    def gather_q(p):
        return Gather(wq, rq, pl.ds(pl.multiple_of(p * local, 128), local), base_q + p * steps)

    gather_o = Gather(wo, rq, pl.ds(0, width), number.take(steps), own_o)
    base_gu = number.take(tiles * steps)

    def tile_lanes(t):
        return pl.ds(pl.multiple_of(t * tile, 128), tile)

    def turn(i, zz):
        return lax.rem(zz + i + 1, zs)

    def gather_u(i):
        return Gather(
            wu, rq, tile_lanes(turn(i, z)), base_gu + i * steps, own_u,
            lambda dz: tile_lanes(turn(i, lax.rem(z + dz, zs))),
        )

    cuts = local // 128
    base_gd = number.take(cuts * (zs + 6))

    def gather_d(i):
        mine = pl.ds(pl.multiple_of(s * local + i * 128, 128), 128)
        others = pl.ds(pl.multiple_of((1 - s) * local + i * 128, 128), 128)
        return GatherHalf(wd, rd, mine, others, base_gd + i * (zs + 6), own_d)

    near_q = []
    for p in range(pairs):
        for part in range(3):
            start = pl.multiple_of(part * width + s * local + p * 128, 128)
            near_q.append(
                pltpu.make_async_copy(
                    own_q.at[:, pl.ds(start, 128)],
                    wq.at[z, block_rows(rq, y, c), pl.ds(p * local + part * 128, 128)],
                    near_sem.at[local_number.take(1)],
                )
            )
    near_rest = []
    half = pl.ds(pl.multiple_of(s * local, 128), local)
    for own, there in (
        (own_o, wo.at[z, block_rows(rq, y, c), :]),
        (own_u, wu.at[z, block_rows(rq, y, c), :]),
        (own_d.at[:, half], wd.at[z, block_rows(rd, y, c), half]),
    ):
        near_rest.append(
            pltpu.make_async_copy(own, there, near_sem.at[local_number.take(1)])
        )
    near_cot = pltpu.make_async_copy(cot, gout, near_sem.at[local_number.take(1)])
    near_tok = pltpu.make_async_copy(tok_own, tok, near_sem.at[local_number.take(1)])
    for copy in near_q + [near_tok] + near_rest + [near_cot]:
        copy.start()

    base_e = number.take(zs + 1)
    for dz in range(1, zs):
        far(table, e_z.at[dz - 1], base_e + dz - 1, z_peers[dz - 1]).start()
    send_tok = far(tok_own, tok_far, number.take(1), x_peer)
    send_tok.start()
    for copy in near_q:
        copy.wait()
    for p in range(pairs):
        gather_q(p).z_start()

    for dz in range(1, zs):
        far(table, e_z.at[dz - 1], base_e + dz - 1, z_peers[dz - 1]).wait_recv()
    total = table[...].astype(F32)
    for dz in range(1, zs):
        total = total + e_z[dz - 1].astype(F32)
    e_own[0] = total.astype(BF)
    y_table = far(e_own.at[0], e_y, base_e + zs - 1, y_peer)
    y_table.start()
    gather_q(0).relay(gather_o)

    ends = []
    end = jnp.int32(0)
    for j in range(lengths.shape[1]):
        end = end + lengths[0, j]
        ends.append(end)
    position = lax.broadcasted_iota(jnp.int32, (1, group), 1)
    start = jnp.zeros((1, group), jnp.int32)
    for end in ends[:-1]:
        start = jnp.where(position >= end, end, start)
    lower[...] = start
    last_valid = ends[-2]

    y_table.wait_recv()
    total = total + e_y[...].astype(F32)
    e_own[1] = total.astype(BF)
    c_table = far(e_own.at[1], e_c, base_e + zs, c_peer)
    c_table.start()
    gather_q(1).relay(gather_d(0))
    c_table.wait_recv()
    total = total + e_c[...].astype(F32)
    for i in range(TABLE):
        vec[i] = total[i : i + 1, :]

    def first_norm(source, at):
        def body(i):
            x = source[pl.ds(pl.multiple_of(i * 128, 128), 128), :].astype(F32)
            scaled, unused = normed(x)
            value = (scaled * vec[GAIN_1] + vec[SHIFT_1]).astype(BF)
            there = pl.ds(pl.multiple_of(at + i * 128, 128), 128)
            first[there, :] = value
            first_t[:, there] = value.T

        loop(rows // 128, body)

    near_tok.wait()
    first_norm(tok, s * rows)

    base_mixed = number.take(pairs)
    near_mixed = local_number.take(pairs)

    def lanes(p, part):
        return pl.ds(pl.multiple_of(p * local + part * 128, 128), 128)

    def send_mixed(p):
        there = pl.ds(pl.multiple_of(s * local + p * 128, 128), 128)
        here = pl.ds(pl.multiple_of(p * 128, 128), 128)
        away = pl.ds(pl.multiple_of((1 - s) * rows, 128), rows)
        return far(mixed_near.at[away, here], mixed.at[:, there], base_mixed + p, x_peer)

    def keep_mixed(p):
        there = pl.ds(pl.multiple_of(s * local + p * 128, 128), 128)
        here = pl.ds(pl.multiple_of(p * 128, 128), 128)
        stay = pl.ds(pl.multiple_of(s * rows, 128), rows)
        return pltpu.make_async_copy(
            mixed_near.at[stay, here], mixed.at[:, there], near_sem.at[near_mixed + p]
        )

    side = 256
    blocks = group // side
    key_at = lax.broadcasted_iota(jnp.int32, (side, side), 0)
    query_at = lax.broadcasted_iota(jnp.int32, (side, side), 1)
    lane = lax.broadcasted_iota(jnp.int32, (side, 128), 1)

    def head_lanes(value, h):
        inside = (lane >= h * HEAD_DIM) & (lane < h * HEAD_DIM + HEAD_DIM)
        return jnp.where(inside, value, 0.0).astype(BF)

    def scores(p, keys_block, query, qi, j):
        raw = mul_nt(keys_block, query)
        ok = key_at + j * side >= lower[:, qi * side : (qi + 1) * side]
        if j == qi:
            ok = ok & (key_at <= query_at)
        return jnp.where(ok, raw, MASKED)

    scale = HEAD_DIM ** (-0.5)

    def pass_on(k):
        @pl.when(k == 0)
        def _():
            gather_o.relay(gather_d(2))

        @pl.when(k == 2)
        def _():
            gather_d(0).relay(gather_u(0))
            gather_d(0).push_x()
            gather_o.relay_y()

        @pl.when(k == 3)
        def _():
            gather_d(1).relay(gather_u(1))
            gather_d(1).push_x()

        @pl.when(k == 4)
        def _():
            gather_d(2).relay(gather_u(2))

    def attend(p):
        def head(h):
            half = pl.ds(pl.multiple_of(h * HEAD_DIM, HEAD_DIM), HEAD_DIM)
            for qi in range(blocks):
                query = head_lanes(
                    qkv[qi * side : (qi + 1) * side, lanes(p, 0)].astype(F32) * scale, h
                )
                raw = []
                top = None
                for j in range(qi + 1):
                    block = scores(p, qkv[j * side : (j + 1) * side, lanes(p, 1)], query, qi, j)
                    raw.append(block)
                    high = jnp.max(block, axis=0, keepdims=True)
                    top = high if top is None else jnp.maximum(top, high)
                amount = jnp.zeros((1, side), F32)
                gathered = jnp.zeros((HEAD_DIM, side), F32)
                for j in range(qi + 1):
                    weight = jnp.exp(raw[j] - top)
                    amount = amount + column_sum(weight)
                    gathered = gathered + mul(
                        v_t[p, half, j * side : (j + 1) * side], weight.astype(BF)
                    )
                o_t[half, qi * side : (qi + 1) * side] = gathered / amount
                lse[p, h, :, qi * side : (qi + 1) * side] = top + jnp.log(amount)
            pass_on(p * 2 + h)

        loop(2, head)
        here = pl.ds(pl.multiple_of(p * 128, 128), 128)
        for qi in range(blocks):
            at = slice(qi * side, (qi + 1) * side)
            mixed_near[at, here] = o_t[:, at].T.astype(BF)

    def project(p, at_row):
        zero = jnp.zeros((1, 128), F32)
        there = pl.ds(pl.multiple_of(s * local + p * 128, 128), 128)
        bias = jnp.concatenate([vec[BIAS_Q, :, there], zero, vec[BIAS_V, :, there]], axis=1)
        weight = flat(wq[:, :, pl.ds(pl.multiple_of(p * local, 128), local)])

        def body(i):
            at = pl.ds(pl.multiple_of(at_row + i * side, side), side)
            value = (mul(first[at, :], weight) + bias).astype(BF)
            qkv[at, pl.ds(pl.multiple_of(p * local, 128), local)] = value
            k_t[p, :, at] = value[:, 128:256].T
            v_t[p, :, at] = value[:, 256:384].T

        loop(rows // side, body)

    gather_q(0).relay_y()
    gather_q(2).relay(gather_d(1))
    gather_q(0).finish()
    project(0, s * rows)
    gather_q(1).relay_y()
    for copy in near_rest:
        copy.wait()
    gather_q(2).relay_y()
    send_tok.wait_recv()
    first_norm(tok_far, (1 - s) * rows)

    def pair_forward(p):
        @pl.when(p > 0)
        def _():
            gather_q(p).finish()
            project(p, s * rows)

        project(p, (1 - s) * rows)
        attend(p)
        send_mixed(p).start()
        keep_mixed(p).start()

    loop(pairs, pair_forward)
    gather_d(0).relay_y()
    gather_d(1).relay_y()
    gather_d(2).push_x()
    gather_u(0).relay(gather_u(3))
    gather_d(2).relay_y()

    gather_o.finish()
    near_cot.wait()
    for p in range(pairs):
        keep_mixed(p).wait()
    for p in range(pairs):
        far(
            mixed_near.at[pl.ds(0, rows), pl.ds(0, 128)],
            mixed.at[:, pl.ds(pl.multiple_of((1 - s) * local + p * 128, 128), 128)],
            base_mixed + p, x_peer,
        ).wait_recv()

    def project_out(i):
        at = pl.ds(pl.multiple_of(i * 128, 128), 128)
        near = mixed[at, :]
        mixed_t[:, at] = near.T
        value = tok[at, :].astype(F32) + mul(near, flat(wo[...])) + vec[BIAS_OUT]
        middle[at, :] = value
        scaled, unused = normed(value)
        rounded = (scaled * vec[GAIN_2] + vec[SHIFT_2]).astype(BF)
        second[at, :] = rounded
        second_t[:, at] = rounded.T
        spot = s * rows + i * 128 + lax.broadcasted_iota(jnp.int32, (128, width), 0)
        gout[at, :] = jnp.where(spot < last_valid, gout[at, :].astype(F32), 0.0).astype(BF)

    loop(rows // 128, project_out)
    for p in range(pairs):
        send_mixed(p).wait_send()
    gather_d(0).relay_x()
    gather_u(1).relay()
    gather_u(0).relay_y()


    base_sib = number.take(tiles * 2)
    base_dx = number.take(tiles * 2)
    base_zd = number.take(zs - 1)
    base_xs = number.take(1)
    mine = pl.ds(pl.multiple_of(s * local, 128), local)
    others = pl.ds(pl.multiple_of((1 - s) * local, 128), local)

    def rows_y(r, yy):
        return pl.ds(pl.multiple_of(yy * r, r), r)

    def sib_d(t, yy):
        return far_g(
            gwd.at[t, block_rows(rd, yy, 1 - c), :], r1_d.at[t, rows_y(rd, yy), :],
            base_sib + t * 2 + yy, c_peer,
        )

    def sib_start_d(t):
        for yy in range(2):
            sib_d(t, yy).start()

    def x_d(t):
        return far_g(r1_d.at[t, :, others], rx_d.at[t], base_dx + t * 2, x_peer)

    def x_start_d(t):
        for yy in range(2):
            sib_d(t, yy).wait_recv()
            at = rows_y(rd, yy)
            r1_d[t, at, :] = (
                r1_d[t, at, :].astype(F32) + gwd[t, block_rows(rd, yy, c), :].astype(F32)
            ).astype(BF)
        x_d(t).start()

    def y_d(t):
        return far_g(rx_d.at[t, rows_y(rd, 1 - y), :], ry_d.at[t], base_dx + t * 2 + 1, y_peer)

    def y_start_d(t):
        x_d(t).wait_recv()
        rx_d[t] = (rx_d[t].astype(F32) + r1_d[t, :, mine].astype(F32)).astype(BF)
        y_d(t).start()

    def z_d(t, dz):
        return far_g(ry_d.at[t], rz_d.at[dz - 1], base_zd + dz - 1, (t * 4 + y * 2 + c, s))

    def z_start_d(t):
        y_d(t).wait_recv()
        ry_d[t] = (ry_d[t].astype(F32) + rx_d[t, rows_y(rd, y), :].astype(F32)).astype(BF)
        dz = lax.rem(t + zs - z, zs)

        @pl.when(dz > 0)
        def _():
            z_d(t, dz).start()

    class Pooled:
        def __init__(self, ref, start, span, parts, base):
            self.ref, self.base = ref, base
            self.r1, self.rx, self.ry, self.rz, self.r5 = parts
            half = span // 2
            self.full = pl.ds(pl.multiple_of(start, 128), span)
            self.mine = pl.ds(pl.multiple_of(start + s * half, 128), half)
            self.others = pl.ds(pl.multiple_of(start + (1 - s) * half, 128), half)
            self.narrow = pl.ds(pl.multiple_of((start - early * span) // 2, 128), half)

        def sib(self, yy):
            return far_g(
                self.ref.at[:, block_rows(rq, yy, 1 - c), self.full],
                self.r1.at[:, rows_y(rq, yy), self.full], self.base + yy, c_peer,
            )

        def sib_start(self):
            for yy in range(2):
                self.sib(yy).start()

        def along_x(self):
            return far_g(
                self.r1.at[:, :, self.others], self.rx.at[:, :, self.narrow], self.base + 2, x_peer
            )

        def x_start(self):
            for yy in range(2):
                self.sib(yy).wait_recv()
                at = rows_y(rq, yy)
                for zz in range(zs):
                    self.r1[zz, at, self.full] = (
                        self.r1[zz, at, self.full].astype(F32)
                        + self.ref[zz, block_rows(rq, yy, c), self.full].astype(F32)
                    ).astype(BF)
            self.along_x().start()

        def along_y(self):
            return far_g(
                self.rx.at[:, rows_y(rq, 1 - y), self.narrow], self.ry.at[:, :, self.narrow],
                self.base + 3, y_peer,
            )

        def y_start(self):
            self.along_x().wait_recv()
            for zz in range(zs):
                self.rx[zz, :, self.narrow] = (
                    self.rx[zz, :, self.narrow].astype(F32)
                    + self.r1[zz, :, self.mine].astype(F32)
                ).astype(BF)
            self.along_y().start()

        def along_z(self, dz):
            return far_g(
                self.ry.at[lax.rem(z + dz, zs), :, self.narrow],
                self.rz.at[dz - 1, :, self.narrow], self.base + 3 + dz, z_peers[dz - 1],
            )

        def z_start(self):
            self.along_y().wait_recv()
            at = rows_y(rq, y)
            for zz in range(zs):
                self.ry[zz, :, self.narrow] = (
                    self.ry[zz, :, self.narrow].astype(F32)
                    + self.rx[zz, at, self.narrow].astype(F32)
                ).astype(BF)
            for dz in range(1, zs):
                self.along_z(dz).start()

        def swap(self, half):
            block = self.r5.at[half, :, self.narrow]
            return far_g(block, block, self.base + 3 + zs, x_peer)

        def finish(self):
            total = self.ry[z, :, self.narrow].astype(F32)
            for dz in range(1, zs):
                self.along_z(dz).wait_recv()
                total = total + self.rz[dz - 1, :, self.narrow].astype(F32)
            self.r5[s, :, self.narrow] = total.astype(BF)
            self.swap(s).start()

        def sent(self):
            for yy in range(2):
                self.sib(yy).wait_send()
            self.along_x().wait_send()
            self.along_y().wait_send()
            for dz in range(1, zs):
                self.along_z(dz).wait_send()
            self.swap(s).wait_send()

    class Spread:
        def __init__(self, ref, columns, r1, r2, r3, base):
            self.ref, self.columns, self.r1, self.r2, self.r3 = ref, columns, r1, r2, r3
            self.base = base

        def sib(self, yy):
            return far_g(
                self.ref.at[:, block_rows(rq, yy, 1 - c), self.columns],
                self.r1.at[:, pl.ds(pl.multiple_of(yy * rq, rq), rq), self.columns],
                self.base + yy, c_peer,
            )

        def sib_start(self):
            self.sib(1 - y).start()
            self.sib(y).start()

        def along_y(self):
            return far_g(
                self.r1.at[:, pl.ds(pl.multiple_of((1 - y) * rq, rq), rq), self.columns],
                self.r2.at[:, :, self.columns], self.base + 2, y_peer,
            )

        def y_start(self):
            self.sib(1 - y).wait_recv()
            at = pl.ds(pl.multiple_of((1 - y) * rq, rq), rq)
            for zz in range(zs):
                self.r1[zz, at, self.columns] = (
                    self.r1[zz, at, self.columns].astype(F32)
                    + self.ref[zz, block_rows(rq, 1 - y, c), self.columns].astype(F32)
                ).astype(BF)
            self.along_y().start()

        def along_z(self, dz):
            return far_g(
                self.r2.at[lax.rem(z + dz, zs), :, self.columns],
                self.r3.at[dz - 1, :, self.columns], self.base + 2 + dz, z_peers[dz - 1],
            )

        def z_start(self):
            self.sib(y).wait_recv()
            self.along_y().wait_recv()
            at = pl.ds(pl.multiple_of(y * rq, rq), rq)
            for zz in range(zs):
                self.r2[zz, :, self.columns] = (
                    self.r2[zz, :, self.columns].astype(F32)
                    + self.r1[zz, at, self.columns].astype(F32)
                    + self.ref[zz, block_rows(rq, y, c), self.columns].astype(F32)
                ).astype(BF)
            for dz in range(1, zs):
                self.along_z(dz).start()

        def z_finish(self):
            total = self.r2[z, :, self.columns].astype(F32)
            for dz in range(1, zs):
                self.along_z(dz).wait_recv()
                total = total + self.r3[dz - 1, :, self.columns].astype(F32)
            return total

        def sent(self):
            self.sib(0).wait_send()
            self.sib(1).wait_send()
            self.along_y().wait_send()
            for dz in range(1, zs):
                self.along_z(dz).wait_send()

    def swap(parts, columns, slot):
        return far_g(parts.at[0, :, columns], parts.at[1, :, columns], slot, x_peer)

    early = tiles // 2
    spread_steps = zs + 2
    base_su = number.take(early * (spread_steps + 1))

    def sum_e(t):
        return Spread(
            wu, tile_lanes(t), r1_u, r2_u, r3_u, base_su + t * (spread_steps + 1)
        )

    def swap_e(t):
        return swap(r4_u, tile_lanes(t), base_su + t * (spread_steps + 1) + spread_steps)

    def finish_e(t):
        r4_u[0, :, tile_lanes(t)] = sum_e(t).z_finish().astype(BF)
        swap_e(t).start()

    whole = pl.ds(0, width)
    sum_o = Spread(wo, whole, r1_o, r2_o, r3_o, number.take(spread_steps))
    swap_o = swap(r4_o, whole, number.take(1))

    def finish_o():
        r4_o[0] = sum_o.z_finish().astype(BF)
        swap_o.start()

    pooled_steps = zs + 4
    base_pu = number.take(tiles * pooled_steps)

    def sum_u(t):
        return Pooled(wu, t * tile, tile, (r1_u, rx_u, ry_u, rz_u, r5_u), base_pu + t * pooled_steps)

    def pass_up(k):
        @pl.when(k == 0)
        def _():
            gather_d(1).relay_x()

        @pl.when(k == 1)
        def _():
            gather_u(2).relay()
            gather_u(1).relay_y()

        @pl.when(k == 2)
        def _():
            x_start_d(turn(0, z))

        @pl.when(k == 3)
        def _():
            gather_u(3).relay()
            gather_u(2).relay_y()

        @pl.when(k == 4)
        def _():
            gather_d(2).relay_x()
            x_start_d(turn(1, z))

        @pl.when(k == 5)
        def _():
            gather_u(3).relay_y()

        @pl.when(k == 6)
        def _():
            x_start_d(turn(2, z))

    def weigh_down(t):
        def part(m):
            at = pl.ds(pl.multiple_of(m * 2 * rd, 2 * rd), 2 * rd)
            gwd[t, at, :] = mul(hidden_t[at, :], gout[...]).astype(BF)

        loop(2, part)
        sib_start_d(t)

    def feed(i):
        t = turn(i, z)
        gather_u(i).finish()
        at = tile_lanes(t)
        pre = mul(second[...], flat(wu[:, :, at])) + vec[BIAS_UP + t]
        square = pre * pre
        bent = 0.5 * jnp.tanh(pre * (SLOPE + (SLOPE * CUBIC) * square)) + 0.5
        value = pre * bent
        bend = bent + value * (1.0 - bent) * (2.0 * SLOPE + (6.0 * SLOPE * CUBIC) * square)
        rounded = value.astype(BF)
        hidden[:, at] = rounded
        hidden_t[...] = rounded.T
        slope[:, at] = bend.astype(BF)
        pass_up(i * 2)

        @pl.when(i < tiles - 1)
        def _():
            weigh_down(t)

        pass_up(i * 2 + 1)

    loop(tiles, feed)
    for i in range(cuts):
        gather_d(i).finish()

    def slopes_back(t):
        at = tile_lanes(t)
        grad = (mul_nt(gout[...], wd[t]) * slope[:, at].astype(F32)).astype(BF)
        slope[:, at] = grad
        gvec[BIAS_UP + t] = column_sum(grad.astype(F32))

    loop(tiles, slopes_back)
    y_start_d(turn(0, z))

    def grow(i):
        at = pl.ds(pl.multiple_of(i * side, side), side)
        gtok[at, :] = mul_nt(slope[at, :], flat(wu[...]))

    loop(rows // side, grow)
    y_start_d(turn(1, z))

    for row in (BIAS_Q, BIAS_V, BIAS_OUT, BIAS_DOWN, GAIN_1, SHIFT_1, GAIN_2, SHIFT_2):
        gvec[row] = jnp.zeros((1, width), F32)
    gattn = mixed
    gmix = second

    def middle_back(i):
        at = pl.ds(pl.multiple_of(i * 128, 128), 128)
        grad = gtok[at, :]
        scaled, inverse = normed(middle[at, :])
        ahead = gout[at, :].astype(F32)
        gvec[GAIN_2] += column_sum(grad * scaled)
        gvec[SHIFT_2] += column_sum(grad)
        gvec[BIAS_DOWN] += column_sum(ahead)
        total = ahead + normed_back(grad, scaled, inverse, vec[GAIN_2])
        gtok[at, :] = total
        rounded = total.astype(BF)
        gattn[at, :] = rounded
        gvec[BIAS_OUT] += column_sum(rounded.astype(F32))
        gmix[at, :] = mul_nt(rounded, flat(wo[...])).astype(BF)

    loop(rows // 128, middle_back)

    class Vectors:
        def __init__(self, first_row, count, base):
            self.rows, self.base = range(first_row, first_row + count), base
            self.at = pl.ds(first_row, count)

        def copy(self, source, there, slot, device):
            return far(source.at[self.at], there.at[self.at], self.base + slot, device)

        def along_z(self, dz):
            return self.copy(gvec, v_z.at[dz - 1], dz - 1, z_peers[dz - 1])

        def step(self, k):
            there, device = ((v_y, y_peer), (v_c, c_peer), (v_x, x_peer))[k]
            return self.copy(v_sum.at[k], there, zs - 1 + k, device)

        def z_start(self):
            for dz in range(1, zs):
                self.along_z(dz).start()

        def y_start(self):
            for dz in range(1, zs):
                self.along_z(dz).wait_recv()
            for i in self.rows:
                total = gvec[i]
                for dz in range(1, zs):
                    total = total + v_z[dz - 1, i]
                v_sum[0, i] = total
            self.step(0).start()

        def next_start(self, k):
            self.step(k - 1).wait_recv()
            there = (v_y, v_c)[k - 1]
            v_sum[k, self.at] = v_sum[k - 1, self.at] + there[self.at]
            self.step(k).start()

        def finish(self):
            self.step(2).wait_recv()
            out_v[self.at] = v_sum[2, self.at] + v_x[self.at]

        def sent(self):
            for dz in range(1, zs):
                self.along_z(dz).wait_send()
            for k in range(3):
                self.step(k).wait_send()

    late_rows = Vectors(BIAS_Q, 4, number.take(zs + 2))
    early_rows = Vectors(BIAS_OUT, 4 + tiles, number.take(zs + 2))

    base_gmix = number.take(pairs)
    near_gmix = local_number.take(1)
    here_rows = pl.ds(pl.multiple_of(s * rows, 128), rows)
    there_rows = pl.ds(pl.multiple_of((1 - s) * rows, 128), rows)

    def send_gmix(p):
        lanes_p = pl.ds(pl.multiple_of((1 - s) * local + p * 128, 128), 128)
        at = pl.ds(pl.multiple_of(p * 128, 128), 128)
        return far(gmix.at[:, lanes_p], mixed_near.at[here_rows, at], base_gmix + p, x_peer)

    def take_gmix(p):
        at = pl.ds(pl.multiple_of(p * 128, 128), 128)
        return far(gmix.at[:, pl.ds(0, 128)], mixed_near.at[there_rows, at], base_gmix + p, x_peer)

    keep_gmix = pltpu.make_async_copy(
        gmix.at[:, mine], mixed_near.at[here_rows, :], near_sem.at[near_gmix]
    )
    send_gmix(0).start()
    keep_gmix.start()
    early_rows.z_start()
    weigh_down(z)

    gather_o.sent()

    wo[...] = mul(mixed_t[...], gattn[...]).astype(BF).reshape(zs, 4 * rq, width)
    x_start_d(z)
    for p in range(1, pairs):
        send_gmix(p).start()
    z_start_d(turn(0, z))
    y_start_d(turn(2, z))
    z_start_d(turn(1, z))
    for t in range(tiles):
        gather_u(t).sent()

    base_sq = number.take(pairs * spread_steps)

    def sum_q(p):
        return Spread(
            gwq, pl.ds(pl.multiple_of(p * local, 128), local), r1_q, r2_q, r3_q,
            base_sq + p * spread_steps,
        )

    sum_o.sib_start()

    def weigh_up_tile(t):
        at = tile_lanes(t)
        wu[:, :, at] = mul(second_t[...], slope[:, at]).astype(BF).reshape(zs, 4 * rq, tile)
        @pl.when(t < early)
        def _():
            sum_e(t).sib_start()

        @pl.when(t >= early)
        def _():
            sum_u(t).sib_start()

        @pl.when(t == 0)
        def _():
            sum_o.y_start()

        @pl.when(t == 1)
        def _():
            early_rows.y_start()

        @pl.when((t > 0) & (t < early))
        def _():
            sum_e(t - 1).y_start()

        @pl.when(t > early)
        def _():
            sum_u(t - 1).x_start()

    loop(tiles, weigh_up_tile)
    z_start_d(turn(2, z))
    sum_u(tiles - 1).x_start()
    keep_gmix.wait()

    xd = far_g(r5_d.at[s], r5_d.at[s], base_xs, x_peer)

    def finish_d():
        total = ry_d[z].astype(F32)
        for dz in range(1, zs):
            far_g(ry_d.at[0], rz_d.at[dz - 1], base_zd + dz - 1, z_peers[dz - 1]).wait_recv()
            total = total + rz_d[dz - 1].astype(F32)
        r5_d[s] = total.astype(BF)
        xd.start()

    def serve(k):
        @pl.when(k == 0)
        def _():
            early_rows.next_start(1)
            sum_o.z_start()
            y_start_d(z)
            sum_e(early - 1).y_start()

        @pl.when(k == 1)
        def _():
            early_rows.next_start(2)

        @pl.when(k == 2)
        def _():
            z_start_d(z)
            sum_e(0).z_start()
            sum_q(0).y_start()

        @pl.when(k == 3)
        def _():
            finish_o()

        @pl.when(k == 4)
        def _():
            sum_e(early - 1).z_start()
            sum_u(2).y_start()
            sum_q(1).y_start()
            finish_d()

        @pl.when(k == 5)
        def _():
            sum_u(3).y_start()
            sum_q(0).z_start()
            finish_e(0)

    per_piece = rows // side

    def dk_at(j):
        return (j // per_piece, slice(j % per_piece * side, (j % per_piece + 1) * side))

    def dv_at(j):
        return dk_at(j + blocks)

    def attend_back(p):
        for i in range(2 * group // rows):
            pieces[i] = jnp.zeros((rows, 128), F32)

        def head(h):
            half = pl.ds(pl.multiple_of(h * HEAD_DIM, HEAD_DIM), HEAD_DIM)
            here = pl.ds(pl.multiple_of(p * 128, 128), 128)
            for qi in range(blocks):
                at = slice(qi * side, (qi + 1) * side)
                query = head_lanes(qkv[at, lanes(p, 0)].astype(F32) * scale, h)
                grad = head_lanes(mixed_near[at, here].astype(F32), h)
                level = lse[p, h, :, at]
                weights, slopes = [], []
                centre = jnp.zeros((1, side), F32)
                for j in range(qi + 1):
                    there = slice(j * side, (j + 1) * side)
                    raw = scores(p, qkv[there, lanes(p, 1)], query, qi, j)
                    weight = jnp.exp(raw - level)
                    slope = mul_nt(qkv[there, lanes(p, 2)], grad)
                    centre = centre + column_sum(weight * slope)
                    weights.append(weight)
                    slopes.append(slope)
                total = jnp.zeros((HEAD_DIM, side), F32)
                for j in range(qi + 1):
                    there = slice(j * side, (j + 1) * side)
                    bend = (weights[j] * (slopes[j] - centre)).astype(BF)
                    pieces[dk_at(j)] += mul(bend, query)
                    pieces[dv_at(j)] += mul(weights[j].astype(BF), grad)
                    total = total + mul(k_t[p, half, there], bend)
                o_t[half, at] = total * scale
            serve(p * 2 + h)

        loop(2, head)
        for qi in range(blocks):
            at = slice(qi * side, (qi + 1) * side)
            qkv[at, lanes(p, 0)] = o_t[:, at].T.astype(BF)
            qkv[at, lanes(p, 1)] = pieces[dk_at(qi)].astype(BF)
            qkv[at, lanes(p, 2)] = pieces[dv_at(qi)].astype(BF)
        own = pl.ds(pl.multiple_of(s * local + p * 128, 128), 128)
        gvec[BIAS_Q, :, own] = column_sum(qkv[:, lanes(p, 0)].astype(F32))
        gvec[BIAS_V, :, own] = column_sum(qkv[:, lanes(p, 2)].astype(F32))
        both = pl.ds(pl.multiple_of(p * local, 128), local)

        gwq[:, :, both] = mul(first_t[...], qkv[:, both]).astype(BF).reshape(zs, 4 * rq, local)

    def pair_back(p):
        take_gmix(p).wait_recv()
        attend_back(p)
        sum_q(p).sib_start()

    loop(pairs, pair_back)

    base_gf = number.take(rows // side)

    def send_gf(i):
        at = pl.ds(pl.multiple_of(i * side, side), side)
        there = pl.ds(pl.multiple_of(rows + i * side, side), side)
        return far(first.at[at, :], first.at[there, :], base_gf + i, x_peer)

    def first_back(i, source, at):
        there = pl.ds(pl.multiple_of(at + i * side, side), side)
        grad = mul_nt(qkv[there, :], flat(wq[...]))
        scaled, unused = normed(source[pl.ds(pl.multiple_of(i * side, side), side), :].astype(F32))
        gvec[GAIN_1] += column_sum(grad * scaled)
        gvec[SHIFT_1] += column_sum(grad)
        return grad

    def away(i):
        grad = first_back(i, tok_far, (1 - s) * rows)
        first[pl.ds(pl.multiple_of(i * side, side), side), :] = grad.astype(BF)
        send_gf(i).start()

    loop(rows // side, away)
    sum_q(2).y_start()

    def stay(i):
        grad = first_back(i, tok, s * rows)
        at = pl.ds(pl.multiple_of(i * side, side), side)
        for j in range(width // 128):
            pieces[j, at, :] = grad[:, j * 128 : (j + 1) * 128]

    loop(rows // side, stay)

    late_rows.z_start()
    sum_u(2).z_start()
    sum_q(1).z_start()
    sum_u(3).z_start()

    def fall(i):
        at = pl.ds(pl.multiple_of(i * side, side), side)
        middle[at, :] += mul(hidden[at, :], flat(wd[...]))

    loop(rows // side, fall)
    late_rows.y_start()
    sum_q(2).z_start()

    def finish_out(i):
        at = pl.ds(pl.multiple_of(i * 128, 128), 128)
        value = middle[at, :] + vec[BIAS_DOWN]
        spot = s * rows + i * 128 + lax.broadcasted_iota(jnp.int32, (128, width), 0)
        out[at, :] = jnp.where(spot < last_valid, value, 0.0).astype(BF)

    loop(rows // 128, finish_out)
    finish_e(1)
    sum_u(2).finish()

    slot_q = number.take(pairs)

    def swap_q(p, half):
        block = r5_q.at[half, :, pl.ds(p * local, local)]
        return far_g(block, block, slot_q + p, x_peer)

    def finish_q(p):
        r5_q[s, :, p * local : (p + 1) * local] = sum_q(p).z_finish().astype(BF)
        swap_q(p, s).start()

    finish_q(0)
    late_rows.next_start(1)
    finish_q(1)
    late_rows.next_start(2)
    sum_u(3).finish()

    def last(i):
        at = pl.ds(pl.multiple_of(i * side, side), side)
        send_gf(i).wait_recv()
        scaled, inverse = normed(tok[at, :].astype(F32))
        there = pl.ds(pl.multiple_of(rows + i * side, side), side)
        own = jnp.concatenate([pieces[j, at, :] for j in range(width // 128)], axis=1)
        grad = own + first[there, :].astype(F32)
        gtok[at, :] = gtok[at, :] + normed_back(grad, scaled, inverse, vec[GAIN_1])

        @pl.when(i == 0)
        def _():
            finish_q(2)

    loop(rows // side, last)

    late_rows.finish()
    early_rows.finish()
    for i in range(BIAS_UP + tiles, TABLE):
        out_v[i] = jnp.zeros((1, width), F32)
    far_g(r5_d.at[1 - s], r5_d.at[1 - s], base_xs, x_peer).wait_recv()
    for half in range(2):
        out_d[:, half * local : (half + 1) * local] = r5_d[half].astype(F32)
    for t in range(early):
        swap_e(t).wait_recv()
        at = slice(t * tile, (t + 1) * tile)
        out_u[:, at] = r4_u[0, :, at].astype(F32) + r4_u[1, :, at].astype(F32)
    for t in range(early, tiles):
        sum_u(t).swap(1 - s).wait_recv()
        for half in range(2):
            wide = t * tile + half * local
            out_u[:, wide : wide + local] = r5_u[
                half, :, (t - early) * local : (t - early + 1) * local
            ].astype(F32)
    swap_o.wait_recv()
    out_o[...] = r4_o[0].astype(F32) + r4_o[1].astype(F32)
    for p in range(pairs):
        swap_q(p, 1 - s).wait_recv()
    for half in range(2):
        for p in range(pairs):
            for part in range(3):
                at = part * width + half * local + p * 128
                out_q[:, at : at + 128] = r5_q[
                    half, :, p * local + part * 128 : p * local + part * 128 + 128
                ].astype(F32)

    for dz in range(1, zs):
        far(table, e_z.at[dz - 1], base_e + dz - 1, z_peers[dz - 1]).wait_send()
        far_g(ry_d.at[0], rz_d.at[dz - 1], base_zd + dz - 1, z_peers[dz - 1]).wait_send()
    late_rows.sent()
    early_rows.sent()
    for copy in (y_table, c_table, send_tok, xd):
        copy.wait_send()
    for p in range(pairs):
        gather_q(p).sent()
        sum_q(p).sent()
        swap_q(p, s).wait_send()
    sum_o.sent()
    for i in range(cuts):
        gather_d(i).sent()
    for p in range(pairs):
        send_gmix(p).wait_send()
    for t in range(tiles):
        for yy in range(2):
            sib_d(t, yy).wait_send()
        x_d(t).wait_send()
        y_d(t).wait_send()
    for t in range(early):
        sum_e(t).sent()
        swap_e(t).wait_send()
    for t in range(early, tiles):
        sum_u(t).sent()
    swap_o.wait_send()
    for i in range(rows // side):
        send_gf(i).wait_send()


def fused_fits(tokens, lengths, own_q, own_d, shards, pair):
    rows, width = tokens.shape
    return (
        shards == 16
        and pair == 2
        and rows % 256 == 0
        and (width // pair) % 128 == 0
        and own_q.shape[0] % 16 == 0
        and own_d.shape[0] % 64 == 0
        and own_d.shape[0] * shards == 4 * width
    )


def fused(tokens, lengths, w_qkv, w_out, w_up, w_down, small, bias_up, cotangent):
    rows, width = tokens.shape
    shards = lax.axis_size("dp")
    zs = shards // 4
    d = lax.axis_index("dp")
    rq, rd = w_qkv.shape[0], w_down.shape[0]
    deep = 4 * rd * zs
    group = 2 * rows
    local = width // 2
    pairs = local // 128
    lane = jnp.arange(width)
    own = jnp.where(lane // rq == d, jnp.tile(jnp.stack(small), (1, shards)), 0)
    at = jnp.arange(zs)[:, None] * width + lane[None, :]
    up = jnp.where(at // rd == d, jnp.tile(bias_up, (width // rd,))[None, :], 0)
    table = jnp.concatenate([own, up, jnp.zeros((TABLE - 8 - zs, width), own.dtype)], axis=0)

    def vm(shape, kind=BF):
        return pltpu.VMEM(shape, kind)

    scratch = [
        vm((zs, 4 * rq, 3 * local)), vm((zs, 4 * rq, width)), vm((zs, 4 * rq, deep)),
        vm((zs, 4 * rd, width)), vm((zs, 4 * rq, 3 * local)), vm((zs, 4 * rd, width)),
        vm((rows, width)), vm((rows, width)), vm((group, width)), vm((width, group)), vm((group, 3 * local)),
        vm((pairs, 128, group)), vm((pairs, 128, group)), vm((1, group), jnp.int32),
        vm((pairs, 2, 1, group), F32), vm((128, group), F32),
        vm((group, local)), vm((rows, width)), vm((width, rows)), vm((rows, width), F32),
        vm((rows, width)), vm((width, rows)), vm((rows, width)),
        vm((rows, deep)), vm((4 * rd, rows)), vm((rows, deep)),
        vm((width // 128, rows, 128), F32),
        vm((2, TABLE, width)), vm((zs - 1, TABLE, width)), vm((TABLE, width)), vm((TABLE, width)),
        vm((TABLE, 1, width), F32), vm((TABLE, 1, width), F32), vm((zs - 1, TABLE, 1, width), F32),
        vm((TABLE, 1, width), F32), vm((TABLE, 1, width), F32), vm((TABLE, 1, width), F32),
        vm((3, TABLE, 1, width), F32),
        vm((zs, 2 * rd, width)), vm((zs, 2 * rd, local)), vm((zs, rd, local)),
        vm((zs - 1, rd, local)), vm((2, rd, local)),
        vm((zs, 2 * rq, deep)), vm((zs, 2 * rq, deep // 4)), vm((zs, rq, deep // 4)),
        vm((zs - 1, rq, deep // 4)), vm((2, rq, deep // 4)),
        vm((zs, rq, deep // 2)), vm((zs - 1, rq, deep // 2)), vm((2, rq, deep // 2)),
        vm((zs, 2 * rq, width)), vm((zs, rq, width)), vm((zs - 1, rq, width)), vm((2, rq, width)),
        vm((zs, 2 * rq, 3 * local)), vm((zs, rq, 3 * local)), vm((zs - 1, rq, 3 * local)),
        vm((2, rq, 3 * local)),
        pltpu.SemaphoreType.DMA((NEAR_COUNT,)),
        pltpu.SemaphoreType.DMA((FAR_COUNT,)),
        pltpu.SemaphoreType.DMA((FAR_COUNT,)),
    ]
    here = pl.BlockSpec(memory_space=pltpu.VMEM)
    away = pl.BlockSpec(memory_space=pl.ANY)
    return pl.pallas_call(
        fused_kernel,
        out_shape=(
            jax.ShapeDtypeStruct((rows, width), BF),
            jax.ShapeDtypeStruct((rows, width), F32),
            jax.ShapeDtypeStruct((rq, 3 * width), F32),
            jax.ShapeDtypeStruct((rq, width), F32),
            jax.ShapeDtypeStruct((rq, deep), F32),
            jax.ShapeDtypeStruct((rd, width), F32),
            jax.ShapeDtypeStruct((TABLE, 1, width), F32),
        ),
        in_specs=[pl.BlockSpec(memory_space=pltpu.SMEM), here, away, away, away, away, away, away],
        out_specs=[here] * 7,
        scratch_shapes=scratch,
        compiler_params=pltpu.CompilerParams(
            collective_id=0, has_side_effects=True, vmem_limit_bytes=67_043_328
        ),
        name="block",
    )(lengths, table, tokens, cotangent, w_qkv, w_out, w_up, w_down)


def closing_kernel(*refs):
    given, table, taken = refs[:6], refs[6], refs[7:]
    d = lax.axis_index("dp")
    for source, there in zip(given, taken[:6]):
        there[...] = source[...]
    own, up = taken[6:14], taken[14]
    width = table.shape[2]
    rq, rd = own[0].shape[1], up.shape[1]
    rows = jnp.concatenate([table[i] for i in range(8)], axis=0)
    moved = pltpu.roll(rows, lax.rem(width - d * rq, width), 1)
    for i in range(8):
        own[i][...] = moved[i : i + 1, :rq]
    row = jnp.broadcast_to(table[BIAS_UP + lax.div(d * rd, width)], (8, width))
    moved = pltpu.roll(row, lax.rem(width - lax.rem(d * rd, width), width), 1)
    up[...] = moved[0:1, :rd]


def per_device(
    tokens, lengths, w_qkv, w_out, w_up, w_down, bias_q, bias_v, bias_out, bias_up, bias_down,
    gain_one, shift_one, gain_two, shift_two, cotangent,
):
    if not fused_fits(
        tokens, lengths, w_qkv, w_down, lax.axis_size("dp"), lax.axis_size("seq")
    ):
        return per_device_plain(
            tokens, lengths, w_qkv, w_out, w_up, w_down, bias_q, bias_v, bias_out, bias_up,
            bias_down, gain_one, shift_one, gain_two, shift_two, cotangent,
        )
    small = [bias_q, bias_v, gain_one, shift_one, bias_out, bias_down, gain_two, shift_two]
    results = fused(
        tokens, lengths, w_qkv, w_out, w_up, w_down, small, bias_up, cotangent
    )
    rq, rd = w_qkv.shape[0], w_down.shape[0]
    steps = 2

    def whole(shape):
        return pl.BlockSpec(shape, lambda i: (0,) * len(shape))

    cut = [pl.BlockSpec((a.shape[0] // steps, a.shape[1]), lambda i: (i, 0)) for a in results[:6]]
    out, gtok, gq, go, gu, gd, *own, up = pl.pallas_call(
        closing_kernel,
        grid=(steps,),
        out_shape=tuple(jax.ShapeDtypeStruct(a.shape, a.dtype) for a in results[:6])
        + (jax.ShapeDtypeStruct((1, rq), F32),) * 8 + (jax.ShapeDtypeStruct((1, rd), F32),),
        in_specs=cut + [whole(results[6].shape)],
        out_specs=cut + [whole((1, rq))] * 8 + [whole((1, rd))],
        name="closing",
    )(*results)
    own, up = [piece[0] for piece in own], up[0]
    return (
        out, gtok, gq, go, gu, gd,
        own[0], own[1], own[4], up, own[5], own[2], own[3], own[6], own[7],
    )


def solution(mesh):
    return jax.shard_map(
        per_device,
        mesh=mesh,
        in_specs=(
            P(("dp", "seq"), None),
            P("dp", None),
            P("dp", None),
            P("dp", None),
            P("dp", None),
            P("dp", None),
            P("dp"),
            P("dp"),
            P("dp"),
            P("dp"),
            P("dp"),
            P("dp"),
            P("dp"),
            P("dp"),
            P("dp"),
            P(("dp", "seq"), None),
        ),
        out_specs=(
            P(("dp", "seq"), None),
            P(("dp", "seq"), None),
            P("dp", None),
            P("dp", None),
            P("dp", None),
            P("dp", None),
            P("dp"),
            P("dp"),
            P("dp"),
            P("dp"),
            P("dp"),
            P("dp"),
            P("dp"),
            P("dp"),
            P("dp"),
        ),
        check_vma=False,
    )
```
